32 devices in a mesh: dp: 8 (over z, y), mem: 4 (over x, core).
Axes of the slice: x: 2, y: 2, z: 4, core: 2. Of those that a mesh axis runs over, the one named last changes fastest.
Arguments:
- dec_in: bfloat16 [8, 1024, 1024], P('dp'), may hold values from -6 to 6
- memory: bfloat16 [8, 1024, 1024], P('dp', 'mem'), may hold values from -6 to 6
- dec_len: int32 [8], P('dp'), may hold values from 512 to 1024, as said below
- mem_len: int32 [8], P('dp'), may hold values from 256 to 1024, as said below
- grad_out: bfloat16 [8, 1024, 1024], P('dp'), may hold values from -6 to 6
- self_qkv: bfloat16 [1024, 3072], replicated, may hold values from -0.1875 to 0.1875
- self_out: bfloat16 [1024, 1024], replicated, may hold values from -3 to 3
- cross_q: bfloat16 [1024, 1024], replicated, may hold values from -0.1875 to 0.1875
- cross_kv: bfloat16 [1024, 2048], replicated, may hold values from -0.1875 to 0.1875
- cross_out: bfloat16 [1024, 1024], replicated, may hold values from -3 to 3
- ffn_in: bfloat16 [1024, 4096], replicated, may hold values from -0.1875 to 0.1875
- ffn_out: bfloat16 [4096, 1024], replicated, may hold values from -0.09375 to 0.09375
- proj_bias: float32 [7, 1024], replicated, may hold values from -3 to 3
- ffn_bias: float32 [4096], replicated, may hold values from -3 to 3
- norm_gain: float32 [3, 1024], replicated, may hold values from 0.5 to 1.5
- norm_shift: float32 [3, 1024], replicated, may hold values from -3 to 3
Outputs:
- layer_out: bfloat16 [8, 1024, 1024], P('dp')
- grad_dec: float32 [8, 1024, 1024], P('dp')
- grad_memory: float32 [8, 1024, 1024], P('dp', 'mem')
- grad_self_qkv: float32 [1024, 3072], P('dp')
- grad_self_out: float32 [1024, 1024], P('dp')
- grad_cross_q: float32 [1024, 1024], P('dp')
- grad_cross_kv: float32 [1024, 2048], P('dp')
- grad_cross_out: float32 [1024, 1024], P('dp')
- grad_ffn_in: float32 [1024, 4096], P('dp')
- grad_ffn_out: float32 [4096, 1024], P('dp')
- grad_proj_bias: float32 [7, 1024], replicated
- grad_ffn_bias: float32 [4096], replicated
- grad_norm_gain: float32 [3, 1024], replicated
- grad_norm_shift: float32 [3, 1024], replicated
The draws below stay inside these ranges and needn't reach their ends.
Inputs may be any that keep to these rules, and one draw needn't show every extreme that they name: `dec_len`: live decoder positions of an item; in every draw some item has all 1024. `mem_len`: valid memory positions of an item, the first ones; in every draw some item has all 1024.
All inputs are finite; a program needn't handle non-finite values.
Results may differ from the reference program's by a relative error of at most 0.023.
Values may be sent and summed in bfloat16 or wider, within the bound.
A program may use at most 448 MiB of HBM per device.

```python
import jax
import jax.numpy as jnp
from jax import lax

D = 1024
FF = 4096
HEAD_DIM = 64
HEADS = 16
DEC = 1024
MEM = 1024
ITEMS = 8


def draw_dec_len(key, part):
    lengths = jax.random.randint(key, (ITEMS,), DEC // 2, DEC + 1, dtype=jnp.int32)
    longest = jax.random.randint(jax.random.fold_in(key, 7), (), 0, ITEMS, dtype=jnp.int32)
    return jnp.where(jnp.arange(ITEMS, dtype=jnp.int32) == longest, DEC, lengths).astype(jnp.int32)


def draw_mem_len(key, part):
    lengths = jax.random.randint(key, (ITEMS,), MEM // 4, MEM + 1, dtype=jnp.int32)
    longest = jax.random.randint(jax.random.fold_in(key, 11), (), 0, ITEMS, dtype=jnp.int32)
    return jnp.where(jnp.arange(ITEMS, dtype=jnp.int32) == longest, MEM, lengths).astype(jnp.int32)


def block_levels(own_key, extent, shards, smallest, largest):
    loudness, own = 1.0, jax.random.fold_in(own_key, 6)
    for axis_at, parts in shards:
        draws = jnp.exp(jax.random.uniform(jax.random.fold_in(own, axis_at), (parts,), jnp.float32, smallest / len(shards), largest / len(shards)))
        loudness = loudness * jnp.repeat(draws, extent[axis_at] // parts).reshape([-1 if axis == axis_at else 1 for axis in range(len(extent))])
    return loudness


def bell_draw(key, shape, deviation, most, pieces=(), kind=jnp.bfloat16):
    values = deviation * jax.random.normal(key, shape, jnp.float32)
    if pieces:
        values = values * block_levels(key, shape, pieces, -0.22, 0.18)
    return jnp.clip(values, -most, most).astype(kind)


def setup_inputs(seed: int = 0) -> dict:
    key_of = jax.random.split(jax.random.key(seed), 17)
    dec_in = bell_draw(key_of[0], (ITEMS, DEC, D), 1.0, 6.0, ((0, 8),))
    memory = bell_draw(key_of[1], (ITEMS, MEM, D), 1.0, 6.0, ((0, 8), (1, 4)))
    dec_len = draw_dec_len(jax.random.fold_in(key_of[16], 71), 0)
    mem_len = draw_mem_len(jax.random.fold_in(key_of[16], 71), 0)
    grad_out = bell_draw(key_of[4], (ITEMS, DEC, D), 1.0, 6.0, ((0, 8),))
    self_qkv = bell_draw(key_of[5], (D, 3 * D), D ** -0.5, 0.1875)
    self_out = bell_draw(key_of[6], (D, D), (max(D // 256, 1)) ** -0.5, 3.0)
    cross_q = bell_draw(key_of[7], (D, D), D ** -0.5, 0.1875)
    cross_kv = bell_draw(key_of[8], (D, 2 * D), D ** -0.5, 0.1875)
    cross_out = bell_draw(key_of[9], (D, D), (max(D // 256, 1)) ** -0.5, 3.0)
    ffn_in = bell_draw(key_of[10], (D, FF), D ** -0.5, 0.1875)
    ffn_out = bell_draw(key_of[11], (FF, D), FF ** -0.5, 0.09375)
    proj_bias = bell_draw(key_of[12], (7, D), 0.5, 3.0, (), jnp.float32)
    ffn_bias = bell_draw(key_of[13], (FF,), 0.5, 3.0, (), jnp.float32)
    norm_gain = jnp.clip(1.0 + 0.1 * jax.random.normal(key_of[14], (3, D), jnp.float32), 0.5, 1.5)
    norm_shift = bell_draw(key_of[15], (3, D), 0.5, 3.0, (), jnp.float32)
    return {"dec_in": dec_in, "memory": memory, "dec_len": dec_len, "mem_len": mem_len, "grad_out": grad_out, "self_qkv": self_qkv, "self_out": self_out, "cross_q": cross_q, "cross_kv": cross_kv, "cross_out": cross_out, "ffn_in": ffn_in, "ffn_out": ffn_out, "proj_bias": proj_bias, "ffn_bias": ffn_bias, "norm_gain": norm_gain, "norm_shift": norm_shift}


@jax.custom_vjp
def low(v):
    return lax.optimization_barrier(v.astype(jnp.bfloat16)).astype(jnp.float32)

@jax.custom_vjp
def low_back(v):
    return v

def low_keep(v):
    return (low(v), None)

def low_pass(kept, grad):
    return (grad,)

def back_keep(v):
    return (v, None)

def back_low(kept, grad):
    return (low(grad),)
low.defvjp(low_keep, low_pass)
low_back.defvjp(back_keep, back_low)
norm_eps = 1e-05
neg_fill = -1e+30
highest = lax.Precision.HIGHEST

def matmul(left_rows, right_rows):
    return jnp.dot(left_rows, right_rows, precision=highest, preferred_element_type=jnp.float32)

def layer_norm(hidden, scale_row, shift_row):
    row_mean = lax.optimization_barrier(jnp.mean(hidden, axis=-1, keepdims=True))
    centered = hidden - row_mean
    variance = lax.optimization_barrier(jnp.mean(centered * centered, axis=-1, keepdims=True))
    return centered * lax.rsqrt(variance + norm_eps) * scale_row + shift_row

def attend(queries, key_rows, value_rows, allowed):
    q_heads = queries.reshape(queries.shape[0], HEADS, HEAD_DIM)
    k_heads = key_rows.reshape(key_rows.shape[0], HEADS, HEAD_DIM)
    v_heads = value_rows.reshape(value_rows.shape[0], HEADS, HEAD_DIM)
    scores = low_back(jnp.einsum('rhe,che->hrc', q_heads, k_heads, precision=highest))
    masked = jnp.where(allowed[None], scores, neg_fill)
    row_max = lax.optimization_barrier(jnp.max(masked, axis=-1, keepdims=True))
    exponent = jnp.where(allowed[None], jnp.exp(masked - row_max), 0.0)
    row_sum = lax.optimization_barrier(jnp.sum(exponent, axis=-1, keepdims=True))
    weights_low = low(exponent / row_sum)
    blended = jnp.einsum('hrc,che->rhe', weights_low, v_heads, precision=highest)
    return low_back(blended.reshape(queries.shape[0], HEADS * HEAD_DIM))

def forward(dec_rows, mem_rows, dec_length, mem_length, params):
    self_qkv, self_out, cross_q, cross_kv, cross_out, ffn_in, ffn_out, proj_bias, ffn_bias, norm_gain, norm_shift = params
    zero_bias = jnp.zeros((D,), jnp.float32)
    qkv_rows = low_back(matmul(low(dec_rows), self_qkv) + jnp.concatenate([proj_bias[0], zero_bias, proj_bias[1]]))
    queries = low(qkv_rows[:, :D] * 0.125)
    key_rows = low(qkv_rows[:, D:2 * D])
    value_rows = low(qkv_rows[:, 2 * D:])
    positions = jnp.arange(DEC, dtype=jnp.int32)
    causal = (positions[None, :] <= positions[:, None]) & (positions[None, :] < dec_length)
    attended = attend(queries, key_rows, value_rows, causal)
    self_branch = low_back(matmul(low(attended), self_out) + proj_bias[2])
    first_out = layer_norm(dec_rows + self_branch, norm_gain[0], norm_shift[0])
    cross_query = low_back(matmul(low(first_out), cross_q) + proj_bias[3])
    cq_rows = low(cross_query * 0.125)
    mem_kv = low_back(matmul(low(mem_rows), cross_kv) + jnp.concatenate([zero_bias, proj_bias[4]]))
    mem_positions = jnp.arange(MEM, dtype=jnp.int32)
    mem_reach = jnp.broadcast_to((mem_positions < mem_length)[None, :], (DEC, MEM))
    crossed = attend(cq_rows, low(mem_kv[:, :D]), low(mem_kv[:, D:]), mem_reach)
    cross_branch = low_back(matmul(low(crossed), cross_out) + proj_bias[5])
    second = layer_norm(first_out + cross_branch, norm_gain[1], norm_shift[1])
    hidden_pre = low_back(matmul(low(second), ffn_in) + ffn_bias)
    activated = low(jax.nn.gelu(hidden_pre, approximate=False))
    ffn_branch = low_back(matmul(activated, ffn_out) + proj_bias[6])
    return layer_norm(second + ffn_branch, norm_gain[2], norm_shift[2])

def reference(dec_in, memory, dec_len, mem_len, grad_out, self_qkv, self_out, cross_q, cross_kv, cross_out, ffn_in, ffn_out, proj_bias, ffn_bias, norm_gain, norm_shift):
    params = (self_qkv.astype(jnp.float32), self_out.astype(jnp.float32), cross_q.astype(jnp.float32), cross_kv.astype(jnp.float32), cross_out.astype(jnp.float32), ffn_in.astype(jnp.float32), ffn_out.astype(jnp.float32), proj_bias.astype(jnp.float32), ffn_bias.astype(jnp.float32), norm_gain.astype(jnp.float32), norm_shift.astype(jnp.float32))
    positions = jnp.arange(DEC, dtype=jnp.int32)

    def one_item(running, item_data):
        dec_rows, mem_rows, dec_length, mem_length, cotangent = item_data

        def item_forward(dec_value, mem_value, param_value):
            return forward(dec_value, mem_value, dec_length, mem_length, param_value)
        result, pullback = jax.vjp(item_forward, dec_rows.astype(jnp.float32), mem_rows.astype(jnp.float32), params)
        live_rows = (positions < dec_length)[:, None]
        cotangent_rows = jnp.where(live_rows, cotangent.astype(jnp.float32), 0.0)
        grad_rows, grad_mem, grad_params = pullback(cotangent_rows)
        running = jax.tree.map(jnp.add, running, grad_params)
        return (running, (result.astype(jnp.bfloat16), grad_rows, grad_mem))
    zero_grads = jax.tree.map(jnp.zeros_like, params)
    totals, stacked = lax.scan(one_item, zero_grads, (dec_in, memory, dec_len, mem_len, grad_out))
    return (stacked[0], stacked[1], stacked[2], totals[0], totals[1], totals[2], totals[3], totals[4], totals[5], totals[6], totals[7], totals[8], totals[9], totals[10])
```

```python
import functools

import jax
import jax.numpy as jnp
from jax import lax
from jax.experimental import pallas as pl
from jax.experimental.pallas import tpu as pltpu
from jax.sharding import PartitionSpec as P

HEAD_DIM = 64
norm_eps = 1e-05
neg_fill = -1e30
low = jnp.bfloat16
VMEM_LIMIT = 56 * 1024 * 1024


def product(left_rows, right_rows):
    return jnp.dot(left_rows, right_rows, preferred_element_type=jnp.float32)


def product_tn(left_rows, right_rows):
    return lax.dot_general(
        left_rows, right_rows, (((0,), (0,)), ((), ())), preferred_element_type=jnp.float32
    )


def product_nt(left_rows, right_rows):
    return lax.dot_general(
        left_rows, right_rows, (((1,), (1,)), ((), ())), preferred_element_type=jnp.float32
    )


def normalize(hidden, scale_row, shift_row):
    row_mean = jnp.mean(hidden, axis=-1, keepdims=True)
    centered = hidden - row_mean
    variance = jnp.mean(centered * centered, axis=-1, keepdims=True)
    inverse = lax.rsqrt(variance + norm_eps)
    normed = centered * inverse
    return (normed * scale_row + shift_row, normed, inverse)


def norm_back(grad_rows, normed, inverse, scale_row):
    scaled = grad_rows * scale_row
    grad_hidden = inverse * (
        scaled
        - jnp.mean(scaled, axis=-1, keepdims=True)
        - normed * jnp.mean(scaled * normed, axis=-1, keepdims=True)
    )
    return (grad_hidden, jnp.sum(grad_rows * normed, axis=0), jnp.sum(grad_rows, axis=0))


def gelu_parts(values):
    cdf = 0.5 * (1.0 + lax.erf(values * 0.7071067811865476))
    density = jnp.exp(-0.5 * values * values) * 0.3989422804014327
    return values * cdf, cdf + values * density


def column_sum(matrix):
    return jnp.sum(matrix.astype(jnp.float32), axis=0)


def lane_head(rows):
    return lax.broadcasted_iota(jnp.int32, (rows, 128), 1) // HEAD_DIM


def pick_head(pair, h):
    return jnp.where(lane_head(pair.shape[0]) == h, pair, jnp.zeros_like(pair))


def self_fwd_kernel(info, q_ref, k_ref, v_ref, o_ref):
    rows = k_ref.shape[0]
    block = rows // 4
    dec_len = info[1]

    def process(qb, slot):
        keys = (qb + 1) * block
        kk, vv = k_ref[:keys, :], v_ref[:keys, :]
        qq = q_ref[qb * block : (qb + 1) * block, :]
        total = None
        for h in range(2):
            s = product_nt(pick_head(qq, h), kk)
            col = lax.broadcasted_iota(jnp.int32, s.shape, 1)
            row = lax.broadcasted_iota(jnp.int32, s.shape, 0) + qb * block
            s = jnp.where((col <= row) & (col < dec_len), s, neg_fill)
            p = jnp.exp(s - jnp.max(s, axis=1, keepdims=True))
            inv = 1.0 / jnp.sum(p, axis=1, keepdims=True)
            part = product(p.astype(low), pick_head(vv, h)) * inv
            total = part if total is None else total + part
        o_ref[slot * block : (slot + 1) * block, :] = total.astype(low)

    @pl.when(info[0] == 0)
    def _():
        process(0, 0)
        process(3, 1)

    @pl.when(info[0] == 1)
    def _():
        process(1, 0)
        process(2, 1)


def self_forward(info, q, k, v):
    rows, width = q.shape
    pairs = width // 128
    spec = pl.BlockSpec((rows, 128), lambda i, s: (0, i))
    return pl.pallas_call(
        self_fwd_kernel,
        out_shape=jax.ShapeDtypeStruct((rows // 2, width), low),
        grid_spec=pltpu.PrefetchScalarGridSpec(
            num_scalar_prefetch=1,
            grid=(pairs,),
            in_specs=[spec, spec, spec],
            out_specs=pl.BlockSpec((rows // 2, 128), lambda i, s: (0, i)),
        ),
        compiler_params=pltpu.CompilerParams(vmem_limit_bytes=VMEM_LIMIT),
        cost_estimate=pl.CostEstimate(
            flops=6 * rows * rows * width, bytes_accessed=8 * rows * width, transcendentals=rows * rows * 3
        ),
        name="self_forward",
    )(info, q, k, v)


def cross_fwd_kernel(q_ref, k_ref, v_ref, bias_ref, o_ref):
    block = 256
    for r in range(q_ref.shape[0] // block):
        qq = q_ref[r * block : (r + 1) * block, :]
        total = None
        for h in range(2):
            s = product_nt(pick_head(qq, h), k_ref[...]) + bias_ref[...]
            p = jnp.exp(s - jnp.max(s, axis=1, keepdims=True))
            inv = 1.0 / jnp.sum(p, axis=1, keepdims=True)
            part = product(p.astype(low), pick_head(v_ref[...], h)) * inv
            total = part if total is None else total + part
        o_ref[r * block : (r + 1) * block, :] = total.astype(low)


def cross_forward(q, k, v, bias_row):
    rows, width = q.shape
    keys = k.shape[0]
    return pl.pallas_call(
        cross_fwd_kernel,
        out_shape=jax.ShapeDtypeStruct((rows, width), low),
        grid=(width // 128,),
        in_specs=[
            pl.BlockSpec((rows, 128), lambda i: (0, i)),
            pl.BlockSpec((keys, 128), lambda i: (0, i)),
            pl.BlockSpec((keys, 128), lambda i: (0, i)),
            pl.BlockSpec((1, keys), lambda i: (0, 0)),
        ],
        out_specs=pl.BlockSpec((rows, 128), lambda i: (0, i)),
        compiler_params=pltpu.CompilerParams(vmem_limit_bytes=VMEM_LIMIT),
        cost_estimate=pl.CostEstimate(
            flops=16 * rows * keys * width, bytes_accessed=8 * rows * width, transcendentals=rows * keys * 8
        ),
        name="cross_forward",
    )(q, k, v, bias_row)


def back_kernel(info, q_ref, k_ref, v_ref, g0_ref, g1_ref, g2_ref, g3_ref, bias_ref, dq_ref, dk_ref, dv_ref, dk_acc, dv_acc, *, causal):
    rows = q_ref.shape[0]
    keys_all = k_ref.shape[0]
    block = rows // 4
    k_t = k_ref[...].T
    dk_acc[...] = jnp.zeros_like(dk_acc)
    dv_acc[...] = jnp.zeros_like(dv_acc)
    for qb in range(4):
        keys = (qb + 1) * block if causal else keys_all
        kk, vv = k_ref[:keys, :], v_ref[:keys, :]
        qq = q_ref[qb * block : (qb + 1) * block, :]
        gg = (g0_ref, g1_ref, g2_ref, g3_ref)[qb][...]
        q_parts = []
        for h in range(2):
            q_h, g_h = pick_head(qq, h), pick_head(gg, h)
            s = product_nt(kk, q_h)
            if causal:
                key = lax.broadcasted_iota(jnp.int32, s.shape, 0)
                row = lax.broadcasted_iota(jnp.int32, s.shape, 1) + qb * block
                s = jnp.where((key <= row) & (key < info[1]), s, neg_fill)
            else:
                s = s + jnp.concatenate([bias_ref[...]] * (block // 128), axis=1)
            p = jnp.exp(s - jnp.max(s, axis=0, keepdims=True))
            p = p * (1.0 / jnp.sum(p, axis=0, keepdims=True))
            dp = product_nt(vv, g_h)
            e = jnp.sum(p * dp, axis=0, keepdims=True)
            ds = (p * (dp - e)).astype(low)
            dv_acc[:keys, :] += product(p.astype(low), g_h)
            dk_acc[:keys, :] += product(ds, q_h)
            q_parts.append(product(k_t[h * HEAD_DIM : (h + 1) * HEAD_DIM, :keys], ds))
        dq_t = jnp.concatenate(q_parts, axis=0) * 0.125
        dq_ref[qb * block : (qb + 1) * block, :] = dq_t.T.astype(low)
    dk_ref[...] = dk_acc[...].astype(low)
    dv_ref[...] = dv_acc[...].astype(low)


def attention_back(info, q, k, v, g, bias, causal):
    rows, width = q.shape
    keys = k.shape[0]
    own = pl.BlockSpec((rows, 128), lambda i, s: (0, i))
    wide = pl.BlockSpec((keys, 128), lambda i, s: (0, s[0] + i))
    mine = pl.BlockSpec((keys, 128), lambda i, s: (0, i))

    def g_block(n):
        return pl.BlockSpec((rows // 4, 128), lambda i, s: (s[2 + n] if causal else n, i))

    q_spec = wide if q.shape[1] == k.shape[1] else own
    width = g.shape[1]
    return pl.pallas_call(
        functools.partial(back_kernel, causal=causal),
        out_shape=[
            jax.ShapeDtypeStruct((rows, width), low),
            jax.ShapeDtypeStruct((keys, width), low),
            jax.ShapeDtypeStruct((keys, width), low),
        ],
        grid_spec=pltpu.PrefetchScalarGridSpec(
            num_scalar_prefetch=1,
            grid=(width // 128,),
            in_specs=[q_spec, wide, wide] + [g_block(n) for n in range(4)] + [pl.BlockSpec(bias.shape, lambda i, s: (0, 0))],
            out_specs=[own, mine, mine],
            scratch_shapes=[pltpu.VMEM((keys, 128), jnp.float32), pltpu.VMEM((keys, 128), jnp.float32)],
        ),
        compiler_params=pltpu.CompilerParams(vmem_limit_bytes=VMEM_LIMIT),
        cost_estimate=pl.CostEstimate(
            flops=40 * rows * keys * width // (2 if causal else 1),
            bytes_accessed=14 * rows * width,
            transcendentals=rows * keys * 4,
        ),
        name="self_back" if causal else "cross_back",
    )(info, q, k, v, g, g, g, g, bias)


def swap(part, axis, distance):
    count = lax.axis_size(axis)
    return lax.ppermute(part, axis, [(i, i ^ distance) for i in range(count)])


def gather_rel(part):
    core = swap(part, "mem", 1)
    across = swap(part, "mem", 2)
    return [part, core, across, swap(across, "mem", 1)]


def scatter_dp(parts):
    count = lax.axis_size("dp")
    me = lax.axis_index("dp")
    kept = [a.reshape(count, a.shape[0] // count, a.shape[1]) for a in parts]
    widths = [a.shape[1] for a in parts]
    distance = 1
    while count > 1:
        bit = (me // distance) % 2
        halves = [a.reshape(count // 2, 2, a.shape[1], a.shape[2]) for a in kept]
        mine = [lax.dynamic_index_in_dim(a, bit, 1, False) for a in halves]
        theirs = [lax.dynamic_index_in_dim(a, 1 - bit, 1, False).astype(low) for a in halves]
        got = swap(jnp.concatenate(theirs, axis=2), "dp", distance)
        start, kept = 0, []
        for a, w in zip(mine, widths):
            kept.append(a + got[:, :, start : start + w].astype(jnp.float32))
            start += w
        count, distance = count // 2, distance * 2
    return [a[0] for a in kept]


def sum_all(vector):
    for axis in ("mem", "dp"):
        distance = 1
        while distance < lax.axis_size(axis):
            vector = vector + swap(vector, axis, distance)
            distance *= 2
    return vector


def per_device(
    dec_in,
    memory,
    dec_len,
    mem_len,
    grad_out,
    self_qkv,
    self_out,
    cross_q,
    cross_kv,
    cross_out,
    ffn_in,
    ffn_out,
    proj_bias,
    ffn_bias,
    norm_gain,
    norm_shift,
):
    x_full = dec_in[0]
    rows, width = x_full.shape
    hidden = ffn_in.shape[1]
    block = rows // 4
    half, quarter = width // 2, width // 4
    groups = lax.axis_size("dp")
    mem_rows = memory[0]
    mem_block = mem_rows.shape[0]
    me = lax.axis_index("mem")
    chip, core = me // 2, me % 2
    quart = 2 * core + chip

    def block_of(m):
        return jnp.where(m // 2 == 0, 3 * (m % 2), 1 + m % 2)

    def columns_half(w, count):
        piece = w.reshape(w.shape[0], count, 2, half)
        return lax.dynamic_index_in_dim(piece, core, 2, False).reshape(w.shape[0], count * half)

    def columns_quarter(w, count):
        piece = w.reshape(w.shape[0], count, 4, quarter)
        return lax.dynamic_index_in_dim(piece, quart, 2, False).reshape(w.shape[0], count * quarter)

    def own_rows(a):
        return lax.dynamic_slice_in_dim(a, block_of(me) * block, block, 0)

    def by_block(slots):
        stacked = jnp.stack(slots)
        order = [0, 2, 3, 1]
        return jnp.concatenate(
            [lax.dynamic_index_in_dim(stacked, me ^ order[n], 0, False) for n in range(4)], axis=0
        )

    def by_quarter(slots):
        stacked = jnp.stack(slots)
        order = [0, 2, 1, 3]
        return [lax.dynamic_index_in_dim(stacked, me ^ order[n], 0, False) for n in range(4)]

    mem_full = jnp.concatenate(gather_rel(mem_rows), axis=0)

    qkv8 = product(x_full, columns_half(self_qkv, 3))
    bias_q8 = lax.dynamic_slice_in_dim(proj_bias[0], core * half, half)
    bias_v8 = lax.dynamic_slice_in_dim(proj_bias[1], core * half, half)
    q8 = ((qkv8[:, :half] + bias_q8) * 0.125).astype(low)
    k8 = qkv8[:, half : 2 * half].astype(low)
    v8 = (qkv8[:, 2 * half :] + bias_v8).astype(low)
    info_f = jnp.stack([chip, dec_len[0]]).astype(jnp.int32)
    att8 = self_forward(info_f, q8, k8, v8)

    def heads_to_rows(a8):
        mine = lax.dynamic_slice_in_dim(a8, core * block, block, 0)
        other = swap(lax.dynamic_slice_in_dim(a8, (1 - core) * block, block, 0), "mem", 1)
        return jnp.where(
            core == 0, jnp.concatenate([mine, other], axis=1), jnp.concatenate([other, mine], axis=1)
        )

    attended = heads_to_rows(att8)
    x_own = own_rows(x_full).astype(jnp.float32)
    first, first_norm, first_inv = normalize(
        x_own + product(attended, self_out) + proj_bias[2], norm_gain[0], norm_shift[0]
    )
    first_low = first.astype(low)
    first_slots = gather_rel(first_low)
    first_chip = jnp.concatenate(
        [
            jnp.where(core == 0, first_slots[0], first_slots[1]),
            jnp.where(core == 0, first_slots[1], first_slots[0]),
        ],
        axis=0,
    )

    bias_cq8 = lax.dynamic_slice_in_dim(proj_bias[3], core * half, half)
    cq8 = ((product(first_chip, columns_half(cross_q, 1)) + bias_cq8) * 0.125).astype(low)
    kv8 = product(mem_full, columns_half(cross_kv, 2))
    bias_cv8 = lax.dynamic_slice_in_dim(proj_bias[4], core * half, half)
    kc8 = kv8[:, :half].astype(low)
    vc8 = (kv8[:, half:] + bias_cv8).astype(low)
    slot_pos = jnp.stack([(me ^ k) * mem_block for k in range(4)])
    mem_pos = (slot_pos[:, None] + jnp.arange(mem_block, dtype=jnp.int32)[None, :]).reshape(-1)
    mem_bias = jnp.where(mem_pos < mem_len[0], 0.0, neg_fill).astype(jnp.float32)
    crossed = heads_to_rows(cross_forward(cq8, kc8, vc8, mem_bias[None, :]))
    second, second_norm, second_inv = normalize(
        first + product(crossed, cross_out) + proj_bias[5], norm_gain[1], norm_shift[1]
    )
    second_low = second.astype(low)

    act, act_grad = gelu_parts(product(second_low, ffn_in) + ffn_bias)
    act, act_grad = act.astype(low), act_grad.astype(low)
    third, third_norm, third_inv = normalize(
        second + product(act, ffn_out) + proj_bias[6], norm_gain[2], norm_shift[2]
    )
    row_pos = block_of(me) * block + jnp.arange(block, dtype=jnp.int32)
    cot = jnp.where((row_pos < dec_len[0])[:, None], own_rows(grad_out[0]).astype(jnp.float32), 0.0)
    dh3, gain_three, shift_three = norm_back(cot, third_norm, third_inv, norm_gain[2])
    dz = dh3.astype(low)
    du = (product_nt(dz, ffn_out) * act_grad.astype(jnp.float32)).astype(low)
    dh2, gain_two, shift_two = norm_back(
        dh3 + product_nt(du, ffn_in), second_norm, second_inv, norm_gain[1]
    )
    dco = dh2.astype(low)

    second_full = jnp.concatenate(gather_rel(second_low), axis=0)
    dz_full = jnp.concatenate(gather_rel(dz), axis=0)
    dco_full = jnp.concatenate(gather_rel(dco), axis=0)
    piece = hidden // groups // 4
    w_in_q = lax.dynamic_index_in_dim(ffn_in.reshape(width, groups, 4, piece), quart, 2, False).reshape(
        width, hidden // 4
    )
    w_out_q = lax.dynamic_index_in_dim(ffn_out.reshape(groups, 4, piece, width), quart, 1, False).reshape(
        hidden // 4, width
    )
    b_in_q = lax.dynamic_index_in_dim(ffn_bias.reshape(groups, 4, piece), quart, 1, False).reshape(-1)
    act_q, slope_q = gelu_parts(product(second_full, w_in_q) + b_in_q)
    act_q = act_q.astype(low)
    du_q = (product_nt(dz_full, w_out_q) * slope_q).astype(low)
    g_in, g_out = scatter_dp([product_tn(second_full, du_q), product_tn(act_q, dz_full)])

    first_full = jnp.concatenate(first_slots, axis=0)
    bias_cq4 = lax.dynamic_slice_in_dim(proj_bias[3], quart * quarter, quarter)
    cq4 = ((product(first_full, columns_quarter(cross_q, 1)) + bias_cq4) * 0.125).astype(low)
    cross_out_q = lax.dynamic_slice_in_dim(cross_out, quart * quarter, quarter, 0)
    dx4 = product_nt(dco_full, cross_out_q).astype(low)
    pair_base = chip * (quarter // 128)
    info_c = jnp.stack([pair_base]).astype(jnp.int32)
    bias_col = jnp.broadcast_to(mem_bias[:, None], (mem_bias.shape[0], 128))
    dq4, dkc4, dvc4 = attention_back(info_c, cq4, kc8, vc8, dx4, bias_col, False)
    dkv4 = jnp.concatenate([dkc4, dvc4], axis=1)

    def to_rows(a, size):
        slots = [a[k * size : (k + 1) * size] for k in range(4)]
        return by_quarter([slots[0]] + [swap(slots[k], "mem", k) for k in (1, 2, 3)])

    dq_own = jnp.concatenate(to_rows(dq4, block), axis=1)
    dkv_parts = to_rows(dkv4, mem_block)
    dkv_own = jnp.concatenate(
        [a[:, :quarter] for a in dkv_parts] + [a[:, quarter:] for a in dkv_parts], axis=1
    )
    grad_memory = product_nt(dkv_own, cross_kv)[None]
    crossed_full = jnp.concatenate(gather_rel(crossed), axis=0)
    dco_q = lax.dynamic_slice_in_dim(dco_full, quart * quarter, quarter, 1)
    g_co, g_cq, g_ckv = scatter_dp(
        [product_tn(crossed_full, dco_q), product_tn(first_full, dq4), product_tn(mem_full, dkv4)]
    )

    dh1, gain_one, shift_one = norm_back(
        dh2 + product_nt(dq_own, cross_q), first_norm, first_inv, norm_gain[0]
    )
    do = dh1.astype(low)
    do_full = jnp.concatenate(gather_rel(do), axis=0)

    self_out_q = lax.dynamic_slice_in_dim(self_out, quart * quarter, quarter, 0)
    da4 = product_nt(do_full, self_out_q).astype(low)
    order = [0, 2, 3, 1]
    info_s = jnp.stack([pair_base, dec_len[0]] + [me ^ order[n] for n in range(4)]).astype(jnp.int32)
    sq4, sk4, sv4 = attention_back(info_s, q8, k8, v8, da4, bias_col[:8], True)
    dqkv4 = jnp.concatenate([sq4, sk4, sv4], axis=1)
    qkv_q = columns_quarter(self_qkv, 3)
    partial = product_nt(dqkv4, qkv_q).reshape(4, block, width)

    def rows_for(m):
        return lax.dynamic_index_in_dim(partial, block_of(m), 0, False)

    sent = jnp.concatenate([rows_for(me ^ 1).astype(low), rows_for(me ^ 3).astype(low)], axis=0)
    got = swap(sent, "mem", 1).astype(jnp.float32)
    across = swap((rows_for(me ^ 2) + got[block:]).astype(low), "mem", 2).astype(jnp.float32)
    grad_own = (dh1 + rows_for(me) + got[:block] + across).astype(low)
    grad_dec = by_block(gather_rel(grad_own)).astype(jnp.float32)[None]
    layer_out = by_block(gather_rel(third.astype(low)))[None]

    attended_full = jnp.concatenate(gather_rel(attended), axis=0)
    do_q = lax.dynamic_slice_in_dim(do_full, quart * quarter, quarter, 1)
    g_qkv, g_so = scatter_dp([product_tn(x_full, dqkv4), product_tn(attended_full, do_q)])

    def gather_parts(parts):
        packed = jnp.concatenate([a.astype(low) for a in parts], axis=1)
        slots = by_quarter(gather_rel(packed))
        out, start = [], 0
        for a in parts:
            out.append([s[:, start : start + a.shape[1]].astype(jnp.float32) for s in slots])
            start += a.shape[1]
        return out

    in_parts, out_parts = gather_parts([g_in, g_out])
    co_parts, cq_parts, ckv_parts = gather_parts([g_co, g_cq, g_ckv])
    qkv_parts, so_parts = gather_parts([g_qkv, g_so])

    def interleave(parts, count):
        r = parts[0].shape[0]
        return jnp.stack([p.reshape(r, count, -1) for p in parts], axis=2).reshape(r, -1)

    place = jnp.zeros((2, width), jnp.float32)
    own_sums = jnp.stack([column_sum(sq4), column_sum(sv4)])
    place = lax.dynamic_update_slice(place, own_sums, (0, quart * quarter))
    packed = jnp.concatenate(
        [
            place,
            jnp.stack(
                [
                    column_sum(do),
                    column_sum(dq_own),
                    column_sum(dkv_own[:, width:]),
                    column_sum(dco),
                    column_sum(dz),
                    gain_one,
                    gain_two,
                    gain_three,
                    shift_one,
                    shift_two,
                    shift_three,
                ]
            ),
            column_sum(du).reshape(hidden // width, width),
        ],
        axis=0,
    )
    packed = sum_all(packed)
    return (
        layer_out,
        grad_dec,
        grad_memory,
        interleave(qkv_parts, 3),
        interleave(so_parts, 1),
        interleave(cq_parts, 1),
        interleave(ckv_parts, 2),
        interleave(co_parts, 1),
        interleave(in_parts, groups),
        jnp.concatenate(out_parts, axis=0),
        packed[:7],
        packed[13:].reshape(hidden),
        packed[7:10],
        packed[10:13],
    )


def solution(mesh):
    in_specs = (
        P("dp", None, None),
        P("dp", "mem", None),
        P("dp"),
        P("dp"),
        P("dp", None, None),
    ) + (P(),) * 11
    out_specs = (
        P("dp", None, None),
        P("dp", None, None),
        P("dp", "mem", None),
    ) + (P("dp", None),) * 7 + (P(),) * 4
    return jax.shard_map(
        per_device, mesh=mesh, in_specs=in_specs, out_specs=out_specs, check_vma=False
    )
```

```python
import functools

import jax
import jax.numpy as jnp
from jax import lax
from jax.experimental import pallas as pl
from jax.experimental.pallas import tpu as pltpu
from jax.sharding import PartitionSpec as P

HEAD_DIM = 64
norm_eps = 1e-05
neg_fill = -1e30
low = jnp.bfloat16
VMEM_LIMIT = 56 * 1024 * 1024


def product(left_rows, right_rows):
    return jnp.dot(left_rows, right_rows, preferred_element_type=jnp.float32)


def product_tn(left_rows, right_rows):
    return lax.dot_general(
        left_rows, right_rows, (((0,), (0,)), ((), ())), preferred_element_type=jnp.float32
    )


def product_nt(left_rows, right_rows):
    return lax.dot_general(
        left_rows, right_rows, (((1,), (1,)), ((), ())), preferred_element_type=jnp.float32
    )


def normalize(hidden, scale_row, shift_row):
    row_mean = jnp.mean(hidden, axis=-1, keepdims=True)
    centered = hidden - row_mean
    variance = jnp.mean(centered * centered, axis=-1, keepdims=True)
    inverse = lax.rsqrt(variance + norm_eps)
    normed = centered * inverse
    return (normed * scale_row + shift_row, normed, inverse)


def norm_back(grad_rows, normed, inverse, scale_row):
    scaled = grad_rows * scale_row
    grad_hidden = inverse * (
        scaled
        - jnp.mean(scaled, axis=-1, keepdims=True)
        - normed * jnp.mean(scaled * normed, axis=-1, keepdims=True)
    )
    return (grad_hidden, jnp.sum(grad_rows * normed, axis=0), jnp.sum(grad_rows, axis=0))


def gelu_parts(values):
    cdf = 0.5 * (1.0 + lax.erf(values * 0.7071067811865476))
    density = jnp.exp(-0.5 * values * values) * 0.3989422804014327
    return values * cdf, cdf + values * density


def column_sum(matrix):
    return jnp.sum(matrix.astype(jnp.float32), axis=0)


def lane_head(rows):
    return lax.broadcasted_iota(jnp.int32, (rows, 128), 1) // HEAD_DIM


def pick_head(pair, h):
    return jnp.where(lane_head(pair.shape[0]) == h, pair, jnp.zeros_like(pair))


def self_fwd_kernel(info, q_ref, k_ref, v_ref, o_ref):
    rows = k_ref.shape[0]
    block = rows // 4
    dec_len = info[1]

    def process(qb, slot):
        keys = (qb + 1) * block
        kk, vv = k_ref[:keys, :], v_ref[:keys, :]
        qq = q_ref[qb * block : (qb + 1) * block, :]
        total = None
        for h in range(2):
            s = product_nt(pick_head(qq, h), kk)
            col = lax.broadcasted_iota(jnp.int32, s.shape, 1)
            row = lax.broadcasted_iota(jnp.int32, s.shape, 0) + qb * block
            s = jnp.where((col <= row) & (col < dec_len), s, neg_fill)
            p = jnp.exp(s - jnp.max(s, axis=1, keepdims=True))
            inv = 1.0 / jnp.sum(p, axis=1, keepdims=True)
            part = product(p.astype(low), pick_head(vv, h)) * inv
            total = part if total is None else total + part
        o_ref[slot * block : (slot + 1) * block, :] = total.astype(low)

    @pl.when(info[0] == 0)
    def _():
        process(0, 0)
        process(3, 1)

    @pl.when(info[0] == 1)
    def _():
        process(1, 0)
        process(2, 1)


def self_forward(info, q, k, v):
    rows, width = q.shape
    pairs = width // 128
    spec = pl.BlockSpec((rows, 128), lambda i, s: (0, i))
    return pl.pallas_call(
        self_fwd_kernel,
        out_shape=jax.ShapeDtypeStruct((rows // 2, width), low),
        grid_spec=pltpu.PrefetchScalarGridSpec(
            num_scalar_prefetch=1,
            grid=(pairs,),
            in_specs=[spec, spec, spec],
            out_specs=pl.BlockSpec((rows // 2, 128), lambda i, s: (0, i)),
        ),
        compiler_params=pltpu.CompilerParams(vmem_limit_bytes=VMEM_LIMIT),
        cost_estimate=pl.CostEstimate(
            flops=6 * rows * rows * width, bytes_accessed=8 * rows * width, transcendentals=rows * rows * 3
        ),
        name="self_forward",
    )(info, q, k, v)


def cross_fwd_kernel(q_ref, k_ref, v_ref, bias_ref, o_ref):
    block = 256
    for r in range(q_ref.shape[0] // block):
        qq = q_ref[r * block : (r + 1) * block, :]
        total = None
        for h in range(2):
            s = product_nt(pick_head(qq, h), k_ref[...]) + bias_ref[...]
            p = jnp.exp(s - jnp.max(s, axis=1, keepdims=True))
            inv = 1.0 / jnp.sum(p, axis=1, keepdims=True)
            part = product(p.astype(low), pick_head(v_ref[...], h)) * inv
            total = part if total is None else total + part
        o_ref[r * block : (r + 1) * block, :] = total.astype(low)


def cross_forward(q, k, v, bias_row):
    rows, width = q.shape
    keys = k.shape[0]
    return pl.pallas_call(
        cross_fwd_kernel,
        out_shape=jax.ShapeDtypeStruct((rows, width), low),
        grid=(width // 128,),
        in_specs=[
            pl.BlockSpec((rows, 128), lambda i: (0, i)),
            pl.BlockSpec((keys, 128), lambda i: (0, i)),
            pl.BlockSpec((keys, 128), lambda i: (0, i)),
            pl.BlockSpec((1, keys), lambda i: (0, 0)),
        ],
        out_specs=pl.BlockSpec((rows, 128), lambda i: (0, i)),
        compiler_params=pltpu.CompilerParams(vmem_limit_bytes=VMEM_LIMIT),
        cost_estimate=pl.CostEstimate(
            flops=16 * rows * keys * width, bytes_accessed=8 * rows * width, transcendentals=rows * keys * 8
        ),
        name="cross_forward",
    )(q, k, v, bias_row)


def back_kernel(info, q_ref, k_ref, v_ref, g0_ref, g1_ref, g2_ref, g3_ref, bias_ref, dq_ref, dk_ref, dv_ref, dk_acc, dv_acc, *, causal):
    rows = q_ref.shape[0]
    keys_all = k_ref.shape[0]
    block = rows // 4
    k_t = k_ref[...].T
    dk_acc[...] = jnp.zeros_like(dk_acc)
    dv_acc[...] = jnp.zeros_like(dv_acc)
    for qb in range(4):
        keys = (qb + 1) * block if causal else keys_all
        kk, vv = k_ref[:keys, :], v_ref[:keys, :]
        qq = q_ref[qb * block : (qb + 1) * block, :]
        gg = (g0_ref, g1_ref, g2_ref, g3_ref)[qb][...]
        q_parts = []
        for h in range(2):
            q_h, g_h = pick_head(qq, h), pick_head(gg, h)
            s = product_nt(kk, q_h)
            if causal:
                key = lax.broadcasted_iota(jnp.int32, s.shape, 0)
                row = lax.broadcasted_iota(jnp.int32, s.shape, 1) + qb * block
                s = jnp.where((key <= row) & (key < info[1]), s, neg_fill)
            else:
                s = s + jnp.concatenate([bias_ref[...]] * (block // 128), axis=1)
            p = jnp.exp(s - jnp.max(s, axis=0, keepdims=True))
            p = p * (1.0 / jnp.sum(p, axis=0, keepdims=True))
            dp = product_nt(vv, g_h)
            e = jnp.sum(p * dp, axis=0, keepdims=True)
            ds = (p * (dp - e)).astype(low)
            dv_acc[:keys, :] += product(p.astype(low), g_h)
            dk_acc[:keys, :] += product(ds, q_h)
            q_parts.append(product(k_t[h * HEAD_DIM : (h + 1) * HEAD_DIM, :keys], ds))
        dq_t = jnp.concatenate(q_parts, axis=0) * 0.125
        dq_ref[qb * block : (qb + 1) * block, :] = dq_t.T.astype(low)
    dk_ref[...] = dk_acc[...].astype(low)
    dv_ref[...] = dv_acc[...].astype(low)


def attention_back(info, q, k, v, g, bias, causal):
    rows, width = q.shape
    keys = k.shape[0]
    own = pl.BlockSpec((rows, 128), lambda i, s: (0, i))
    wide = pl.BlockSpec((keys, 128), lambda i, s: (0, s[0] + i))
    mine = pl.BlockSpec((keys, 128), lambda i, s: (0, i))

    def g_block(n):
        return pl.BlockSpec((rows // 4, 128), lambda i, s: (s[2 + n] if causal else n, i))

    q_spec = wide if q.shape[1] == k.shape[1] else own
    width = g.shape[1]
    return pl.pallas_call(
        functools.partial(back_kernel, causal=causal),
        out_shape=[
            jax.ShapeDtypeStruct((rows, width), low),
            jax.ShapeDtypeStruct((keys, width), low),
            jax.ShapeDtypeStruct((keys, width), low),
        ],
        grid_spec=pltpu.PrefetchScalarGridSpec(
            num_scalar_prefetch=1,
            grid=(width // 128,),
            in_specs=[q_spec, wide, wide] + [g_block(n) for n in range(4)] + [pl.BlockSpec(bias.shape, lambda i, s: (0, 0))],
            out_specs=[own, mine, mine],
            scratch_shapes=[pltpu.VMEM((keys, 128), jnp.float32), pltpu.VMEM((keys, 128), jnp.float32)],
        ),
        compiler_params=pltpu.CompilerParams(vmem_limit_bytes=VMEM_LIMIT),
        cost_estimate=pl.CostEstimate(
            flops=40 * rows * keys * width // (2 if causal else 1),
            bytes_accessed=14 * rows * width,
            transcendentals=rows * keys * 4,
        ),
        name="self_back" if causal else "cross_back",
    )(info, q, k, v, g, g, g, g, bias)


def pick_kernel(info, in_ref, out_ref):
    out_ref[...] = in_ref[...]


def pick_columns(matrix, size, count, stride, offset):
    rows = matrix.shape[0]
    return pl.pallas_call(
        pick_kernel,
        out_shape=jax.ShapeDtypeStruct((rows, size * count), matrix.dtype),
        grid_spec=pltpu.PrefetchScalarGridSpec(
            num_scalar_prefetch=1,
            grid=(count,),
            in_specs=[pl.BlockSpec((rows, size), lambda n, s: (0, n * stride + s[0]))],
            out_specs=pl.BlockSpec((rows, size), lambda n, s: (0, n)),
        ),
        cost_estimate=pl.CostEstimate(flops=0, bytes_accessed=4 * rows * size * count, transcendentals=0),
        name="pick_columns",
    )(offset.astype(jnp.int32).reshape(1), matrix)


def swap(part, axis, distance):
    count = lax.axis_size(axis)
    return lax.ppermute(part, axis, [(i, i ^ distance) for i in range(count)])


ORDER = (0, 2, 1, 3)


def gather_rows(part):
    pair = jnp.concatenate([part, swap(part, "mem", 2)], axis=0)
    return jnp.concatenate([pair, swap(pair, "mem", 1)], axis=0)


def bits_of(count, first):
    every = [1 << i for i in range(count.bit_length() - 1)]
    return [first] + [d for d in every if d != first]


class Halving:
    def __init__(self, parts, first):
        count = lax.axis_size("dp")
        self.dims = [count]
        self.kept = [a.reshape(count, a.shape[0] // count, a.shape[1]) for a in parts]
        self.left = bits_of(count, first)
        self.done_bits = []
        self.count = count

    def send(self):
        me = lax.axis_index("dp")
        distance = self.left[0]
        below = sum(1 for d in self.left if d < distance)
        low_size = 1 << below
        bit = (me // distance) % 2
        self.mine, theirs = [], []
        for a in self.kept:
            n, r, w = a.shape
            split = a.reshape(n // (2 * low_size), 2, low_size, r, w)
            self.mine.append(lax.dynamic_index_in_dim(split, bit, 1, False).reshape(n // 2, r, w))
            theirs.append(lax.dynamic_index_in_dim(split, 1 - bit, 1, False).reshape(n // 2, r, w))
        return jnp.concatenate([t.astype(low) for t in theirs], axis=2)

    def move(self, sent):
        return swap(sent, "dp", self.left.pop(0))

    def add(self, got):
        start, self.kept = 0, []
        for a in self.mine:
            self.kept.append(a + got[:, :, start : start + a.shape[2]].astype(jnp.float32))
            start += a.shape[2]

    def step(self):
        self.add(self.move(self.send()))

    def finish(self):
        while self.left:
            self.step()
        return [a[0] for a in self.kept]


def tie(*values):
    return lax.optimization_barrier(values)


def finale_kernel(a_ref, b_ref, f_ref, g_ref, h_ref, v_ref,
                  oa_ref, ob_ref, of_ref, og_ref, ov_ref,
                  ay, by, az, bz, gc, gs, gx, vs, vc, vx, vy, vz, send, recv):
    dp, mem = lax.axis_index("dp"), lax.axis_index("mem")
    y, row = dp % 2, dp // 2
    chip, core = mem // 2, mem % 2
    groups = b_ref.shape[0]
    far = a_ref.shape[0]

    def quarter_of(m):
        return 2 * (m % 2) + m // 2

    def block_of(m):
        return (m // 2) + (m % 2) * (3 - 2 * (m // 2))

    barrier = pltpu.get_barrier_semaphore()
    peers = [{"mem": mem ^ 1}, {"mem": mem ^ 2}, {"dp": dp ^ 1}]
    peers += [{"dp": (row ^ j) * 2 + y} for j in range(1, groups)]
    for peer in peers:
        pl.semaphore_signal(barrier, inc=1, device_id=peer, device_id_type=pl.DeviceIdType.MESH)
    pl.semaphore_wait(barrier, len(peers))

    count = [0]
    sent = []

    def start(src, dst, peer):
        n = count[0]
        count[0] += 1
        copy = pltpu.make_async_remote_copy(
            src_ref=src, dst_ref=dst, send_sem=send.at[n], recv_sem=recv.at[n],
            device_id=peer, device_id_type=pl.DeviceIdType.MESH,
        )
        copy.start()
        sent.append(copy)
        return copy

    core_peer, chip_peer, y_peer = peers[:3]
    f32 = jnp.float32

    copy_ay = start(a_ref.at[:, 1 - y], ay, y_peer)
    copy_by = start(b_ref.at[:, 1 - y], by, y_peer)
    mine_q = quarter_of(mem)
    of_ref[mine_q] = f_ref[...]
    copy_fx = start(f_ref, of_ref.at[mine_q], chip_peer)
    copy_fc = start(f_ref, of_ref.at[mine_q], core_peer)
    copy_g1 = start(g_ref.at[block_of(mem ^ 1)], gc.at[0], core_peer)
    copy_g3 = start(g_ref.at[block_of(mem ^ 3)], gc.at[1], core_peer)
    copy_vc = start(v_ref, vc, core_peer)

    copy_g3.wait_recv()
    gs[...] = (g_ref[block_of(mem ^ 2)].astype(f32) + gc[1].astype(f32)).astype(low)
    copy_gx = start(gs, gx, chip_peer)
    copy_vc.wait_recv()
    vs[0] = v_ref[...] + vc[...]
    copy_vx = start(vs.at[0], vx, chip_peer)
    copy_g1.wait_recv()

    copy_vx.wait_recv()
    vs[1] = vs[0] + vx[...]
    copy_vy = start(vs.at[1], vy, y_peer)

    copy_ay.wait_recv()
    own_far = row // 2
    for t in range(far):
        ay[t] = (ay[t].astype(f32) + a_ref[t, y].astype(f32)).astype(low)
    az[own_far] = ay[own_far]
    copies_az = [
        start(ay.at[own_far ^ j], az.at[own_far], {"dp": ((own_far ^ j) * 2 + row % 2) * 2 + y})
        for j in range(1, far)
    ]
    copy_vy.wait_recv()
    vs[2] = vs[1] + vy[...]
    vz[row] = vs[2]
    copies_vz = [start(vs.at[2], vz.at[row], {"dp": (row ^ j) * 2 + y}) for j in range(1, groups)]
    copy_gx.wait_recv()
    block = block_of(mem)
    total = h_ref[...] + g_ref[block].astype(f32) + gc[0].astype(f32) + gx[...].astype(f32)
    og_ref[block] = total.astype(low)
    copy_gax = start(og_ref.at[block], og_ref.at[block], chip_peer)
    copy_gac = start(og_ref.at[block], og_ref.at[block], core_peer)
    copy_by.wait_recv()
    for t in range(groups):
        by[t] = (by[t].astype(f32) + b_ref[t, y].astype(f32)).astype(low)
    bz[row] = by[row]
    copies_bz = [start(by.at[row ^ j], bz.at[row], {"dp": (row ^ j) * 2 + y}) for j in range(1, groups)]

    other_q = quarter_of(mem ^ 2)
    copy_fx.wait_recv()
    copy_fr = start(of_ref.at[other_q], of_ref.at[other_q], core_peer)
    for copy in copies_az:
        copy.wait_recv()
    total = az[0].astype(f32)
    for t in range(1, far):
        total = total + az[t].astype(f32)
    oa_ref[mine_q] = total.astype(low)
    copy_aax = start(oa_ref.at[mine_q], oa_ref.at[mine_q], chip_peer)
    copy_aac = start(oa_ref.at[mine_q], oa_ref.at[mine_q], core_peer)
    copy_gax.wait_recv()
    other = block_of(mem ^ 2)
    copy_gr = start(og_ref.at[other], og_ref.at[other], core_peer)
    for copy in copies_vz:
        copy.wait_recv()
    total = vz[0]
    for t in range(1, groups):
        total = total + vz[t]
    ov_ref[...] = total
    for copy in copies_bz:
        copy.wait_recv()
    total = bz[0].astype(f32)
    for t in range(1, groups):
        total = total + bz[t].astype(f32)
    ob_ref[mine_q] = total.astype(low)
    copy_bax = start(ob_ref.at[mine_q], ob_ref.at[mine_q], chip_peer)
    copy_bac = start(ob_ref.at[mine_q], ob_ref.at[mine_q], core_peer)
    copy_aax.wait_recv()
    copy_ar = start(oa_ref.at[other_q], oa_ref.at[other_q], core_peer)
    copy_bax.wait_recv()
    copy_br = start(ob_ref.at[other_q], ob_ref.at[other_q], core_peer)
    for copy in (copy_fc, copy_gac, copy_aac, copy_bac, copy_fr, copy_gr, copy_ar, copy_br):
        copy.wait_recv()
    for copy in sent:
        copy.wait_send()


def finale(a, b, f, g, h, v):
    far, groups = a.shape[0], b.shape[0]
    r, wa, wb, wf = a.shape[2], a.shape[3], b.shape[3], f.shape[1]
    copies = 17 + (far - 1) + 2 * (groups - 1) + 4
    vmem = pl.BlockSpec(memory_space=pltpu.VMEM)
    f32 = jnp.float32
    return pl.pallas_call(
        finale_kernel,
        out_shape=[
            jax.ShapeDtypeStruct((4, r, wa), low),
            jax.ShapeDtypeStruct((4, r, wb), low),
            jax.ShapeDtypeStruct((4, r, wf), low),
            jax.ShapeDtypeStruct(g.shape, low),
            jax.ShapeDtypeStruct(v.shape, f32),
        ],
        in_specs=[vmem] * 6,
        out_specs=[vmem] * 5,
        scratch_shapes=[
            pltpu.VMEM((far, r, wa), low),
            pltpu.VMEM((groups, r, wb), low),
            pltpu.VMEM((far, r, wa), low),
            pltpu.VMEM((groups, r, wb), low),
            pltpu.VMEM((2,) + g.shape[1:], low),
            pltpu.VMEM(g.shape[1:], low),
            pltpu.VMEM(g.shape[1:], low),
            pltpu.VMEM((3,) + v.shape, f32),
            pltpu.VMEM(v.shape, f32),
            pltpu.VMEM(v.shape, f32),
            pltpu.VMEM(v.shape, f32),
            pltpu.VMEM((groups,) + v.shape, f32),
            pltpu.SemaphoreType.DMA((copies,)),
            pltpu.SemaphoreType.DMA((copies,)),
        ],
        compiler_params=pltpu.CompilerParams(
            collective_id=0, has_side_effects=True, vmem_limit_bytes=VMEM_LIMIT
        ),
        cost_estimate=pl.CostEstimate(flops=10**6, bytes_accessed=10**8, transcendentals=0),
        name="finale",
    )(a, b, f, g, h, v)


def unpack_kernel(a_ref, b_ref, f_ref, g_ref, qkv_ref, so_ref, cq_ref, ckv_ref, co_ref, fi_ref, fo_ref, gd_ref, *, quarter, piece):
    f32 = jnp.float32

    def spread(source, start, count, size, target):
        for p in range(4):
            for n in range(count):
                target[:, (n * 4 + p) * size : (n * 4 + p + 1) * size] = source[
                    p, :, start + n * size : start + (n + 1) * size
                ].astype(f32)

    spread(b_ref, 0, 3, quarter, qkv_ref)
    spread(a_ref, 0, 1, quarter, co_ref)
    spread(a_ref, quarter, 1, quarter, cq_ref)
    spread(a_ref, 2 * quarter, 2, quarter, ckv_ref)
    spread(a_ref, 4 * quarter, 1, quarter, so_ref)
    spread(f_ref, 0, quarter * 4 // piece, piece, fi_ref)
    for p in range(4):
        fo_ref[p] = f_ref[p, :, 4 * quarter :].astype(f32)
        gd_ref[p] = g_ref[p].astype(f32)


def unpack(a, b, f, g, width, hidden, piece):
    r = a.shape[1]
    steps = 4 if r % 64 == 0 else 1
    h, gh = r // steps, g.shape[1] // steps
    f32 = jnp.float32

    def slots(x, n):
        return pl.BlockSpec((4, n, x.shape[2]), lambda i: (0, i, 0))

    wide = [3 * width, width, width, 2 * width, width, hidden]
    return pl.pallas_call(
        functools.partial(unpack_kernel, quarter=width // 4, piece=piece),
        out_shape=[jax.ShapeDtypeStruct((r, w), f32) for w in wide]
        + [jax.ShapeDtypeStruct((4, r, width), f32), jax.ShapeDtypeStruct(g.shape, f32)],
        grid=(steps,),
        in_specs=[slots(a, h), slots(b, h), slots(f, h), slots(g, gh)],
        out_specs=[pl.BlockSpec((h, w), lambda i: (i, 0)) for w in wide]
        + [pl.BlockSpec((4, h, width), lambda i: (0, i, 0)), slots(g, gh)],
        compiler_params=pltpu.CompilerParams(vmem_limit_bytes=VMEM_LIMIT),
        cost_estimate=pl.CostEstimate(flops=10**6, bytes_accessed=2 * 10**7, transcendentals=0),
        name="unpack",
    )(a, b, f, g)


def per_device(
    dec_in,
    memory,
    dec_len,
    mem_len,
    grad_out,
    self_qkv,
    self_out,
    cross_q,
    cross_kv,
    cross_out,
    ffn_in,
    ffn_out,
    proj_bias,
    ffn_bias,
    norm_gain,
    norm_shift,
):
    x_full = dec_in[0]
    rows, width = x_full.shape
    hidden = ffn_in.shape[1]
    block = rows // 4
    half, quarter = width // 2, width // 4
    groups = lax.axis_size("dp")
    mem_rows = memory[0]
    mem_block = mem_rows.shape[0]
    me = lax.axis_index("mem")
    chip, core = me // 2, me % 2
    quart = 2 * core + chip

    def block_of(m):
        return jnp.where(m // 2 == 0, 3 * (m % 2), 1 + m % 2)

    def cut(a, start, size, axis=1):
        return lax.dynamic_slice_in_dim(a, start, size, axis)

    def own_rows(a):
        return cut(a, block_of(me) * block, block, 0)

    def by_block(gathered):
        size = gathered.shape[0] // 4
        where = [0, 2, 3, 1]
        pieces = []
        for n in range(4):
            offset = me ^ where[n]
            slot = (offset % 2) * 2 + offset // 2
            pieces.append(cut(gathered, slot * size, size, 0))
        return jnp.concatenate(pieces, axis=0)

    def by_quarter(slots):
        stacked = jnp.stack(slots)
        where = [0, 2, 1, 3]
        out = []
        for n in range(4):
            offset = me ^ where[n]
            out.append(lax.dynamic_index_in_dim(stacked, (offset % 2) * 2 + offset // 2, 0, False))
        return out

    mem_full = gather_rows(mem_rows)

    side = core * half
    q8 = ((product(x_full, cut(self_qkv, side, half)) + cut(proj_bias[0], side, half, 0)) * 0.125).astype(low)
    k8 = product(x_full, cut(self_qkv, width + side, half)).astype(low)
    v8 = (product(x_full, cut(self_qkv, 2 * width + side, half)) + cut(proj_bias[1], side, half, 0)).astype(low)
    info_f = jnp.stack([chip, dec_len[0]]).astype(jnp.int32)
    att8 = self_forward(info_f, q8, k8, v8)

    def heads_to_rows(a8):
        mine = cut(a8, core * block, block, 0)
        other = swap(cut(a8, (1 - core) * block, block, 0), "mem", 1)
        return jnp.where(
            core == 0, jnp.concatenate([mine, other], axis=1), jnp.concatenate([other, mine], axis=1)
        )

    attended = heads_to_rows(att8)
    x_own = own_rows(x_full).astype(jnp.float32)
    first, first_norm, first_inv = normalize(
        x_own + product(attended, self_out) + proj_bias[2], norm_gain[0], norm_shift[0]
    )
    first_low = first.astype(low)
    first_other = swap(first_low, "mem", 1)
    first_chip = jnp.where(
        core == 0,
        jnp.concatenate([first_low, first_other], axis=0),
        jnp.concatenate([first_other, first_low], axis=0),
    )

    cq8 = ((product(first_chip, cut(cross_q, side, half)) + cut(proj_bias[3], side, half, 0)) * 0.125).astype(low)
    kc8 = product(mem_full, cut(cross_kv, side, half)).astype(low)
    vc8 = (product(mem_full, cut(cross_kv, width + side, half)) + cut(proj_bias[4], side, half, 0)).astype(low)
    slot_pos = jnp.stack([(me ^ k) * mem_block for k in ORDER])
    mem_pos = (slot_pos[:, None] + jnp.arange(mem_block, dtype=jnp.int32)[None, :]).reshape(-1)
    mem_bias = jnp.where(mem_pos < mem_len[0], 0.0, neg_fill).astype(jnp.float32)
    crossed = heads_to_rows(cross_forward(cq8, kc8, vc8, mem_bias[None, :]))
    second, second_norm, second_inv = normalize(
        first + product(crossed, cross_out) + proj_bias[5], norm_gain[1], norm_shift[1]
    )
    second_low = second.astype(low)

    act, act_grad = gelu_parts(product(second_low, ffn_in) + ffn_bias)
    act, act_grad = act.astype(low), act_grad.astype(low)
    third, third_norm, third_inv = normalize(
        second + product(act, ffn_out) + proj_bias[6], norm_gain[2], norm_shift[2]
    )
    row_pos = block_of(me) * block + jnp.arange(block, dtype=jnp.int32)
    cot = jnp.where((row_pos < dec_len[0])[:, None], own_rows(grad_out[0]).astype(jnp.float32), 0.0)
    dh3, gain_three, shift_three = norm_back(cot, third_norm, third_inv, norm_gain[2])
    dz = dh3.astype(low)
    du = (product_nt(dz, ffn_out) * act_grad.astype(jnp.float32)).astype(low)
    dh2, gain_two, shift_two = norm_back(
        dh3 + product_nt(du, ffn_in), second_norm, second_inv, norm_gain[1]
    )
    dco = dh2.astype(low)

    second_full = gather_rows(second_low)
    dz_full = gather_rows(dz)
    dco_full = gather_rows(dco)
    piece = hidden // groups // 4
    if piece % 128 == 0:
        w_in_q = pick_columns(ffn_in, piece, groups, 4, quart)
    else:
        w_in_q = lax.dynamic_index_in_dim(ffn_in.reshape(width, groups, 4, piece), quart, 2, False)
        w_in_q = w_in_q.reshape(width, hidden // 4)
    w_out_q = lax.dynamic_index_in_dim(ffn_out.reshape(groups, 4, piece, width), quart, 1, False)
    w_out_q = w_out_q.reshape(hidden // 4, width)
    b_in_q = lax.dynamic_index_in_dim(ffn_bias.reshape(groups, 4, piece), quart, 1, False).reshape(-1)
    act_q, slope_q = gelu_parts(product(second_full, w_in_q) + b_in_q)
    act_q = act_q.astype(low)
    du_q = (product_nt(dz_full, w_out_q) * slope_q).astype(low)
    sum_in = Halving([product_tn(second_full, du_q)], 1)
    sum_out = Halving([product_tn(act_q, dz_full)], min(2, groups // 2))
    send_in, send_out = sum_in.send(), sum_out.send()

    first_full = gather_rows(first_low)
    wide = quart * quarter
    cq4 = ((product(first_full, cut(cross_q, wide, quarter)) + cut(proj_bias[3], wide, quarter, 0)) * 0.125).astype(low)
    dx4 = product_nt(dco_full, cut(cross_out, wide, quarter, 0)).astype(low)
    pair_base = chip * (quarter // 128)
    info_c = jnp.stack([pair_base]).astype(jnp.int32)
    bias_col = jnp.broadcast_to(mem_bias[:, None], (mem_bias.shape[0], 128))
    dx4, send_in, send_out = tie(dx4, send_in, send_out)
    got_in, got_out = sum_in.move(send_in), sum_out.move(send_out)
    dq4, dkc4, dvc4 = attention_back(info_c, cq4, kc8, vc8, dx4, bias_col, False)
    dq4, dkc4, dvc4, got_in, got_out = tie(dq4, dkc4, dvc4, got_in, got_out)
    sum_in.add(got_in)
    sum_out.add(got_out)
    dkv4 = jnp.concatenate([dkc4, dvc4], axis=1)

    def to_rows(a):
        b0, b2, b1, b3 = jnp.split(a, 4, axis=0)
        over = swap(jnp.concatenate([b2, b3], axis=0), "mem", 2)
        size = b0.shape[0]
        mine = jnp.concatenate([b0, over[:size]], axis=0)
        other = swap(jnp.concatenate([b1, over[size:]], axis=0), "mem", 1)
        return by_quarter([mine[:size], mine[size:], other[:size], other[size:]])

    dq_own = jnp.concatenate(to_rows(dq4), axis=1)
    dkv_parts = to_rows(dkv4)
    dkv_own = jnp.concatenate(
        [a[:, :quarter] for a in dkv_parts] + [a[:, quarter:] for a in dkv_parts], axis=1
    )
    grad_memory = product_nt(dkv_own, cross_kv)[None]
    crossed_full = gather_rows(crossed)
    attended_full = gather_rows(attended)
    send_in, send_out = sum_in.send(), sum_out.send()
    got_in, got_out = sum_in.move(send_in), sum_out.move(send_out)

    dh1, gain_one, shift_one = norm_back(
        dh2 + product_nt(dq_own, cross_q), first_norm, first_inv, norm_gain[0]
    )
    do = dh1.astype(low)
    do_full = gather_rows(do)
    sum_cross = Halving(
        [
            product_tn(crossed_full, cut(dco_full, wide, quarter)),
            product_tn(first_full, dq4),
            product_tn(mem_full, dkv4),
            product_tn(attended_full, cut(do_full, wide, quarter)),
        ],
        min(2, groups // 2),
    )
    send_cross = sum_cross.send()

    da4 = product_nt(do_full, cut(self_out, wide, quarter, 0)).astype(low)
    where = [0, 2, 3, 1]
    slots = [((me ^ n) % 2) * 2 + (me ^ n) // 2 for n in where]
    info_s = jnp.stack([pair_base, dec_len[0]] + slots).astype(jnp.int32)
    da4, got_in, got_out, send_cross = tie(da4, got_in, got_out, send_cross)
    sum_in.add(got_in)
    sum_out.add(got_out)
    send_in, send_out = sum_in.send(), sum_out.send()
    da4, send_in, send_out = tie(da4, send_in, send_out)
    got_in, got_out, got_cross = sum_in.move(send_in), sum_out.move(send_out), sum_cross.move(send_cross)
    sq4, sk4, sv4 = attention_back(info_s, q8, k8, v8, da4, bias_col[:8], True)
    sq4, sk4, sv4, got_in, got_out, got_cross = tie(sq4, sk4, sv4, got_in, got_out, got_cross)
    sum_in.add(got_in)
    sum_out.add(got_out)
    sum_cross.add(got_cross)
    (g_in,), (g_out,) = sum_in.finish(), sum_out.finish()

    dqkv4 = jnp.concatenate([sq4, sk4, sv4], axis=1)
    per = width // groups
    qkv_grad = product_tn(x_full, dqkv4).astype(low).reshape(groups // 2, 2, per, 3 * quarter)
    qkv_q = jnp.concatenate([cut(self_qkv, n * width + wide, quarter) for n in range(3)], axis=1)
    partial = product_nt(dqkv4, qkv_q).astype(low).reshape(4, block, width)
    cross_grad = jnp.concatenate([part.astype(low) for part in sum_cross.kept], axis=2)
    cross_grad = cross_grad.reshape(groups // 4, 2, per, cross_grad.shape[2])
    ffn_grad = jnp.concatenate([g_in.astype(low), g_out.astype(low)], axis=1)
    layer_out = by_block(gather_rows(third.astype(low)))[None]

    place = jnp.zeros((2, width), jnp.float32)
    own_sums = jnp.stack([column_sum(sq4), column_sum(sv4)])
    place = lax.dynamic_update_slice(place, own_sums, (0, quart * quarter))
    packed = jnp.concatenate(
        [
            place,
            jnp.stack(
                [
                    column_sum(do),
                    column_sum(dq_own),
                    column_sum(dkv_own[:, width:]),
                    column_sum(dco),
                    column_sum(dz),
                    gain_one,
                    gain_two,
                    gain_three,
                    shift_one,
                    shift_two,
                    shift_three,
                ]
            ),
            column_sum(du).reshape(hidden // width, width),
        ],
        axis=0,
    )
    packed = jnp.pad(packed, ((0, -packed.shape[0] % 8), (0, 0)))
    cross_w, qkv_w, ffn_w, grad_rows, packed = finale(cross_grad, qkv_grad, ffn_grad, partial, dh1, packed)
    w_qkv, w_so, w_cq, w_ckv, w_co, w_fi, w_fo, grad_dec = unpack(
        cross_w, qkv_w, ffn_w, grad_rows, width, hidden, piece
    )
    return (
        layer_out,
        grad_dec.reshape(1, rows, width),
        grad_memory,
        w_qkv,
        w_so,
        w_cq,
        w_ckv,
        w_co,
        w_fi,
        w_fo.reshape(-1, width),
        packed[:7],
        packed[13 : 13 + hidden // width].reshape(hidden),
        packed[7:10],
        packed[10:13],
    )


def solution(mesh):
    in_specs = (
        P("dp", None, None),
        P("dp", "mem", None),
        P("dp"),
        P("dp"),
        P("dp", None, None),
    ) + (P(),) * 11
    out_specs = (
        P("dp", None, None),
        P("dp", None, None),
        P("dp", "mem", None),
    ) + (P("dp", None),) * 7 + (P(),) * 4
    return jax.shard_map(
        per_device, mesh=mesh, in_specs=in_specs, out_specs=out_specs, check_vma=False
    )
```

```python
import functools

import jax
import jax.numpy as jnp
from jax import lax
from jax.experimental import pallas as pl
from jax.experimental.pallas import tpu as pltpu
from jax.sharding import PartitionSpec as P

HEAD_DIM = 64
norm_eps = 1e-05
neg_fill = -1e30
low = jnp.bfloat16
VMEM_LIMIT = 56 * 1024 * 1024


def product(left_rows, right_rows):
    return jnp.dot(left_rows, right_rows, preferred_element_type=jnp.float32)


def product_tn(left_rows, right_rows):
    return lax.dot_general(
        left_rows, right_rows, (((0,), (0,)), ((), ())), preferred_element_type=jnp.float32
    )


def product_nt(left_rows, right_rows):
    return lax.dot_general(
        left_rows, right_rows, (((1,), (1,)), ((), ())), preferred_element_type=jnp.float32
    )


def normalize(hidden, scale_row, shift_row):
    row_mean = jnp.mean(hidden, axis=-1, keepdims=True)
    centered = hidden - row_mean
    variance = jnp.mean(centered * centered, axis=-1, keepdims=True)
    inverse = lax.rsqrt(variance + norm_eps)
    normed = centered * inverse
    return (normed * scale_row + shift_row, normed, inverse)


def norm_back(grad_rows, normed, inverse, scale_row):
    scaled = grad_rows * scale_row
    grad_hidden = inverse * (
        scaled
        - jnp.mean(scaled, axis=-1, keepdims=True)
        - normed * jnp.mean(scaled * normed, axis=-1, keepdims=True)
    )
    return (grad_hidden, jnp.sum(grad_rows * normed, axis=0), jnp.sum(grad_rows, axis=0))


def gelu_parts(values):
    cdf = 0.5 * (1.0 + lax.erf(values * 0.7071067811865476))
    density = jnp.exp(-0.5 * values * values) * 0.3989422804014327
    return values * cdf, cdf + values * density


def column_sum(matrix):
    return jnp.sum(matrix.astype(jnp.float32), axis=0)


def lane_head(rows):
    return lax.broadcasted_iota(jnp.int32, (rows, 128), 1) // HEAD_DIM


def pick_head(pair, h):
    return jnp.where(lane_head(pair.shape[0]) == h, pair, jnp.zeros_like(pair))


def self_fwd_kernel(info, q_ref, k_ref, v_ref, o_ref):
    rows = k_ref.shape[0]
    block = rows // 4
    dec_len = info[1]

    def process(qb, slot):
        keys = (qb + 1) * block
        kk, vv = k_ref[:keys, :], v_ref[:keys, :]
        qq = q_ref[qb * block : (qb + 1) * block, :]
        total = None
        for h in range(2):
            s = product_nt(pick_head(qq, h), kk)
            col = lax.broadcasted_iota(jnp.int32, s.shape, 1)
            row = lax.broadcasted_iota(jnp.int32, s.shape, 0) + qb * block
            s = jnp.where((col <= row) & (col < dec_len), s, neg_fill)
            p = jnp.exp(s - jnp.max(s, axis=1, keepdims=True))
            inv = 1.0 / jnp.sum(p, axis=1, keepdims=True)
            part = product(p.astype(low), pick_head(vv, h)) * inv
            total = part if total is None else total + part
        o_ref[slot * block : (slot + 1) * block, :] = total.astype(low)

    @pl.when(info[0] == 0)
    def _():
        process(0, 0)
        process(3, 1)

    @pl.when(info[0] == 1)
    def _():
        process(1, 0)
        process(2, 1)


def self_forward(info, q, k, v):
    rows, width = q.shape
    pairs = width // 128
    spec = pl.BlockSpec((rows, 128), lambda i, s: (0, i))
    return pl.pallas_call(
        self_fwd_kernel,
        out_shape=jax.ShapeDtypeStruct((rows // 2, width), low),
        grid_spec=pltpu.PrefetchScalarGridSpec(
            num_scalar_prefetch=1,
            grid=(pairs,),
            in_specs=[spec, spec, spec],
            out_specs=pl.BlockSpec((rows // 2, 128), lambda i, s: (0, i)),
        ),
        compiler_params=pltpu.CompilerParams(vmem_limit_bytes=VMEM_LIMIT),
        cost_estimate=pl.CostEstimate(
            flops=6 * rows * rows * width, bytes_accessed=8 * rows * width, transcendentals=rows * rows * 3
        ),
        name="self_forward",
    )(info, q, k, v)


def cross_fwd_kernel(q_ref, k_ref, v_ref, bias_ref, o_ref):
    block = 256
    for r in range(q_ref.shape[0] // block):
        qq = q_ref[r * block : (r + 1) * block, :]
        total = None
        for h in range(2):
            s = product_nt(pick_head(qq, h), k_ref[...]) + bias_ref[...]
            p = jnp.exp(s - jnp.max(s, axis=1, keepdims=True))
            inv = 1.0 / jnp.sum(p, axis=1, keepdims=True)
            part = product(p.astype(low), pick_head(v_ref[...], h)) * inv
            total = part if total is None else total + part
        o_ref[r * block : (r + 1) * block, :] = total.astype(low)


def cross_forward(q, k, v, bias_row):
    rows, width = q.shape
    keys = k.shape[0]
    return pl.pallas_call(
        cross_fwd_kernel,
        out_shape=jax.ShapeDtypeStruct((rows, width), low),
        grid=(width // 128,),
        in_specs=[
            pl.BlockSpec((rows, 128), lambda i: (0, i)),
            pl.BlockSpec((keys, 128), lambda i: (0, i)),
            pl.BlockSpec((keys, 128), lambda i: (0, i)),
            pl.BlockSpec((1, keys), lambda i: (0, 0)),
        ],
        out_specs=pl.BlockSpec((rows, 128), lambda i: (0, i)),
        compiler_params=pltpu.CompilerParams(vmem_limit_bytes=VMEM_LIMIT),
        cost_estimate=pl.CostEstimate(
            flops=16 * rows * keys * width, bytes_accessed=8 * rows * width, transcendentals=rows * keys * 8
        ),
        name="cross_forward",
    )(q, k, v, bias_row)


def back_kernel(info, q_ref, k_ref, v_ref, g0_ref, g1_ref, g2_ref, g3_ref, bias_ref, dq_ref, dk_ref, dv_ref, dk_acc, dv_acc, *, causal):
    rows = q_ref.shape[0]
    keys_all = k_ref.shape[0]
    block = rows // 4
    k_t = k_ref[...].T
    dk_acc[...] = jnp.zeros_like(dk_acc)
    dv_acc[...] = jnp.zeros_like(dv_acc)
    for qb in range(4):
        keys = (qb + 1) * block if causal else keys_all
        kk, vv = k_ref[:keys, :], v_ref[:keys, :]
        qq = q_ref[qb * block : (qb + 1) * block, :]
        gg = (g0_ref, g1_ref, g2_ref, g3_ref)[qb][...]
        q_parts = []
        for h in range(2):
            q_h, g_h = pick_head(qq, h), pick_head(gg, h)
            s = product_nt(kk, q_h)
            if causal:
                key = lax.broadcasted_iota(jnp.int32, s.shape, 0)
                row = lax.broadcasted_iota(jnp.int32, s.shape, 1) + qb * block
                s = jnp.where((key <= row) & (key < info[1]), s, neg_fill)
            else:
                s = s + jnp.concatenate([bias_ref[...]] * (block // 128), axis=1)
            p = jnp.exp(s - jnp.max(s, axis=0, keepdims=True))
            p = p * (1.0 / jnp.sum(p, axis=0, keepdims=True))
            dp = product_nt(vv, g_h)
            e = jnp.sum(p * dp, axis=0, keepdims=True)
            ds = (p * (dp - e)).astype(low)
            dv_acc[:keys, :] += product(p.astype(low), g_h)
            dk_acc[:keys, :] += product(ds, q_h)
            q_parts.append(product(k_t[h * HEAD_DIM : (h + 1) * HEAD_DIM, :keys], ds))
        dq_t = jnp.concatenate(q_parts, axis=0) * 0.125
        dq_ref[qb * block : (qb + 1) * block, :] = dq_t.T.astype(low)
    dk_ref[...] = dk_acc[...].astype(low)
    dv_ref[...] = dv_acc[...].astype(low)


def attention_back(info, q, k, v, g, bias, causal):
    rows, width = q.shape
    keys = k.shape[0]
    own = pl.BlockSpec((rows, 128), lambda i, s: (0, i))
    wide = pl.BlockSpec((keys, 128), lambda i, s: (0, s[0] + i))
    mine = pl.BlockSpec((keys, 128), lambda i, s: (0, i))

    def g_block(n):
        return pl.BlockSpec((rows // 4, 128), lambda i, s: (s[2 + n] if causal else n, i))

    q_spec = wide if q.shape[1] == k.shape[1] else own
    width = g.shape[1]
    return pl.pallas_call(
        functools.partial(back_kernel, causal=causal),
        out_shape=[
            jax.ShapeDtypeStruct((rows, width), low),
            jax.ShapeDtypeStruct((keys, width), low),
            jax.ShapeDtypeStruct((keys, width), low),
        ],
        grid_spec=pltpu.PrefetchScalarGridSpec(
            num_scalar_prefetch=1,
            grid=(width // 128,),
            in_specs=[q_spec, wide, wide] + [g_block(n) for n in range(4)] + [pl.BlockSpec(bias.shape, lambda i, s: (0, 0))],
            out_specs=[own, mine, mine],
            scratch_shapes=[pltpu.VMEM((keys, 128), jnp.float32), pltpu.VMEM((keys, 128), jnp.float32)],
        ),
        compiler_params=pltpu.CompilerParams(vmem_limit_bytes=VMEM_LIMIT),
        cost_estimate=pl.CostEstimate(
            flops=40 * rows * keys * width // (2 if causal else 1),
            bytes_accessed=14 * rows * width,
            transcendentals=rows * keys * 4,
        ),
        name="self_back" if causal else "cross_back",
    )(info, q, k, v, g, g, g, g, bias)


def self_weights_kernel(info, x_ref, q_ref, k_ref, v_ref, wq_ref, wk_ref, wv_ref, grad_ref, part_ref, sums_ref):
    block = part_ref.shape[0]
    size = q_ref.shape[1]
    at = pl.ds(pl.multiple_of(pl.program_id(0) * block, block), block)
    total = None
    for n, (d_ref, w_ref) in enumerate(((q_ref, wq_ref), (k_ref, wk_ref), (v_ref, wv_ref))):
        grad_ref[:, n * size : (n + 1) * size] = product_tn(x_ref[...], d_ref[...]).astype(low)
        part = product_nt(d_ref[at, :], w_ref[...])
        total = part if total is None else total + part
    part_ref[...] = total.astype(low)

    @pl.when(pl.program_id(0) == 0)
    def _():
        sums_ref[...] = jnp.zeros_like(sums_ref)
        sums_ref[0:1, :] = jnp.sum(q_ref[...].astype(jnp.float32), axis=0, keepdims=True)
        sums_ref[1:2, :] = jnp.sum(v_ref[...].astype(jnp.float32), axis=0, keepdims=True)


def self_weights(quart, x, dq, dk, dv, weight):
    rows, width = x.shape
    size = dq.shape[1]
    block = 256
    whole = pl.BlockSpec((rows, size), lambda i, s: (0, 0))

    def slab(n):
        return pl.BlockSpec((width, size), lambda i, s: (0, n * (width // size) + s[0]))

    return pl.pallas_call(
        self_weights_kernel,
        out_shape=[
            jax.ShapeDtypeStruct((width, 3 * size), low),
            jax.ShapeDtypeStruct((rows, width), low),
            jax.ShapeDtypeStruct((8, size), jnp.float32),
        ],
        grid_spec=pltpu.PrefetchScalarGridSpec(
            num_scalar_prefetch=1,
            grid=(rows // block,),
            in_specs=[pl.BlockSpec((rows, block), lambda i, s: (0, i)), whole, whole, whole, slab(0), slab(1), slab(2)],
            out_specs=[
                pl.BlockSpec((block, 3 * size), lambda i, s: (i, 0)),
                pl.BlockSpec((block, width), lambda i, s: (i, 0)),
                pl.BlockSpec((8, size), lambda i, s: (0, 0)),
            ],
        ),
        compiler_params=pltpu.CompilerParams(vmem_limit_bytes=VMEM_LIMIT),
        cost_estimate=pl.CostEstimate(
            flops=12 * rows * width * size, bytes_accessed=20 * rows * width, transcendentals=0
        ),
        name="self_weights",
    )(quart.astype(jnp.int32).reshape(1), x, dq, dk, dv, weight, weight, weight)


def pick_kernel(info, in_ref, out_ref):
    out_ref[...] = in_ref[...]


def pick_columns(matrix, size, count, stride, offset):
    rows = matrix.shape[0]
    return pl.pallas_call(
        pick_kernel,
        out_shape=jax.ShapeDtypeStruct((rows, size * count), matrix.dtype),
        grid_spec=pltpu.PrefetchScalarGridSpec(
            num_scalar_prefetch=1,
            grid=(count,),
            in_specs=[pl.BlockSpec((rows, size), lambda n, s: (0, n * stride + s[0]))],
            out_specs=pl.BlockSpec((rows, size), lambda n, s: (0, n)),
        ),
        cost_estimate=pl.CostEstimate(flops=0, bytes_accessed=4 * rows * size * count, transcendentals=0),
        name="pick_columns",
    )(offset.astype(jnp.int32).reshape(1), matrix)


def swap(part, axis, distance):
    count = lax.axis_size(axis)
    return lax.ppermute(part, axis, [(i, i ^ distance) for i in range(count)])


ORDER = (0, 2, 1, 3)


def gather_rows(part):
    pair = jnp.concatenate([part, swap(part, "mem", 2)], axis=0)
    return jnp.concatenate([pair, swap(pair, "mem", 1)], axis=0)


def bits_of(count, first):
    every = [1 << i for i in range(count.bit_length() - 1)]
    return [first] + [d for d in every if d != first]


def join(part, far):
    pair = jnp.concatenate([part, far], axis=0)
    return jnp.concatenate([pair, swap(pair, "mem", 1)], axis=0)


class Halving:
    def __init__(self, parts, first):
        count = lax.axis_size("dp")
        self.dims = [count]
        self.kept = [a.reshape(count, a.shape[0] // count, a.shape[1]) for a in parts]
        self.left = bits_of(count, first)
        self.done_bits = []
        self.count = count

    def send(self):
        me = lax.axis_index("dp")
        distance = self.left[0]
        below = sum(1 for d in self.left if d < distance)
        low_size = 1 << below
        bit = (me // distance) % 2
        self.mine, theirs = [], []
        for a in self.kept:
            n, r, w = a.shape
            split = a.reshape(n // (2 * low_size), 2, low_size, r, w)
            self.mine.append(lax.dynamic_index_in_dim(split, bit, 1, False).reshape(n // 2, r, w))
            theirs.append(lax.dynamic_index_in_dim(split, 1 - bit, 1, False).reshape(n // 2, r, w))
        return jnp.concatenate([t.astype(low) for t in theirs], axis=2)

    def move(self, sent):
        return swap(sent, "dp", self.left.pop(0))

    def add(self, got):
        start, self.kept = 0, []
        for a in self.mine:
            self.kept.append(a + got[:, :, start : start + a.shape[2]].astype(jnp.float32))
            start += a.shape[2]

    def step(self):
        self.add(self.move(self.send()))

    def finish(self):
        while self.left:
            self.step()
        return [a[0] for a in self.kept]


def tie(*values):
    return lax.optimization_barrier(values)


def finale_kernel(c_ref, f_ref, e_ref, s_ref, b_ref, g_ref, h_ref, v_ref,
                  oc_ref, of_ref, os_ref, ob_ref, og_ref, ov_ref,
                  by, bz, sz, gc, gs, gx, vs, vc, vx, vy, vz, send, recv):
    dp, mem = lax.axis_index("dp"), lax.axis_index("mem")
    y, row = dp % 2, dp // 2
    groups = b_ref.shape[0]
    f32 = jnp.float32
    wide = b_ref.shape[3] // 2
    tall = h_ref.shape[0] // 2

    def quarter_of(m):
        return 2 * (m % 2) + m // 2

    def block_of(m):
        return (m // 2) + (m % 2) * (3 - 2 * (m // 2))

    barrier = pltpu.get_barrier_semaphore()
    core_peer, chip_peer, y_peer = {"mem": mem ^ 1}, {"mem": mem ^ 2}, {"dp": dp ^ 1}
    row_peers = [{"dp": (row ^ j) * 2 + y} for j in range(1, groups)]
    peers = [core_peer, chip_peer, y_peer] + row_peers
    for peer in peers:
        pl.semaphore_signal(barrier, inc=1, device_id=peer, device_id_type=pl.DeviceIdType.MESH)
    pl.semaphore_wait(barrier, len(peers))

    sent = []

    def start(src, dst, peer):
        n = len(sent)
        copy = pltpu.make_async_remote_copy(
            src_ref=src, dst_ref=dst, send_sem=send.at[n], recv_sem=recv.at[n],
            device_id=peer, device_id_type=pl.DeviceIdType.MESH,
        )
        copy.start()
        sent.append(copy)
        return copy

    def to_rows(source, target, own):
        return [start(source(row ^ j), target(own), row_peers[j - 1]) for j in range(1, groups)]

    def wait_all(copies):
        for copy in copies:
            copy.wait_recv()

    def columns(n):
        return pl.ds(n * wide, wide)

    def lines(n):
        return pl.ds(n * tall, tall)

    mine_q, other_q = quarter_of(mem), quarter_of(mem ^ 2)
    block, other = block_of(mem), block_of(mem ^ 2)

    copy_vy = start(v_ref, vy, y_peer)
    copies_by = [start(b_ref.at[:, 1 - y, :, columns(n)], by.at[:, :, columns(n)], y_peer) for n in range(2)]
    copy_g3 = start(g_ref.at[block_of(mem ^ 3)], gc.at[1], core_peer)
    copy_cx = start(c_ref, oc_ref.at[mine_q], chip_peer)
    copies_sz = to_rows(lambda t: s_ref.at[t], lambda t: sz.at[t], row)
    copy_g1 = start(g_ref.at[block_of(mem ^ 1)], gc.at[0], core_peer)
    copy_cc = start(c_ref, oc_ref.at[mine_q], core_peer)
    copy_f0 = start(f_ref, of_ref.at[mine_q], core_peer)
    copy_f1 = start(e_ref, of_ref.at[other_q], core_peer)
    sz[row] = s_ref[row]

    copy_g3.wait_recv()
    copies_gx = []
    for n in range(2):
        gs[lines(n)] = (g_ref[other, lines(n)].astype(f32) + gc[1, lines(n)].astype(f32)).astype(low)
        copies_gx.append(start(gs.at[lines(n)], gx.at[lines(n)], chip_peer))
    copy_vy.wait_recv()
    vs[0] = v_ref[...] + vy[...]
    vz[row] = vs[0]
    copies_vz = to_rows(lambda t: vs.at[0], lambda t: vz.at[t], row)
    oc_ref[mine_q] = c_ref[...]
    of_ref[mine_q] = f_ref[...]
    of_ref[other_q] = e_ref[...]
    copy_g1.wait_recv()

    copies_bz = []

    def first_half(n):
        copies_by[n].wait_recv()
        for t in range(groups):
            by[t, :, columns(n)] = (
                by[t, :, columns(n)].astype(f32) + b_ref[t, y, :, columns(n)].astype(f32)
            ).astype(low)
        bz[row, :, columns(n)] = by[row, :, columns(n)]
        copies_bz.append(
            to_rows(lambda t: by.at[t, :, columns(n)], lambda t: bz.at[t, :, columns(n)], row)
        )

    def rows_total(n):
        copies_gx[n].wait_recv()
        total = h_ref[lines(n)] + g_ref[block, lines(n)].astype(f32)
        total = total + gc[0, lines(n)].astype(f32) + gx[lines(n)].astype(f32)
        og_ref[block, lines(n)] = total.astype(low)
        piece = og_ref.at[block, lines(n)]
        return [start(piece, piece, chip_peer), start(piece, piece, core_peer)]

    first_half(0)
    wait_all(copies_vz)
    total = vz[0]
    for t in range(1, groups):
        total = total + vz[t]
    vs[1] = total
    copy_vc = start(vs.at[1], vc, core_peer)
    wait_all(copies_sz)
    total = sz[0].astype(f32)
    for t in range(1, groups):
        total = total + sz[t].astype(f32)
    os_ref[mine_q] = total.astype(low)
    piece_s = os_ref.at[mine_q]
    copy_sx, copy_sc = start(piece_s, piece_s, chip_peer), start(piece_s, piece_s, core_peer)
    copies_g0 = rows_total(0)
    copy_vc.wait_recv()
    vs[2] = vs[1] + vc[...]
    copy_vx = start(vs.at[2], vx, chip_peer)
    copy_cx.wait_recv()
    copy_cr = start(oc_ref.at[other_q], oc_ref.at[other_q], core_peer)
    first_half(1)
    copies_g1 = rows_total(1)
    copy_sx.wait_recv()
    copy_sr = start(os_ref.at[other_q], os_ref.at[other_q], core_peer)

    copies_b, relays = [], []
    for n in range(2):
        wait_all(copies_bz[n])
        total = bz[0, :, columns(n)].astype(f32)
        for t in range(1, groups):
            total = total + bz[t, :, columns(n)].astype(f32)
        ob_ref[mine_q, :, columns(n)] = total.astype(low)
        piece = ob_ref.at[mine_q, :, columns(n)]
        copies_b.append([start(piece, piece, chip_peer), start(piece, piece, core_peer)])
        (copies_g0, copies_g1)[n][0].wait_recv()
        piece = og_ref.at[other, lines(n)]
        relays.append(start(piece, piece, core_peer))
    copy_vx.wait_recv()
    ov_ref[...] = vs[2] + vx[...]
    for n in range(2):
        copies_b[n][0].wait_recv()
        piece = ob_ref.at[other_q, :, columns(n)]
        relays.append(start(piece, piece, core_peer))
    wait_all([copy_cc, copy_f0, copy_f1, copy_cr, copy_sc, copy_sr])
    wait_all([copies_g0[1], copies_g1[1], copies_b[0][1], copies_b[1][1]] + relays)
    for copy in sent:
        copy.wait_send()


def finale(c, f, e, s, b, g, h, v):
    groups, _, r, wb = b.shape
    ws = s.shape[2]
    copies = 29 + 4 * (groups - 1)
    vmem = pl.BlockSpec(memory_space=pltpu.VMEM)
    f32 = jnp.float32
    half_rows = pltpu.VMEM(g.shape[1:], low)
    vector = pltpu.VMEM(v.shape, f32)
    return pl.pallas_call(
        finale_kernel,
        out_shape=[jax.ShapeDtypeStruct((4, r, a.shape[-1]), low) for a in (c, f, s, b)]
        + [jax.ShapeDtypeStruct(g.shape, low), jax.ShapeDtypeStruct(v.shape, f32)],
        in_specs=[vmem] * 8,
        out_specs=[vmem] * 6,
        scratch_shapes=[
            pltpu.VMEM((groups, r, wb), low),
            pltpu.VMEM((groups, r, wb), low),
            pltpu.VMEM((groups, r, ws), low),
            pltpu.VMEM((2,) + g.shape[1:], low),
            half_rows,
            half_rows,
            pltpu.VMEM((3,) + v.shape, f32),
            vector,
            vector,
            vector,
            pltpu.VMEM((groups,) + v.shape, f32),
            pltpu.SemaphoreType.DMA((copies,)),
            pltpu.SemaphoreType.DMA((copies,)),
        ],
        compiler_params=pltpu.CompilerParams(
            collective_id=0, has_side_effects=True, vmem_limit_bytes=VMEM_LIMIT
        ),
        cost_estimate=pl.CostEstimate(flops=10**6, bytes_accessed=10**8, transcendentals=0),
        name="finale",
    )(c, f, e, s, b, g, h, v)


def unpack_kernel(c_ref, f_ref, s_ref, b_ref, g_ref, v_ref, qkv_ref, so_ref, cq_ref, ckv_ref, co_ref, fi_ref, fo_ref, gd_ref,
                  pb_ref, ng_ref, ns_ref, fb_ref, *, quarter, piece):
    f32 = jnp.float32

    def spread(source, start, count, size, target):
        for p in range(4):
            for n in range(count):
                target[:, (n * 4 + p) * size : (n * 4 + p + 1) * size] = source[
                    p, :, start + n * size : start + (n + 1) * size
                ].astype(f32)

    spread(b_ref, 0, 3, quarter, qkv_ref)
    spread(c_ref, 0, 1, quarter, co_ref)
    spread(c_ref, quarter, 1, quarter, cq_ref)
    spread(c_ref, 2 * quarter, 2, quarter, ckv_ref)
    spread(s_ref, 0, 1, quarter, so_ref)
    spread(f_ref, 0, quarter * 4 // piece, piece, fi_ref)
    for p in range(4):
        fo_ref[p] = f_ref[p, :, 4 * quarter :].astype(f32)
        gd_ref[p] = g_ref[p].astype(f32)
    at = 0
    for target in (pb_ref, ng_ref, ns_ref, fb_ref):
        target[...] = v_ref[at : at + target.shape[0], :]
        at += target.shape[0]


def unpack(c, f, s, b, g, v, width, hidden, piece):
    r = c.shape[1]
    steps = 4 if r % 64 == 0 else 1
    h, gh = r // steps, g.shape[1] // steps
    f32 = jnp.float32

    def slots(x, n):
        return pl.BlockSpec((4, n, x.shape[2]), lambda i: (0, i, 0))

    wide = [3 * width, width, width, 2 * width, width, hidden]
    counts = [7, 3, 3, hidden // width]
    return pl.pallas_call(
        functools.partial(unpack_kernel, quarter=width // 4, piece=piece),
        out_shape=[jax.ShapeDtypeStruct((r, w), f32) for w in wide]
        + [jax.ShapeDtypeStruct((4, r, width), f32), jax.ShapeDtypeStruct(g.shape, f32)]
        + [jax.ShapeDtypeStruct((n, width), f32) for n in counts],
        grid=(steps,),
        in_specs=[slots(c, h), slots(f, h), slots(s, h), slots(b, h), slots(g, gh), pl.BlockSpec(v.shape, lambda i: (0, 0))],
        out_specs=[pl.BlockSpec((h, w), lambda i: (i, 0)) for w in wide]
        + [pl.BlockSpec((4, h, width), lambda i: (0, i, 0)), slots(g, gh)]
        + [pl.BlockSpec((n, width), lambda i: (0, 0)) for n in counts],
        compiler_params=pltpu.CompilerParams(vmem_limit_bytes=VMEM_LIMIT),
        cost_estimate=pl.CostEstimate(flops=10**6, bytes_accessed=2 * 10**7, transcendentals=0),
        name="unpack",
    )(c, f, s, b, g, v)


def per_device(
    dec_in,
    memory,
    dec_len,
    mem_len,
    grad_out,
    self_qkv,
    self_out,
    cross_q,
    cross_kv,
    cross_out,
    ffn_in,
    ffn_out,
    proj_bias,
    ffn_bias,
    norm_gain,
    norm_shift,
):
    x_full = dec_in[0]
    rows, width = x_full.shape
    hidden = ffn_in.shape[1]
    block = rows // 4
    half, quarter = width // 2, width // 4
    groups = lax.axis_size("dp")
    mem_rows = memory[0]
    mem_block = mem_rows.shape[0]
    me = lax.axis_index("mem")
    chip, core = me // 2, me % 2
    quart = 2 * core + chip

    def block_of(m):
        return jnp.where(m // 2 == 0, 3 * (m % 2), 1 + m % 2)

    def cut(a, start, size, axis=1):
        return lax.dynamic_slice_in_dim(a, start, size, axis)

    def own_rows(a):
        return cut(a, block_of(me) * block, block, 0)

    def by_block(gathered):
        size = gathered.shape[0] // 4
        where = [0, 2, 3, 1]
        pieces = []
        for n in range(4):
            offset = me ^ where[n]
            slot = (offset % 2) * 2 + offset // 2
            pieces.append(cut(gathered, slot * size, size, 0))
        return jnp.concatenate(pieces, axis=0)

    def by_quarter(slots):
        stacked = jnp.stack(slots)
        where = [0, 2, 1, 3]
        out = []
        for n in range(4):
            offset = me ^ where[n]
            out.append(lax.dynamic_index_in_dim(stacked, (offset % 2) * 2 + offset // 2, 0, False))
        return out

    mem_full = gather_rows(mem_rows)

    side = core * half
    q8 = ((product(x_full, cut(self_qkv, side, half)) + cut(proj_bias[0], side, half, 0)) * 0.125).astype(low)
    k8 = product(x_full, cut(self_qkv, width + side, half)).astype(low)
    v8 = (product(x_full, cut(self_qkv, 2 * width + side, half)) + cut(proj_bias[1], side, half, 0)).astype(low)
    info_f = jnp.stack([chip, dec_len[0]]).astype(jnp.int32)
    att8 = self_forward(info_f, q8, k8, v8)

    def heads_to_rows(a8):
        mine = cut(a8, core * block, block, 0)
        other = swap(cut(a8, (1 - core) * block, block, 0), "mem", 1)
        return jnp.where(
            core == 0, jnp.concatenate([mine, other], axis=1), jnp.concatenate([other, mine], axis=1)
        )

    attended = heads_to_rows(att8)
    x_own = own_rows(x_full).astype(jnp.float32)
    first, first_norm, first_inv = normalize(
        x_own + product(attended, self_out) + proj_bias[2], norm_gain[0], norm_shift[0]
    )
    first_low = first.astype(low)
    first_other = swap(first_low, "mem", 1)
    first_chip = jnp.where(
        core == 0,
        jnp.concatenate([first_low, first_other], axis=0),
        jnp.concatenate([first_other, first_low], axis=0),
    )

    cq8 = ((product(first_chip, cut(cross_q, side, half)) + cut(proj_bias[3], side, half, 0)) * 0.125).astype(low)
    kc8 = product(mem_full, cut(cross_kv, side, half)).astype(low)
    vc8 = (product(mem_full, cut(cross_kv, width + side, half)) + cut(proj_bias[4], side, half, 0)).astype(low)
    slot_pos = jnp.stack([(me ^ k) * mem_block for k in ORDER])
    mem_pos = (slot_pos[:, None] + jnp.arange(mem_block, dtype=jnp.int32)[None, :]).reshape(-1)
    mem_bias = jnp.where(mem_pos < mem_len[0], 0.0, neg_fill).astype(jnp.float32)
    crossed = heads_to_rows(cross_forward(cq8, kc8, vc8, mem_bias[None, :]))
    second, second_norm, second_inv = normalize(
        first + product(crossed, cross_out) + proj_bias[5], norm_gain[1], norm_shift[1]
    )
    second_low = second.astype(low)

    act, act_grad = gelu_parts(product(second_low, ffn_in) + ffn_bias)
    act, act_grad = act.astype(low), act_grad.astype(low)
    third, third_norm, third_inv = normalize(
        second + product(act, ffn_out) + proj_bias[6], norm_gain[2], norm_shift[2]
    )
    row_pos = block_of(me) * block + jnp.arange(block, dtype=jnp.int32)
    cot = jnp.where((row_pos < dec_len[0])[:, None], own_rows(grad_out[0]).astype(jnp.float32), 0.0)
    dh3, gain_three, shift_three = norm_back(cot, third_norm, third_inv, norm_gain[2])
    dz = dh3.astype(low)
    du = (product_nt(dz, ffn_out) * act_grad.astype(jnp.float32)).astype(low)
    dh2, gain_two, shift_two = norm_back(
        dh3 + product_nt(du, ffn_in), second_norm, second_inv, norm_gain[1]
    )
    dco = dh2.astype(low)

    crossed_far = swap(crossed, "mem", 2)
    dz, crossed_far = tie(dz, crossed_far)
    second_full = gather_rows(second_low)
    dz_full = gather_rows(dz)
    dco_far = swap(dco, "mem", 2)
    piece = hidden // groups // 4
    if piece % 128 == 0:
        w_in_q = pick_columns(ffn_in, piece, groups, 4, quart)
    else:
        w_in_q = lax.dynamic_index_in_dim(ffn_in.reshape(width, groups, 4, piece), quart, 2, False)
        w_in_q = w_in_q.reshape(width, hidden // 4)
    w_out_q = lax.dynamic_index_in_dim(ffn_out.reshape(groups, 4, piece, width), quart, 1, False)
    w_out_q = w_out_q.reshape(hidden // 4, width)
    b_in_q = lax.dynamic_index_in_dim(ffn_bias.reshape(groups, 4, piece), quart, 1, False).reshape(-1)
    act_q, slope_q = gelu_parts(product(second_full, w_in_q) + b_in_q)
    act_q = act_q.astype(low)
    du_q = (product_nt(dz_full, w_out_q) * slope_q).astype(low)
    du_q, dco_far, third_low = tie(du_q, dco_far, third.astype(low))
    dco_full = join(dco, dco_far)
    third_far = swap(third_low, "mem", 2)
    sum_in = Halving([product_tn(second_full, du_q)], 1)
    sum_out = Halving([product_tn(act_q, dz_full)], min(2, groups // 2))
    send_in, send_out = sum_in.send(), sum_out.send()

    first_full = gather_rows(first_low)
    wide = quart * quarter
    cq4 = ((product(first_full, cut(cross_q, wide, quarter)) + cut(proj_bias[3], wide, quarter, 0)) * 0.125).astype(low)
    dx4 = product_nt(dco_full, cut(cross_out, wide, quarter, 0)).astype(low)
    pair_base = chip * (quarter // 128)
    info_c = jnp.stack([pair_base]).astype(jnp.int32)
    bias_col = jnp.broadcast_to(mem_bias[:, None], (mem_bias.shape[0], 128))
    dx4, send_in, send_out, third_far = tie(dx4, send_in, send_out, third_far)
    got_in, got_out = sum_in.move(send_in), sum_out.move(send_out)
    dq4, dkc4, dvc4 = attention_back(info_c, cq4, kc8, vc8, dx4, bias_col, False)
    dq4, dkc4, dvc4, got_in, got_out = tie(dq4, dkc4, dvc4, got_in, got_out)
    sum_in.add(got_in)
    sum_out.add(got_out)
    dkv4 = jnp.concatenate([dkc4, dvc4], axis=1)

    def over_chips(a):
        b0, b2, b1, b3 = jnp.split(a, 4, axis=0)
        return jnp.concatenate([b2, b3], axis=0), b0, b1

    def to_rows(over, b0, b1):
        size = b0.shape[0]
        mine = jnp.concatenate([b0, over[:size]], axis=0)
        other = swap(jnp.concatenate([b1, over[size:]], axis=0), "mem", 1)
        return by_quarter([mine[:size], mine[size:], other[:size], other[size:]])

    dq_leave, dq_0, dq_1 = over_chips(dq4)
    dq_own = jnp.concatenate(to_rows(swap(dq_leave, "mem", 2), dq_0, dq_1), axis=1)
    send_in, send_out = sum_in.send(), sum_out.send()
    got_in, got_out = sum_in.move(send_in), sum_out.move(send_out)
    crossed_full = join(crossed, crossed_far)
    attended_full = gather_rows(attended)
    sum_q = Halving(
        [product_tn(crossed_full, cut(dco_full, wide, quarter)), product_tn(first_full, dq4)], 1
    )
    sum_kv = Halving([product_tn(mem_full, dkv4)], min(2, groups // 2))
    send_q, send_kv = sum_q.send(), sum_kv.send()
    got_q = sum_q.move(send_q)

    dh1, gain_one, shift_one = norm_back(
        dh2 + product_nt(dq_own, cross_q), first_norm, first_inv, norm_gain[0]
    )
    do = dh1.astype(low)
    sum_in.add(got_in)
    sum_out.add(got_out)
    send_in, send_out = sum_in.send(), sum_out.send()
    do, send_in, send_out, send_kv = tie(do, send_in, send_out, send_kv)
    got_in, got_out = sum_in.move(send_in), sum_out.move(send_out)
    got_kv = sum_kv.move(send_kv)
    dkv_leave, dkv_0, dkv_1 = over_chips(dkv4)
    do_far = swap(do, "mem", 2)
    do_far, got_in, got_out, got_q, dkv_leave = tie(do_far, got_in, got_out, got_q, dkv_leave)
    do_full = join(do, do_far)
    dkv_far = swap(dkv_leave, "mem", 2)
    sum_so = Halving([product_tn(attended_full, cut(do_full, wide, quarter))], 1)

    da4 = product_nt(do_full, cut(self_out, wide, quarter, 0)).astype(low)
    where = [0, 2, 3, 1]
    slots = [((me ^ n) % 2) * 2 + (me ^ n) // 2 for n in where]
    info_s = jnp.stack([pair_base, dec_len[0]] + slots).astype(jnp.int32)
    sum_in.add(got_in)
    sum_out.add(got_out)
    sum_q.add(got_q)
    da4, got_kv = tie(da4, got_kv)
    sum_kv.add(got_kv)
    (g_in,), (g_out,) = sum_in.finish(), sum_out.finish()
    ffn_grad = jnp.concatenate([g_in.astype(low), g_out.astype(low)], axis=1)
    send_q, send_kv, send_so = sum_q.send(), sum_kv.send(), sum_so.send()
    da4, send_q, send_kv, send_so, ffn_grad = tie(da4, send_q, send_kv, send_so, ffn_grad)
    got_q, got_kv, got_so = sum_q.move(send_q), sum_kv.move(send_kv), sum_so.move(send_so)
    ffn_far = swap(ffn_grad, "mem", 2)
    sq4, sk4, sv4 = attention_back(info_s, q8, k8, v8, da4, bias_col[:8], True)
    sq4, sk4, sv4, got_q, got_kv, got_so, ffn_far, dkv_far = tie(
        sq4, sk4, sv4, got_q, got_kv, got_so, ffn_far, dkv_far
    )
    sum_q.add(got_q)
    sum_kv.add(got_kv)
    sum_so.add(got_so)
    sum_q.kept = sum_q.kept + sum_kv.kept
    send_q = sum_q.send()
    sq4, sk4, sv4, send_q = tie(sq4, sk4, sv4, send_q)
    sum_q.add(sum_q.move(send_q))

    per = width // groups
    qkv_grad, partial, own_sums = self_weights(quart, x_full, sq4, sk4, sv4, self_qkv)
    qkv_grad = qkv_grad.reshape(groups // 2, 2, per, 3 * quarter)
    partial = partial.reshape(4, block, width)
    cross_grad = jnp.concatenate([part.astype(low) for part in sum_q.finish()], axis=1)
    (so_grad,) = sum_so.kept
    so_grad = so_grad.astype(low)
    layer_out = by_block(join(third_low, third_far))[None]
    dkv_parts = to_rows(dkv_far, dkv_0, dkv_1)
    dkv_own = jnp.concatenate(
        [a[:, :quarter] for a in dkv_parts] + [a[:, quarter:] for a in dkv_parts], axis=1
    )
    grad_memory = product_nt(dkv_own, cross_kv)[None]

    place = jnp.zeros((2, width), jnp.float32)
    own_sums = own_sums[:2]
    place = lax.dynamic_update_slice(place, own_sums, (0, quart * quarter))
    packed = jnp.concatenate(
        [
            place,
            jnp.stack(
                [
                    column_sum(do),
                    column_sum(dq_own),
                    column_sum(dkv_own[:, width:]),
                    column_sum(dco),
                    column_sum(dz),
                    gain_one,
                    gain_two,
                    gain_three,
                    shift_one,
                    shift_two,
                    shift_three,
                ]
            ),
            column_sum(du).reshape(hidden // width, width),
        ],
        axis=0,
    )
    packed = jnp.pad(packed, ((0, -packed.shape[0] % 8), (0, 0)))
    cross_w, ffn_w, so_w, qkv_w, grad_rows, packed = finale(
        cross_grad, ffn_grad, ffn_far, so_grad, qkv_grad, partial, dh1, packed
    )
    w_qkv, w_so, w_cq, w_ckv, w_co, w_fi, w_fo, grad_dec, p_bias, n_gain, n_shift, f_bias = unpack(
        cross_w, ffn_w, so_w, qkv_w, grad_rows, packed, width, hidden, piece
    )
    return (
        layer_out,
        grad_dec.reshape(1, rows, width),
        grad_memory,
        w_qkv,
        w_so,
        w_cq,
        w_ckv,
        w_co,
        w_fi,
        w_fo.reshape(-1, width),
        p_bias,
        f_bias.reshape(hidden),
        n_gain,
        n_shift,
    )


def solution(mesh):
    in_specs = (
        P("dp", None, None),
        P("dp", "mem", None),
        P("dp"),
        P("dp"),
        P("dp", None, None),
    ) + (P(),) * 11
    out_specs = (
        P("dp", None, None),
        P("dp", None, None),
        P("dp", "mem", None),
    ) + (P("dp", None),) * 7 + (P(),) * 4
    return jax.shard_map(
        per_device, mesh=mesh, in_specs=in_specs, out_specs=out_specs, check_vma=False
    )
```

```python
import functools

import jax
import jax.numpy as jnp
from jax import lax
from jax.experimental import pallas as pl
from jax.experimental.pallas import tpu as pltpu
from jax.sharding import PartitionSpec as P

HEAD_DIM = 64
norm_eps = 1e-05
neg_fill = -1e30
low = jnp.bfloat16
VMEM_LIMIT = 56 * 1024 * 1024


def product(left_rows, right_rows):
    return jnp.dot(left_rows, right_rows, preferred_element_type=jnp.float32)


def product_tn(left_rows, right_rows):
    return lax.dot_general(
        left_rows, right_rows, (((0,), (0,)), ((), ())), preferred_element_type=jnp.float32
    )


def product_nt(left_rows, right_rows):
    return lax.dot_general(
        left_rows, right_rows, (((1,), (1,)), ((), ())), preferred_element_type=jnp.float32
    )


def normalize(hidden, scale_row, shift_row):
    row_mean = jnp.mean(hidden, axis=-1, keepdims=True)
    centered = hidden - row_mean
    variance = jnp.mean(centered * centered, axis=-1, keepdims=True)
    inverse = lax.rsqrt(variance + norm_eps)
    normed = centered * inverse
    return (normed * scale_row + shift_row, normed, inverse)


def norm_back(grad_rows, normed, inverse, scale_row):
    scaled = grad_rows * scale_row
    grad_hidden = inverse * (
        scaled
        - jnp.mean(scaled, axis=-1, keepdims=True)
        - normed * jnp.mean(scaled * normed, axis=-1, keepdims=True)
    )
    return (grad_hidden, jnp.sum(grad_rows * normed, axis=0), jnp.sum(grad_rows, axis=0))


def gelu_parts(values):
    cdf = 0.5 * (1.0 + lax.erf(values * 0.7071067811865476))
    density = jnp.exp(-0.5 * values * values) * 0.3989422804014327
    return values * cdf, cdf + values * density


def column_sum(matrix):
    return jnp.sum(matrix.astype(jnp.float32), axis=0)


def lane_head(rows):
    return lax.broadcasted_iota(jnp.int32, (rows, 128), 1) // HEAD_DIM


def pick_head(pair, h):
    return jnp.where(lane_head(pair.shape[0]) == h, pair, jnp.zeros_like(pair))


def project_kernel(info, x_ref, w_ref, bias_ref, o_ref, *, bias_rows, scales):
    total = product(x_ref[...], w_ref[...])
    for n, (bias_row, scale) in enumerate(zip(bias_rows, scales)):

        @pl.when(pl.program_id(0) == n)
        def _():
            out = total
            if bias_row is not None:
                out = out + bias_ref[bias_row : bias_row + 1, :]
            if scale != 1.0:
                out = out * scale
            o_ref[...] = out.astype(low)


def project(core, x, weight, bias, bias_rows, scales):
    rows, width = x.shape
    half = width // 2
    size = 256
    count = half // size
    parts = len(scales)
    return pl.pallas_call(
        functools.partial(project_kernel, bias_rows=bias_rows, scales=scales),
        out_shape=jax.ShapeDtypeStruct((rows, parts * half), low),
        grid_spec=pltpu.PrefetchScalarGridSpec(
            num_scalar_prefetch=1,
            grid=(parts, count),
            in_specs=[
                pl.BlockSpec((rows, width), lambda p, j, s: (0, 0)),
                pl.BlockSpec((width, size), lambda p, j, s: (0, p * 2 * count + s[0] * count + j)),
                pl.BlockSpec((bias.shape[0], size), lambda p, j, s: (0, s[0] * count + j)),
            ],
            out_specs=pl.BlockSpec((rows, size), lambda p, j, s: (0, p * count + j)),
        ),
        compiler_params=pltpu.CompilerParams(vmem_limit_bytes=VMEM_LIMIT),
        cost_estimate=pl.CostEstimate(
            flops=2 * rows * width * half * parts, bytes_accessed=2 * rows * width * (1 + parts), transcendentals=0
        ),
        name="project",
    )(core.astype(jnp.int32).reshape(1), x, weight, bias)


def self_fwd_kernel(info, q_ref, k_ref, v_ref, o_ref):
    rows = k_ref.shape[0]
    block = rows // 4
    dec_len = info[1]

    def process(qb, slot):
        keys = (qb + 1) * block
        kk, vv = k_ref[:keys, :], v_ref[:keys, :]
        qq = q_ref[qb * block : (qb + 1) * block, :]
        total = None
        for h in range(2):
            s = product_nt(pick_head(qq, h), kk)
            col = lax.broadcasted_iota(jnp.int32, s.shape, 1)
            row = lax.broadcasted_iota(jnp.int32, s.shape, 0) + qb * block
            s = jnp.where((col <= row) & (col < dec_len), s, neg_fill)
            p = jnp.exp(s - jnp.max(s, axis=1, keepdims=True))
            inv = 1.0 / jnp.sum(p, axis=1, keepdims=True)
            part = product(p.astype(low), pick_head(vv, h)) * inv
            total = part if total is None else total + part
        o_ref[slot * block : (slot + 1) * block, :] = total.astype(low)

    @pl.when(info[0] == 0)
    def _():
        process(0, 0)
        process(3, 1)

    @pl.when(info[0] == 1)
    def _():
        process(1, 0)
        process(2, 1)


def self_forward(info, qkv):
    rows, width = qkv.shape[0], qkv.shape[1] // 3
    pairs = width // 128

    def spec(n):
        return pl.BlockSpec((rows, 128), lambda i, s: (0, n * pairs + i))

    return pl.pallas_call(
        self_fwd_kernel,
        out_shape=jax.ShapeDtypeStruct((rows // 2, width), low),
        grid_spec=pltpu.PrefetchScalarGridSpec(
            num_scalar_prefetch=1,
            grid=(pairs,),
            in_specs=[spec(0), spec(1), spec(2)],
            out_specs=pl.BlockSpec((rows // 2, 128), lambda i, s: (0, i)),
        ),
        compiler_params=pltpu.CompilerParams(vmem_limit_bytes=VMEM_LIMIT),
        cost_estimate=pl.CostEstimate(
            flops=6 * rows * rows * width, bytes_accessed=8 * rows * width, transcendentals=rows * rows * 3
        ),
        name="self_forward",
    )(info, qkv, qkv, qkv)


def cross_fwd_kernel(q_ref, k_ref, v_ref, bias_ref, o_ref):
    block = 256
    for r in range(q_ref.shape[0] // block):
        qq = q_ref[r * block : (r + 1) * block, :]
        total = None
        for h in range(2):
            s = product_nt(pick_head(qq, h), k_ref[...]) + bias_ref[...]
            p = jnp.exp(s - jnp.max(s, axis=1, keepdims=True))
            inv = 1.0 / jnp.sum(p, axis=1, keepdims=True)
            part = product(p.astype(low), pick_head(v_ref[...], h)) * inv
            total = part if total is None else total + part
        o_ref[r * block : (r + 1) * block, :] = total.astype(low)


def cross_forward(q, kv, bias_row):
    rows, width = q.shape
    keys = kv.shape[0]
    return pl.pallas_call(
        cross_fwd_kernel,
        out_shape=jax.ShapeDtypeStruct((rows, width), low),
        grid=(width // 128,),
        in_specs=[
            pl.BlockSpec((rows, 128), lambda i: (0, i)),
            pl.BlockSpec((keys, 128), lambda i: (0, i)),
            pl.BlockSpec((keys, 128), lambda i: (0, width // 128 + i)),
            pl.BlockSpec((1, keys), lambda i: (0, 0)),
        ],
        out_specs=pl.BlockSpec((rows, 128), lambda i: (0, i)),
        compiler_params=pltpu.CompilerParams(vmem_limit_bytes=VMEM_LIMIT),
        cost_estimate=pl.CostEstimate(
            flops=16 * rows * keys * width, bytes_accessed=8 * rows * width, transcendentals=rows * keys * 8
        ),
        name="cross_forward",
    )(q, kv, kv, bias_row)


def back_kernel(info, q_ref, k_ref, v_ref, g0_ref, g1_ref, g2_ref, g3_ref, bias_ref, dq_ref, dk_ref, dv_ref, dk_acc, dv_acc, *, causal):
    rows = q_ref.shape[0]
    keys_all = k_ref.shape[0]
    block = rows // 4
    k_t = k_ref[...].T
    dk_acc[...] = jnp.zeros_like(dk_acc)
    dv_acc[...] = jnp.zeros_like(dv_acc)
    for qb in range(4):
        keys = (qb + 1) * block if causal else keys_all
        kk, vv = k_ref[:keys, :], v_ref[:keys, :]
        qq = q_ref[qb * block : (qb + 1) * block, :]
        gg = (g0_ref, g1_ref, g2_ref, g3_ref)[qb][...]
        q_parts = []
        for h in range(2):
            q_h, g_h = pick_head(qq, h), pick_head(gg, h)
            s = product_nt(kk, q_h)
            if causal:
                key = lax.broadcasted_iota(jnp.int32, s.shape, 0)
                row = lax.broadcasted_iota(jnp.int32, s.shape, 1) + qb * block
                s = jnp.where((key <= row) & (key < info[1]), s, neg_fill)
            else:
                s = s + jnp.concatenate([bias_ref[...]] * (block // 128), axis=1)
            p = jnp.exp(s - jnp.max(s, axis=0, keepdims=True))
            p = p * (1.0 / jnp.sum(p, axis=0, keepdims=True))
            dp = product_nt(vv, g_h)
            e = jnp.sum(p * dp, axis=0, keepdims=True)
            ds = (p * (dp - e)).astype(low)
            dv_acc[:keys, :] += product(p.astype(low), g_h)
            dk_acc[:keys, :] += product(ds, q_h)
            q_parts.append(product(k_t[h * HEAD_DIM : (h + 1) * HEAD_DIM, :keys], ds))
        dq_t = jnp.concatenate(q_parts, axis=0) * 0.125
        dq_ref[qb * block : (qb + 1) * block, :] = dq_t.T.astype(low)
    dk_ref[...] = dk_acc[...].astype(low)
    dv_ref[...] = dv_acc[...].astype(low)


def attention_back(info, q, kv, g, bias, causal):
    rows = q.shape[0]
    keys = kv.shape[0]
    own = pl.BlockSpec((rows, 128), lambda i, s: (0, i))
    pairs = g.shape[1] // 64

    def wide(n):
        return pl.BlockSpec((keys, 128), lambda i, s: (0, n * pairs + s[0] + i))

    mine = pl.BlockSpec((keys, 128), lambda i, s: (0, i))

    def g_block(n):
        return pl.BlockSpec((rows // 4, 128), lambda i, s: (s[2 + n] if causal else n, i))

    first = 1 if causal else 0
    q_spec = wide(0) if causal else own
    width = g.shape[1]
    return pl.pallas_call(
        functools.partial(back_kernel, causal=causal),
        out_shape=[
            jax.ShapeDtypeStruct((rows, width), low),
            jax.ShapeDtypeStruct((keys, width), low),
            jax.ShapeDtypeStruct((keys, width), low),
        ],
        grid_spec=pltpu.PrefetchScalarGridSpec(
            num_scalar_prefetch=1,
            grid=(width // 128,),
            in_specs=[q_spec, wide(first), wide(first + 1)] + [g_block(n) for n in range(4)] + [pl.BlockSpec(bias.shape, lambda i, s: (0, 0))],
            out_specs=[own, mine, mine],
            scratch_shapes=[pltpu.VMEM((keys, 128), jnp.float32), pltpu.VMEM((keys, 128), jnp.float32)],
        ),
        compiler_params=pltpu.CompilerParams(vmem_limit_bytes=VMEM_LIMIT),
        cost_estimate=pl.CostEstimate(
            flops=40 * rows * keys * width // (2 if causal else 1),
            bytes_accessed=14 * rows * width,
            transcendentals=rows * keys * 4,
        ),
        name="self_back" if causal else "cross_back",
    )(info, q, kv, kv, g, g, g, g, bias)


def self_weights_kernel(info, x_ref, q_ref, k_ref, v_ref, wq_ref, wk_ref, wv_ref, grad_ref, part_ref, sums_ref):
    block = part_ref.shape[0]
    size = q_ref.shape[1]
    at = pl.ds(pl.multiple_of(pl.program_id(0) * block, block), block)
    total = None
    for n, (d_ref, w_ref) in enumerate(((q_ref, wq_ref), (k_ref, wk_ref), (v_ref, wv_ref))):
        grad_ref[:, n * size : (n + 1) * size] = product_tn(x_ref[...], d_ref[...]).astype(low)
        part = product_nt(d_ref[at, :], w_ref[...])
        total = part if total is None else total + part
    part_ref[...] = total.astype(low)

    @pl.when(pl.program_id(0) == 0)
    def _():
        sums_ref[...] = jnp.zeros_like(sums_ref)
        sums_ref[0:1, :] = jnp.sum(q_ref[...].astype(jnp.float32), axis=0, keepdims=True)
        sums_ref[1:2, :] = jnp.sum(v_ref[...].astype(jnp.float32), axis=0, keepdims=True)


def self_weights(quart, x, dq, dk, dv, weight):
    rows, width = x.shape
    size = dq.shape[1]
    block = 256
    whole = pl.BlockSpec((rows, size), lambda i, s: (0, 0))

    def slab(n):
        return pl.BlockSpec((width, size), lambda i, s: (0, n * (width // size) + s[0]))

    return pl.pallas_call(
        self_weights_kernel,
        out_shape=[
            jax.ShapeDtypeStruct((width, 3 * size), low),
            jax.ShapeDtypeStruct((rows, width), low),
            jax.ShapeDtypeStruct((8, size), jnp.float32),
        ],
        grid_spec=pltpu.PrefetchScalarGridSpec(
            num_scalar_prefetch=1,
            grid=(rows // block,),
            in_specs=[pl.BlockSpec((rows, block), lambda i, s: (0, i)), whole, whole, whole, slab(0), slab(1), slab(2)],
            out_specs=[
                pl.BlockSpec((block, 3 * size), lambda i, s: (i, 0)),
                pl.BlockSpec((block, width), lambda i, s: (i, 0)),
                pl.BlockSpec((8, size), lambda i, s: (0, 0)),
            ],
        ),
        compiler_params=pltpu.CompilerParams(vmem_limit_bytes=VMEM_LIMIT),
        cost_estimate=pl.CostEstimate(
            flops=12 * rows * width * size, bytes_accessed=20 * rows * width, transcendentals=0
        ),
        name="self_weights",
    )(quart.astype(jnp.int32).reshape(1), x, dq, dk, dv, weight, weight, weight)


def pick_kernel(info, in_ref, out_ref):
    out_ref[...] = in_ref[...]


def pick_columns(matrix, size, count, stride, offset):
    rows = matrix.shape[0]
    return pl.pallas_call(
        pick_kernel,
        out_shape=jax.ShapeDtypeStruct((rows, size * count), matrix.dtype),
        grid_spec=pltpu.PrefetchScalarGridSpec(
            num_scalar_prefetch=1,
            grid=(count,),
            in_specs=[pl.BlockSpec((rows, size), lambda n, s: (0, n * stride + s[0]))],
            out_specs=pl.BlockSpec((rows, size), lambda n, s: (0, n)),
        ),
        cost_estimate=pl.CostEstimate(flops=0, bytes_accessed=4 * rows * size * count, transcendentals=0),
        name="pick_columns",
    )(offset.astype(jnp.int32).reshape(1), matrix)


def swap(part, axis, distance):
    count = lax.axis_size(axis)
    return lax.ppermute(part, axis, [(i, i ^ distance) for i in range(count)])


ORDER = (0, 2, 1, 3)


def gather_rows(part):
    pair = jnp.concatenate([part, swap(part, "mem", 2)], axis=0)
    return jnp.concatenate([pair, swap(pair, "mem", 1)], axis=0)


def bits_of(count, first):
    every = [1 << i for i in range(count.bit_length() - 1)]
    return [first] + [d for d in every if d != first]


def join(part, far):
    pair = jnp.concatenate([part, far], axis=0)
    return jnp.concatenate([pair, swap(pair, "mem", 1)], axis=0)


class Halving:
    def __init__(self, parts, first):
        count = lax.axis_size("dp")
        self.dims = [count]
        self.kept = [a.reshape(count, a.shape[0] // count, a.shape[1]) for a in parts]
        self.left = bits_of(count, first)
        self.done_bits = []
        self.count = count

    def send(self):
        me = lax.axis_index("dp")
        distance = self.left[0]
        below = sum(1 for d in self.left if d < distance)
        low_size = 1 << below
        bit = (me // distance) % 2
        self.mine, theirs = [], []
        for a in self.kept:
            n, r, w = a.shape
            split = a.reshape(n // (2 * low_size), 2, low_size, r, w)
            self.mine.append(lax.dynamic_index_in_dim(split, bit, 1, False).reshape(n // 2, r, w))
            theirs.append(lax.dynamic_index_in_dim(split, 1 - bit, 1, False).reshape(n // 2, r, w))
        return jnp.concatenate([t.astype(low) for t in theirs], axis=2)

    def move(self, sent):
        return swap(sent, "dp", self.left.pop(0))

    def add(self, got):
        start, self.kept = 0, []
        for a in self.mine:
            self.kept.append(a + got[:, :, start : start + a.shape[2]].astype(jnp.float32))
            start += a.shape[2]

    def step(self):
        self.add(self.move(self.send()))

    def finish(self):
        while self.left:
            self.step()
        return [a[0] for a in self.kept]


def tie(*values):
    return lax.optimization_barrier(values)


def finale_kernel(c_ref, f_ref, e_ref, s_ref, b_ref, g_ref, h_ref, v_ref,
                  oc_ref, of_ref, os_ref, ob_ref, og_ref, ov_ref,
                  by, bz, sz, gc, gs, gx, vs, vc, vx, vy, vz, send, recv):
    dp, mem = lax.axis_index("dp"), lax.axis_index("mem")
    y, row = dp % 2, dp // 2
    groups = b_ref.shape[0]
    f32 = jnp.float32
    wide = b_ref.shape[3] // 2
    tall = h_ref.shape[0] // 2

    def quarter_of(m):
        return 2 * (m % 2) + m // 2

    def block_of(m):
        return (m // 2) + (m % 2) * (3 - 2 * (m // 2))

    barrier = pltpu.get_barrier_semaphore()
    core_peer, chip_peer, y_peer = {"mem": mem ^ 1}, {"mem": mem ^ 2}, {"dp": dp ^ 1}
    row_peers = [{"dp": (row ^ j) * 2 + y} for j in range(1, groups)]
    peers = [core_peer, chip_peer, y_peer] + row_peers
    for peer in peers:
        pl.semaphore_signal(barrier, inc=1, device_id=peer, device_id_type=pl.DeviceIdType.MESH)
    pl.semaphore_wait(barrier, len(peers))

    sent = []

    def start(src, dst, peer):
        n = len(sent)
        copy = pltpu.make_async_remote_copy(
            src_ref=src, dst_ref=dst, send_sem=send.at[n], recv_sem=recv.at[n],
            device_id=peer, device_id_type=pl.DeviceIdType.MESH,
        )
        copy.start()
        sent.append(copy)
        return copy

    def to_rows(source, target, own):
        return [start(source(row ^ j), target(own), row_peers[j - 1]) for j in range(1, groups)]

    def wait_all(copies):
        for copy in copies:
            copy.wait_recv()

    def columns(n):
        return pl.ds(n * wide, wide)

    def lines(n):
        return pl.ds(n * tall, tall)

    mine_q, other_q = quarter_of(mem), quarter_of(mem ^ 2)
    block, other = block_of(mem), block_of(mem ^ 2)

    copy_vy = start(v_ref, vy, y_peer)
    copies_by = [start(b_ref.at[:, 1 - y, :, columns(n)], by.at[:, :, columns(n)], y_peer) for n in range(2)]
    copy_g3 = start(g_ref.at[block_of(mem ^ 3)], gc.at[1], core_peer)
    copy_cx = start(c_ref, oc_ref.at[mine_q], chip_peer)
    copies_sz = to_rows(lambda t: s_ref.at[t], lambda t: sz.at[t], row)
    copy_g1 = start(g_ref.at[block_of(mem ^ 1)], gc.at[0], core_peer)
    copy_cc = start(c_ref, oc_ref.at[mine_q], core_peer)
    copy_f0 = start(f_ref, of_ref.at[mine_q], core_peer)
    copy_f1 = start(e_ref, of_ref.at[other_q], core_peer)
    sz[row] = s_ref[row]

    copy_g3.wait_recv()
    copies_gx = []
    for n in range(2):
        gs[lines(n)] = (g_ref[other, lines(n)].astype(f32) + gc[1, lines(n)].astype(f32)).astype(low)
        copies_gx.append(start(gs.at[lines(n)], gx.at[lines(n)], chip_peer))
    copy_vy.wait_recv()
    vs[0] = v_ref[...] + vy[...]
    vz[row] = vs[0]
    copies_vz = to_rows(lambda t: vs.at[0], lambda t: vz.at[t], row)
    oc_ref[mine_q] = c_ref[...]
    of_ref[mine_q] = f_ref[...]
    of_ref[other_q] = e_ref[...]
    copy_g1.wait_recv()

    copies_bz = []

    def first_half(n):
        copies_by[n].wait_recv()
        for t in range(groups):
            by[t, :, columns(n)] = (
                by[t, :, columns(n)].astype(f32) + b_ref[t, y, :, columns(n)].astype(f32)
            ).astype(low)
        bz[row, :, columns(n)] = by[row, :, columns(n)]
        copies_bz.append(
            to_rows(lambda t: by.at[t, :, columns(n)], lambda t: bz.at[t, :, columns(n)], row)
        )

    def rows_total(n):
        copies_gx[n].wait_recv()
        total = h_ref[lines(n)] + g_ref[block, lines(n)].astype(f32)
        total = total + gc[0, lines(n)].astype(f32) + gx[lines(n)].astype(f32)
        og_ref[block, lines(n)] = total.astype(low)
        piece = og_ref.at[block, lines(n)]
        return [start(piece, piece, chip_peer), start(piece, piece, core_peer)]

    first_half(0)
    wait_all(copies_vz)
    total = vz[0]
    for t in range(1, groups):
        total = total + vz[t]
    vs[1] = total
    copy_vc = start(vs.at[1], vc, core_peer)
    wait_all(copies_sz)
    total = sz[0].astype(f32)
    for t in range(1, groups):
        total = total + sz[t].astype(f32)
    os_ref[mine_q] = total.astype(low)
    piece_s = os_ref.at[mine_q]
    copy_sx, copy_sc = start(piece_s, piece_s, chip_peer), start(piece_s, piece_s, core_peer)
    copies_g0 = rows_total(0)
    copy_vc.wait_recv()
    vs[2] = vs[1] + vc[...]
    copy_vx = start(vs.at[2], vx, chip_peer)
    copy_cx.wait_recv()
    copy_cr = start(oc_ref.at[other_q], oc_ref.at[other_q], core_peer)
    first_half(1)
    copies_g1 = rows_total(1)
    copy_sx.wait_recv()
    copy_sr = start(os_ref.at[other_q], os_ref.at[other_q], core_peer)

    copies_b, relays = [], []
    for n in range(2):
        wait_all(copies_bz[n])
        total = bz[0, :, columns(n)].astype(f32)
        for t in range(1, groups):
            total = total + bz[t, :, columns(n)].astype(f32)
        ob_ref[mine_q, :, columns(n)] = total.astype(low)
        piece = ob_ref.at[mine_q, :, columns(n)]
        copies_b.append([start(piece, piece, chip_peer), start(piece, piece, core_peer)])
        (copies_g0, copies_g1)[n][0].wait_recv()
        piece = og_ref.at[other, lines(n)]
        relays.append(start(piece, piece, core_peer))
    copy_vx.wait_recv()
    ov_ref[...] = vs[2] + vx[...]
    for n in range(2):
        copies_b[n][0].wait_recv()
        piece = ob_ref.at[other_q, :, columns(n)]
        relays.append(start(piece, piece, core_peer))
    wait_all([copy_cc, copy_f0, copy_f1, copy_cr, copy_sc, copy_sr])
    wait_all([copies_g0[1], copies_g1[1], copies_b[0][1], copies_b[1][1]] + relays)
    for copy in sent:
        copy.wait_send()


def finale(c, f, e, s, b, g, h, v):
    groups, _, r, wb = b.shape
    ws = s.shape[2]
    copies = 29 + 4 * (groups - 1)
    vmem = pl.BlockSpec(memory_space=pltpu.VMEM)
    f32 = jnp.float32
    half_rows = pltpu.VMEM(g.shape[1:], low)
    vector = pltpu.VMEM(v.shape, f32)
    return pl.pallas_call(
        finale_kernel,
        out_shape=[jax.ShapeDtypeStruct((4, r, a.shape[-1]), low) for a in (c, f, s, b)]
        + [jax.ShapeDtypeStruct(g.shape, low), jax.ShapeDtypeStruct(v.shape, f32)],
        in_specs=[vmem] * 8,
        out_specs=[vmem] * 6,
        scratch_shapes=[
            pltpu.VMEM((groups, r, wb), low),
            pltpu.VMEM((groups, r, wb), low),
            pltpu.VMEM((groups, r, ws), low),
            pltpu.VMEM((2,) + g.shape[1:], low),
            half_rows,
            half_rows,
            pltpu.VMEM((3,) + v.shape, f32),
            vector,
            vector,
            vector,
            pltpu.VMEM((groups,) + v.shape, f32),
            pltpu.SemaphoreType.DMA((copies,)),
            pltpu.SemaphoreType.DMA((copies,)),
        ],
        compiler_params=pltpu.CompilerParams(
            collective_id=0, has_side_effects=True, vmem_limit_bytes=VMEM_LIMIT
        ),
        cost_estimate=pl.CostEstimate(flops=10**6, bytes_accessed=10**8, transcendentals=0),
        name="finale",
    )(c, f, e, s, b, g, h, v)


def unpack_kernel(c_ref, f_ref, s_ref, b_ref, g_ref, v_ref, qkv_ref, so_ref, cq_ref, ckv_ref, co_ref, fi_ref, fo_ref, gd_ref,
                  pb_ref, ng_ref, ns_ref, fb_ref, *, quarter, piece):
    f32 = jnp.float32

    def spread(source, start, count, size, target):
        for p in range(4):
            for n in range(count):
                target[:, (n * 4 + p) * size : (n * 4 + p + 1) * size] = source[
                    p, :, start + n * size : start + (n + 1) * size
                ].astype(f32)

    spread(b_ref, 0, 3, quarter, qkv_ref)
    spread(c_ref, 0, 1, quarter, co_ref)
    spread(c_ref, quarter, 1, quarter, cq_ref)
    spread(c_ref, 2 * quarter, 2, quarter, ckv_ref)
    spread(s_ref, 0, 1, quarter, so_ref)
    spread(f_ref, 0, quarter * 4 // piece, piece, fi_ref)
    for p in range(4):
        fo_ref[p] = f_ref[p, :, 4 * quarter :].astype(f32)
        gd_ref[p] = g_ref[p].astype(f32)
    at = 0
    for target in (pb_ref, ng_ref, ns_ref, fb_ref):
        target[...] = v_ref[at : at + target.shape[0], :]
        at += target.shape[0]


def unpack(c, f, s, b, g, v, width, hidden, piece):
    r = c.shape[1]
    steps = 4 if r % 64 == 0 else 1
    h, gh = r // steps, g.shape[1] // steps
    f32 = jnp.float32

    def slots(x, n):
        return pl.BlockSpec((4, n, x.shape[2]), lambda i: (0, i, 0))

    wide = [3 * width, width, width, 2 * width, width, hidden]
    counts = [7, 3, 3, hidden // width]
    return pl.pallas_call(
        functools.partial(unpack_kernel, quarter=width // 4, piece=piece),
        out_shape=[jax.ShapeDtypeStruct((r, w), f32) for w in wide]
        + [jax.ShapeDtypeStruct((4, r, width), f32), jax.ShapeDtypeStruct(g.shape, f32)]
        + [jax.ShapeDtypeStruct((n, width), f32) for n in counts],
        grid=(steps,),
        in_specs=[slots(c, h), slots(f, h), slots(s, h), slots(b, h), slots(g, gh), pl.BlockSpec(v.shape, lambda i: (0, 0))],
        out_specs=[pl.BlockSpec((h, w), lambda i: (i, 0)) for w in wide]
        + [pl.BlockSpec((4, h, width), lambda i: (0, i, 0)), slots(g, gh)]
        + [pl.BlockSpec((n, width), lambda i: (0, 0)) for n in counts],
        compiler_params=pltpu.CompilerParams(vmem_limit_bytes=VMEM_LIMIT),
        cost_estimate=pl.CostEstimate(flops=10**6, bytes_accessed=2 * 10**7, transcendentals=0),
        name="unpack",
    )(c, f, s, b, g, v)


def per_device(
    dec_in,
    memory,
    dec_len,
    mem_len,
    grad_out,
    self_qkv,
    self_out,
    cross_q,
    cross_kv,
    cross_out,
    ffn_in,
    ffn_out,
    proj_bias,
    ffn_bias,
    norm_gain,
    norm_shift,
):
    x_full = dec_in[0]
    rows, width = x_full.shape
    hidden = ffn_in.shape[1]
    block = rows // 4
    half, quarter = width // 2, width // 4
    groups = lax.axis_size("dp")
    mem_rows = memory[0]
    mem_block = mem_rows.shape[0]
    me = lax.axis_index("mem")
    chip, core = me // 2, me % 2
    quart = 2 * core + chip

    def block_of(m):
        return jnp.where(m // 2 == 0, 3 * (m % 2), 1 + m % 2)

    def cut(a, start, size, axis=1):
        return lax.dynamic_slice_in_dim(a, start, size, axis)

    def own_rows(a):
        return cut(a, block_of(me) * block, block, 0)

    def by_block(gathered):
        size = gathered.shape[0] // 4
        where = [0, 2, 3, 1]
        pieces = []
        for n in range(4):
            offset = me ^ where[n]
            slot = (offset % 2) * 2 + offset // 2
            pieces.append(cut(gathered, slot * size, size, 0))
        return jnp.concatenate(pieces, axis=0)

    def by_quarter(slots):
        stacked = jnp.stack(slots)
        where = [0, 2, 1, 3]
        out = []
        for n in range(4):
            offset = me ^ where[n]
            out.append(lax.dynamic_index_in_dim(stacked, (offset % 2) * 2 + offset // 2, 0, False))
        return out

    mem_far = swap(mem_rows, "mem", 2)

    side = core * half
    qkv8 = project(core, x_full, self_qkv, proj_bias, (0, None, 1), (0.125, 1.0, 1.0))
    info_f = jnp.stack([chip, dec_len[0]]).astype(jnp.int32)
    att8 = self_forward(info_f, qkv8)
    att8, mem_far = tie(att8, mem_far)
    mem_full = join(mem_rows, mem_far)

    def heads_to_rows(a8):
        mine = cut(a8, core * block, block, 0)
        other = swap(cut(a8, (1 - core) * block, block, 0), "mem", 1)
        return jnp.where(
            core == 0, jnp.concatenate([mine, other], axis=1), jnp.concatenate([other, mine], axis=1)
        )

    attended = heads_to_rows(att8)
    x_own = own_rows(x_full).astype(jnp.float32)
    first, first_norm, first_inv = normalize(
        x_own + product(attended, self_out) + proj_bias[2], norm_gain[0], norm_shift[0]
    )
    first_low = first.astype(low)
    first_other = swap(first_low, "mem", 1)
    first_chip = jnp.where(
        core == 0,
        jnp.concatenate([first_low, first_other], axis=0),
        jnp.concatenate([first_other, first_low], axis=0),
    )

    cq8 = ((product(first_chip, cut(cross_q, side, half)) + cut(proj_bias[3], side, half, 0)) * 0.125).astype(low)
    kvc8 = project(core, mem_full, cross_kv, proj_bias, (None, 4), (1.0, 1.0))
    slot_pos = jnp.stack([(me ^ k) * mem_block for k in ORDER])
    mem_pos = (slot_pos[:, None] + jnp.arange(mem_block, dtype=jnp.int32)[None, :]).reshape(-1)
    mem_bias = jnp.where(mem_pos < mem_len[0], 0.0, neg_fill).astype(jnp.float32)
    crossed = heads_to_rows(cross_forward(cq8, kvc8, mem_bias[None, :]))
    second, second_norm, second_inv = normalize(
        first + product(crossed, cross_out) + proj_bias[5], norm_gain[1], norm_shift[1]
    )
    second_low = second.astype(low)

    second_low, late = tie(second_low, quart)
    second_far = swap(second_low, "mem", 2)
    piece = hidden // groups // 4
    if piece % 128 == 0:
        w_in_q = pick_columns(ffn_in, piece, groups, 4, late)
    else:
        w_in_q = lax.dynamic_index_in_dim(ffn_in.reshape(width, groups, 4, piece), late, 2, False)
        w_in_q = w_in_q.reshape(width, hidden // 4)
    w_out_q = lax.dynamic_index_in_dim(ffn_out.reshape(groups, 4, piece, width), late, 1, False)
    w_out_q = w_out_q.reshape(hidden // 4, width)
    inner = product(second_low, ffn_in) + ffn_bias
    inner, second_far, w_in_q, w_out_q = tie(inner, second_far, w_in_q, w_out_q)
    second_full = join(second_low, second_far)
    act, act_grad = gelu_parts(inner)
    act, act_grad = act.astype(low), act_grad.astype(low)
    third, third_norm, third_inv = normalize(
        second + product(act, ffn_out) + proj_bias[6], norm_gain[2], norm_shift[2]
    )
    row_pos = block_of(me) * block + jnp.arange(block, dtype=jnp.int32)
    cot = jnp.where((row_pos < dec_len[0])[:, None], own_rows(grad_out[0]).astype(jnp.float32), 0.0)
    dh3, gain_three, shift_three = norm_back(cot, third_norm, third_inv, norm_gain[2])
    dz = dh3.astype(low)
    first_full = gather_rows(first_low)
    dz_far = swap(dz, "mem", 2)
    wide = quart * quarter
    cq4 = ((product(first_full, cut(cross_q, wide, quarter)) + cut(proj_bias[3], wide, quarter, 0)) * 0.125).astype(low)
    du = (product_nt(dz, ffn_out) * act_grad.astype(jnp.float32)).astype(low)
    du, dz_far = tie(du, dz_far)
    dh2, gain_two, shift_two = norm_back(
        dh3 + product_nt(du, ffn_in), second_norm, second_inv, norm_gain[1]
    )
    dco = dh2.astype(low)

    dz_full = join(dz, dz_far)
    dco_far = swap(dco, "mem", 2)
    b_in_q = lax.dynamic_index_in_dim(ffn_bias.reshape(groups, 4, piece), quart, 1, False).reshape(-1)
    act_q, slope_q = gelu_parts(product(second_full, w_in_q) + b_in_q)
    act_q = act_q.astype(low)
    du_q = (product_nt(dz_full, w_out_q) * slope_q).astype(low)
    du_q, dco_far, third_low = tie(du_q, dco_far, third.astype(low))
    dco_full = join(dco, dco_far)
    third_far = swap(third_low, "mem", 2)
    sum_in = Halving([product_tn(second_full, du_q)], 1)
    sum_out = Halving([product_tn(act_q, dz_full)], min(2, groups // 2))
    send_in, send_out = sum_in.send(), sum_out.send()

    dx4 = product_nt(dco_full, cut(cross_out, wide, quarter, 0)).astype(low)
    pair_base = chip * (quarter // 128)
    info_c = jnp.stack([pair_base]).astype(jnp.int32)
    bias_col = jnp.broadcast_to(mem_bias[:, None], (mem_bias.shape[0], 128))
    dx4, send_in, send_out, third_far, crossed_late = tie(dx4, send_in, send_out, third_far, crossed)
    crossed_far = swap(crossed_late, "mem", 2)
    got_in, got_out = sum_in.move(send_in), sum_out.move(send_out)
    dq4, dkc4, dvc4 = attention_back(info_c, cq4, kvc8, dx4, bias_col, False)
    dq4, dkc4, dvc4, got_in, got_out, crossed_far = tie(dq4, dkc4, dvc4, got_in, got_out, crossed_far)
    sum_in.add(got_in)
    sum_out.add(got_out)
    dkv4 = jnp.concatenate([dkc4, dvc4], axis=1)

    def over_chips(a):
        b0, b2, b1, b3 = jnp.split(a, 4, axis=0)
        return jnp.concatenate([b2, b3], axis=0), b0, b1

    def to_rows(over, b0, b1):
        size = b0.shape[0]
        mine = jnp.concatenate([b0, over[:size]], axis=0)
        other = swap(jnp.concatenate([b1, over[size:]], axis=0), "mem", 1)
        return by_quarter([mine[:size], mine[size:], other[:size], other[size:]])

    dq_leave, dq_0, dq_1 = over_chips(dq4)
    dkv_leave, dkv_0, dkv_1 = over_chips(dkv4)
    dq_far = swap(dq_leave, "mem", 2)
    send_in, send_out = sum_in.send(), sum_out.send()
    dq_far, send_in, send_out = tie(dq_far, send_in, send_out)
    dq_own = jnp.concatenate(to_rows(dq_far, dq_0, dq_1), axis=1)
    got_in, got_out = sum_in.move(send_in), sum_out.move(send_out)
    crossed_full = join(crossed, crossed_far)
    attended_full = gather_rows(attended)
    dh1, gain_one, shift_one = norm_back(
        dh2 + product_nt(dq_own, cross_q), first_norm, first_inv, norm_gain[0]
    )
    do = dh1.astype(low)
    sum_w = Halving(
        [product_tn(crossed_full, cut(dco_full, wide, quarter)), product_tn(first_full, dq4)], 1
    )
    sum_kv = Halving([product_tn(mem_full, dkv4)], min(2, groups // 2))
    got_w, got_kv = sum_w.move(sum_w.send()), sum_kv.move(sum_kv.send())
    do_far = swap(do, "mem", 2)
    do_far, got_in, got_out, got_w, got_kv = tie(do_far, got_in, got_out, got_w, got_kv)
    do_full = join(do, do_far)
    sum_in.add(got_in)
    sum_out.add(got_out)
    sum_in.kept = sum_in.kept + sum_out.kept
    sum_w.add(got_w)
    sum_kv.add(got_kv)
    sum_so = Halving([product_tn(attended_full, cut(do_full, wide, quarter))], 1)

    da4 = product_nt(do_full, cut(self_out, wide, quarter, 0)).astype(low)
    where = [0, 2, 3, 1]
    slots = [((me ^ n) % 2) * 2 + (me ^ n) // 2 for n in where]
    info_s = jnp.stack([pair_base, dec_len[0]] + slots).astype(jnp.int32)
    send_in, send_w, send_kv, send_so = sum_in.send(), sum_w.send(), sum_kv.send(), sum_so.send()
    da4, send_in, send_w, send_kv, send_so, dkv_leave = tie(da4, send_in, send_w, send_kv, send_so, dkv_leave)
    got_in, got_w, got_kv = sum_in.move(send_in), sum_w.move(send_w), sum_kv.move(send_kv)
    got_so = sum_so.move(send_so)
    dkv_far = swap(dkv_leave, "mem", 2)
    sq4, sk4, sv4 = attention_back(info_s, qkv8, qkv8, da4, bias_col[:8], True)
    sq4, sk4, sv4, got_in, got_w, got_kv, got_so, dkv_far = tie(
        sq4, sk4, sv4, got_in, got_w, got_kv, got_so, dkv_far
    )
    sum_in.add(got_in)
    ffn_grad = jnp.concatenate([part.astype(low) for part in sum_in.finish()], axis=1)
    sum_w.add(got_w)
    sum_kv.add(got_kv)
    sum_so.add(got_so)
    sum_w.kept = sum_w.kept + sum_kv.kept
    send_w = sum_w.send()
    sq4, sk4, sv4, send_w, ffn_grad = tie(sq4, sk4, sv4, send_w, ffn_grad)
    ffn_far = swap(ffn_grad, "mem", 2)
    got_w = sum_w.move(send_w)
    dkv_parts = to_rows(dkv_far, dkv_0, dkv_1)
    dkv_own = jnp.concatenate(
        [a[:, :quarter] for a in dkv_parts] + [a[:, quarter:] for a in dkv_parts], axis=1
    )
    grad_memory = product_nt(dkv_own, cross_kv)[None]

    per = width // groups
    qkv_grad, partial, own_sums = self_weights(quart, x_full, sq4, sk4, sv4, self_qkv)
    qkv_grad = qkv_grad.reshape(groups // 2, 2, per, 3 * quarter)
    partial = partial.reshape(4, block, width)
    qkv_grad, got_w, ffn_far, grad_memory = tie(qkv_grad, got_w, ffn_far, grad_memory)
    sum_w.add(got_w)
    cross_grad = jnp.concatenate([part.astype(low) for part in sum_w.finish()], axis=1)
    so_grad = sum_so.kept[0].astype(low)
    layer_out = by_block(join(third_low, third_far))[None]

    place = jnp.zeros((2, width), jnp.float32)
    own_sums = own_sums[:2]
    place = lax.dynamic_update_slice(place, own_sums, (0, quart * quarter))
    packed = jnp.concatenate(
        [
            place,
            jnp.stack(
                [
                    column_sum(do),
                    column_sum(dq_own),
                    column_sum(dkv_own[:, width:]),
                    column_sum(dco),
                    column_sum(dz),
                    gain_one,
                    gain_two,
                    gain_three,
                    shift_one,
                    shift_two,
                    shift_three,
                ]
            ),
            column_sum(du).reshape(hidden // width, width),
        ],
        axis=0,
    )
    packed = jnp.pad(packed, ((0, -packed.shape[0] % 8), (0, 0)))
    cross_w, ffn_w, so_w, qkv_w, grad_rows, packed = finale(
        cross_grad, ffn_grad, ffn_far, so_grad, qkv_grad, partial, dh1, packed
    )
    w_qkv, w_so, w_cq, w_ckv, w_co, w_fi, w_fo, grad_dec, p_bias, n_gain, n_shift, f_bias = unpack(
        cross_w, ffn_w, so_w, qkv_w, grad_rows, packed, width, hidden, piece
    )
    return (
        layer_out,
        grad_dec.reshape(1, rows, width),
        grad_memory,
        w_qkv,
        w_so,
        w_cq,
        w_ckv,
        w_co,
        w_fi,
        w_fo.reshape(-1, width),
        p_bias,
        f_bias.reshape(hidden),
        n_gain,
        n_shift,
    )


def solution(mesh):
    in_specs = (
        P("dp", None, None),
        P("dp", "mem", None),
        P("dp"),
        P("dp"),
        P("dp", None, None),
    ) + (P(),) * 11
    out_specs = (
        P("dp", None, None),
        P("dp", None, None),
        P("dp", "mem", None),
    ) + (P("dp", None),) * 7 + (P(),) * 4
    return jax.shard_map(
        per_device, mesh=mesh, in_specs=in_specs, out_specs=out_specs, check_vma=False
    )
```

```python
import functools

import jax
import jax.numpy as jnp
from jax import lax
from jax.experimental import pallas as pl
from jax.experimental.pallas import tpu as pltpu
from jax.sharding import PartitionSpec as P

HEAD_DIM = 64
norm_eps = 1e-05
neg_fill = -1e30
low = jnp.bfloat16
VMEM_LIMIT = 56 * 1024 * 1024


def product(left_rows, right_rows):
    return jnp.dot(left_rows, right_rows, preferred_element_type=jnp.float32)


def product_tn(left_rows, right_rows):
    return lax.dot_general(
        left_rows, right_rows, (((0,), (0,)), ((), ())), preferred_element_type=jnp.float32
    )


def product_nt(left_rows, right_rows):
    return lax.dot_general(
        left_rows, right_rows, (((1,), (1,)), ((), ())), preferred_element_type=jnp.float32
    )


def normalize(hidden, scale_row, shift_row):
    row_mean = jnp.mean(hidden, axis=-1, keepdims=True)
    centered = hidden - row_mean
    variance = jnp.mean(centered * centered, axis=-1, keepdims=True)
    inverse = lax.rsqrt(variance + norm_eps)
    normed = centered * inverse
    return (normed * scale_row + shift_row, normed, inverse)


def norm_back(grad_rows, normed, inverse, scale_row):
    scaled = grad_rows * scale_row
    grad_hidden = inverse * (
        scaled
        - jnp.mean(scaled, axis=-1, keepdims=True)
        - normed * jnp.mean(scaled * normed, axis=-1, keepdims=True)
    )
    return (grad_hidden, jnp.sum(grad_rows * normed, axis=0), jnp.sum(grad_rows, axis=0))


def gelu_parts(values):
    cdf = 0.5 * (1.0 + lax.erf(values * 0.7071067811865476))
    density = jnp.exp(-0.5 * values * values) * 0.3989422804014327
    return values * cdf, cdf + values * density


def column_sum(matrix):
    return jnp.sum(matrix.astype(jnp.float32), axis=0)


def lane_head(rows):
    return lax.broadcasted_iota(jnp.int32, (rows, 128), 1) // HEAD_DIM


def pick_head(pair, h):
    return jnp.where(lane_head(pair.shape[0]) == h, pair, jnp.zeros_like(pair))


def project_kernel(info, x_ref, w_ref, bias_ref, o_ref, *, bias_rows, scales):
    total = product(x_ref[...], w_ref[...])
    for n, (bias_row, scale) in enumerate(zip(bias_rows, scales)):

        @pl.when(pl.program_id(0) == n)
        def _():
            out = total
            if bias_row is not None:
                out = out + bias_ref[bias_row : bias_row + 1, :]
            if scale != 1.0:
                out = out * scale
            o_ref[...] = out.astype(low)


def project(core, x, weight, bias, bias_rows, scales):
    rows, width = x.shape
    half = width // 2
    size = 256
    count = half // size
    parts = len(scales)
    return pl.pallas_call(
        functools.partial(project_kernel, bias_rows=bias_rows, scales=scales),
        out_shape=jax.ShapeDtypeStruct((rows, parts * half), low),
        grid_spec=pltpu.PrefetchScalarGridSpec(
            num_scalar_prefetch=1,
            grid=(parts, count),
            in_specs=[
                pl.BlockSpec((rows, width), lambda p, j, s: (0, 0)),
                pl.BlockSpec((width, size), lambda p, j, s: (0, p * 2 * count + s[0] * count + j)),
                pl.BlockSpec((bias.shape[0], size), lambda p, j, s: (0, s[0] * count + j)),
            ],
            out_specs=pl.BlockSpec((rows, size), lambda p, j, s: (0, p * count + j)),
        ),
        compiler_params=pltpu.CompilerParams(vmem_limit_bytes=VMEM_LIMIT),
        cost_estimate=pl.CostEstimate(
            flops=2 * rows * width * half * parts, bytes_accessed=2 * rows * width * (1 + parts), transcendentals=0
        ),
        name="project",
    )(core.astype(jnp.int32).reshape(1), x, weight, bias)


def self_fwd_kernel(info, q_ref, k_ref, v_ref, o_ref):
    rows = k_ref.shape[0]
    block = rows // 4
    dec_len = info[1]

    def process(qb, slot):
        keys = (qb + 1) * block
        kk, vv = k_ref[:keys, :], v_ref[:keys, :]
        qq = q_ref[qb * block : (qb + 1) * block, :]
        total = None
        for h in range(2):
            s = product_nt(pick_head(qq, h), kk)
            col = lax.broadcasted_iota(jnp.int32, s.shape, 1)
            row = lax.broadcasted_iota(jnp.int32, s.shape, 0) + qb * block
            s = jnp.where((col <= row) & (col < dec_len), s, neg_fill)
            p = jnp.exp(s - jnp.max(s, axis=1, keepdims=True))
            inv = 1.0 / jnp.sum(p, axis=1, keepdims=True)
            part = product(p.astype(low), pick_head(vv, h)) * inv
            total = part if total is None else total + part
        o_ref[slot * block : (slot + 1) * block, :] = total.astype(low)

    @pl.when(info[0] == 0)
    def _():
        process(0, 0)
        process(3, 1)

    @pl.when(info[0] == 1)
    def _():
        process(1, 0)
        process(2, 1)


def self_forward(info, qkv):
    rows, width = qkv.shape[0], qkv.shape[1] // 3
    pairs = width // 128

    def spec(n):
        return pl.BlockSpec((rows, 128), lambda i, s: (0, n * pairs + i))

    return pl.pallas_call(
        self_fwd_kernel,
        out_shape=jax.ShapeDtypeStruct((rows // 2, width), low),
        grid_spec=pltpu.PrefetchScalarGridSpec(
            num_scalar_prefetch=1,
            grid=(pairs,),
            in_specs=[spec(0), spec(1), spec(2)],
            out_specs=pl.BlockSpec((rows // 2, 128), lambda i, s: (0, i)),
        ),
        compiler_params=pltpu.CompilerParams(vmem_limit_bytes=VMEM_LIMIT),
        cost_estimate=pl.CostEstimate(
            flops=6 * rows * rows * width, bytes_accessed=8 * rows * width, transcendentals=rows * rows * 3
        ),
        name="self_forward",
    )(info, qkv, qkv, qkv)


def cross_fwd_kernel(q_ref, k_ref, v_ref, bias_ref, o_ref):
    block = 256
    for r in range(q_ref.shape[0] // block):
        qq = q_ref[r * block : (r + 1) * block, :]
        total = None
        for h in range(2):
            s = product_nt(pick_head(qq, h), k_ref[...]) + bias_ref[...]
            p = jnp.exp(s - jnp.max(s, axis=1, keepdims=True))
            inv = 1.0 / jnp.sum(p, axis=1, keepdims=True)
            part = product(p.astype(low), pick_head(v_ref[...], h)) * inv
            total = part if total is None else total + part
        o_ref[r * block : (r + 1) * block, :] = total.astype(low)


def cross_forward(q, kv, bias_row):
    rows, width = q.shape
    keys = kv.shape[0]
    return pl.pallas_call(
        cross_fwd_kernel,
        out_shape=jax.ShapeDtypeStruct((rows, width), low),
        grid=(width // 128,),
        in_specs=[
            pl.BlockSpec((rows, 128), lambda i: (0, i)),
            pl.BlockSpec((keys, 128), lambda i: (0, i)),
            pl.BlockSpec((keys, 128), lambda i: (0, width // 128 + i)),
            pl.BlockSpec((1, keys), lambda i: (0, 0)),
        ],
        out_specs=pl.BlockSpec((rows, 128), lambda i: (0, i)),
        compiler_params=pltpu.CompilerParams(vmem_limit_bytes=VMEM_LIMIT),
        cost_estimate=pl.CostEstimate(
            flops=16 * rows * keys * width, bytes_accessed=8 * rows * width, transcendentals=rows * keys * 8
        ),
        name="cross_forward",
    )(q, kv, kv, bias_row)


def back_kernel(info, q_ref, k_ref, v_ref, g0_ref, g1_ref, g2_ref, g3_ref, bias_ref, dq_ref, dk_ref, dv_ref, dk_acc, dv_acc, *, causal):
    rows = q_ref.shape[0]
    keys_all = k_ref.shape[0]
    block = rows // 4
    k_t = k_ref[...].T
    dk_acc[...] = jnp.zeros_like(dk_acc)
    dv_acc[...] = jnp.zeros_like(dv_acc)
    for qb in range(4):
        keys = (qb + 1) * block if causal else keys_all
        kk, vv = k_ref[:keys, :], v_ref[:keys, :]
        qq = q_ref[qb * block : (qb + 1) * block, :]
        gg = (g0_ref, g1_ref, g2_ref, g3_ref)[qb][...]
        q_parts = []
        for h in range(2):
            q_h, g_h = pick_head(qq, h), pick_head(gg, h)
            s = product_nt(kk, q_h)
            if causal:
                key = lax.broadcasted_iota(jnp.int32, s.shape, 0)
                row = lax.broadcasted_iota(jnp.int32, s.shape, 1) + qb * block
                s = jnp.where((key <= row) & (key < info[1]), s, neg_fill)
            else:
                s = s + jnp.concatenate([bias_ref[...]] * (block // 128), axis=1)
            p = jnp.exp(s - jnp.max(s, axis=0, keepdims=True))
            p = p * (1.0 / jnp.sum(p, axis=0, keepdims=True))
            dp = product_nt(vv, g_h)
            e = jnp.sum(p * dp, axis=0, keepdims=True)
            ds = (p * (dp - e)).astype(low)
            dv_acc[:keys, :] += product(p.astype(low), g_h)
            dk_acc[:keys, :] += product(ds, q_h)
            q_parts.append(product(k_t[h * HEAD_DIM : (h + 1) * HEAD_DIM, :keys], ds))
        dq_t = jnp.concatenate(q_parts, axis=0) * 0.125
        dq_ref[qb * block : (qb + 1) * block, :] = dq_t.T.astype(low)
    dk_ref[...] = dk_acc[...].astype(low)
    dv_ref[...] = dv_acc[...].astype(low)


def attention_back(info, q, kv, g, bias, causal):
    rows = q.shape[0]
    keys = kv.shape[0]
    own = pl.BlockSpec((rows, 128), lambda i, s: (0, i))
    pairs = g.shape[1] // 64

    def wide(n):
        return pl.BlockSpec((keys, 128), lambda i, s: (0, n * pairs + s[0] + i))

    mine = pl.BlockSpec((keys, 128), lambda i, s: (0, i))

    def g_block(n):
        return pl.BlockSpec((rows // 4, 128), lambda i, s: (s[2 + n] if causal else n, i))

    first = 1 if causal else 0
    q_spec = wide(0) if causal else own
    width = g.shape[1]
    return pl.pallas_call(
        functools.partial(back_kernel, causal=causal),
        out_shape=[
            jax.ShapeDtypeStruct((rows, width), low),
            jax.ShapeDtypeStruct((keys, width), low),
            jax.ShapeDtypeStruct((keys, width), low),
        ],
        grid_spec=pltpu.PrefetchScalarGridSpec(
            num_scalar_prefetch=1,
            grid=(width // 128,),
            in_specs=[q_spec, wide(first), wide(first + 1)] + [g_block(n) for n in range(4)] + [pl.BlockSpec(bias.shape, lambda i, s: (0, 0))],
            out_specs=[own, mine, mine],
            scratch_shapes=[pltpu.VMEM((keys, 128), jnp.float32), pltpu.VMEM((keys, 128), jnp.float32)],
        ),
        compiler_params=pltpu.CompilerParams(vmem_limit_bytes=VMEM_LIMIT),
        cost_estimate=pl.CostEstimate(
            flops=40 * rows * keys * width // (2 if causal else 1),
            bytes_accessed=14 * rows * width,
            transcendentals=rows * keys * 4,
        ),
        name="self_back" if causal else "cross_back",
    )(info, q, kv, kv, g, g, g, g, bias)


def self_weights_kernel(info, x_ref, q_ref, k_ref, v_ref, wq_ref, wk_ref, wv_ref, grad_ref, part_ref, sums_ref):
    block = part_ref.shape[0]
    size = q_ref.shape[1]
    at = pl.ds(pl.multiple_of(pl.program_id(0) * block, block), block)
    total = None
    for n, (d_ref, w_ref) in enumerate(((q_ref, wq_ref), (k_ref, wk_ref), (v_ref, wv_ref))):
        grad_ref[:, n * size : (n + 1) * size] = product_tn(x_ref[...], d_ref[...]).astype(low)
        part = product_nt(d_ref[at, :], w_ref[...])
        total = part if total is None else total + part
    part_ref[...] = total.astype(low)

    @pl.when(pl.program_id(0) == 0)
    def _():
        sums_ref[...] = jnp.zeros_like(sums_ref)
        sums_ref[0:1, :] = jnp.sum(q_ref[...].astype(jnp.float32), axis=0, keepdims=True)
        sums_ref[1:2, :] = jnp.sum(v_ref[...].astype(jnp.float32), axis=0, keepdims=True)


def self_weights(quart, x, dq, dk, dv, weight):
    rows, width = x.shape
    size = dq.shape[1]
    block = 256
    whole = pl.BlockSpec((rows, size), lambda i, s: (0, 0))

    def slab(n):
        return pl.BlockSpec((width, size), lambda i, s: (0, n * (width // size) + s[0]))

    return pl.pallas_call(
        self_weights_kernel,
        out_shape=[
            jax.ShapeDtypeStruct((width, 3 * size), low),
            jax.ShapeDtypeStruct((rows, width), low),
            jax.ShapeDtypeStruct((8, size), jnp.float32),
        ],
        grid_spec=pltpu.PrefetchScalarGridSpec(
            num_scalar_prefetch=1,
            grid=(rows // block,),
            in_specs=[pl.BlockSpec((rows, block), lambda i, s: (0, i)), whole, whole, whole, slab(0), slab(1), slab(2)],
            out_specs=[
                pl.BlockSpec((block, 3 * size), lambda i, s: (i, 0)),
                pl.BlockSpec((block, width), lambda i, s: (i, 0)),
                pl.BlockSpec((8, size), lambda i, s: (0, 0)),
            ],
        ),
        compiler_params=pltpu.CompilerParams(vmem_limit_bytes=VMEM_LIMIT),
        cost_estimate=pl.CostEstimate(
            flops=12 * rows * width * size, bytes_accessed=20 * rows * width, transcendentals=0
        ),
        name="self_weights",
    )(quart.astype(jnp.int32).reshape(1), x, dq, dk, dv, weight, weight, weight)


def pick_kernel(info, in_ref, out_ref):
    out_ref[...] = in_ref[...]


def pick_columns(matrix, size, count, stride, offset):
    rows = matrix.shape[0]
    return pl.pallas_call(
        pick_kernel,
        out_shape=jax.ShapeDtypeStruct((rows, size * count), matrix.dtype),
        grid_spec=pltpu.PrefetchScalarGridSpec(
            num_scalar_prefetch=1,
            grid=(count,),
            in_specs=[pl.BlockSpec((rows, size), lambda n, s: (0, n * stride + s[0]))],
            out_specs=pl.BlockSpec((rows, size), lambda n, s: (0, n)),
        ),
        cost_estimate=pl.CostEstimate(flops=0, bytes_accessed=4 * rows * size * count, transcendentals=0),
        name="pick_columns",
    )(offset.astype(jnp.int32).reshape(1), matrix)


def swap(part, axis, distance):
    count = lax.axis_size(axis)
    return lax.ppermute(part, axis, [(i, i ^ distance) for i in range(count)])


ORDER = (0, 2, 1, 3)


def gather_rows(part):
    pair = jnp.concatenate([part, swap(part, "mem", 2)], axis=0)
    return jnp.concatenate([pair, swap(pair, "mem", 1)], axis=0)


def bits_of(count, first):
    every = [1 << i for i in range(count.bit_length() - 1)]
    return [first] + [d for d in every if d != first]


def join(part, far):
    pair = jnp.concatenate([part, far], axis=0)
    return jnp.concatenate([pair, swap(pair, "mem", 1)], axis=0)


class Halving:
    def __init__(self, parts, first):
        count = lax.axis_size("dp")
        self.dims = [count]
        self.kept = [a.reshape(count, a.shape[0] // count, a.shape[1]) for a in parts]
        self.left = bits_of(count, first)
        self.done_bits = []
        self.count = count

    def send(self):
        me = lax.axis_index("dp")
        distance = self.left[0]
        below = sum(1 for d in self.left if d < distance)
        low_size = 1 << below
        bit = (me // distance) % 2
        self.mine, theirs = [], []
        for a in self.kept:
            n, r, w = a.shape
            split = a.reshape(n // (2 * low_size), 2, low_size, r, w)
            self.mine.append(lax.dynamic_index_in_dim(split, bit, 1, False).reshape(n // 2, r, w))
            theirs.append(lax.dynamic_index_in_dim(split, 1 - bit, 1, False).reshape(n // 2, r, w))
        return jnp.concatenate([t.astype(low) for t in theirs], axis=2)

    def move(self, sent):
        return swap(sent, "dp", self.left.pop(0))

    def add(self, got):
        start, self.kept = 0, []
        for a in self.mine:
            self.kept.append(a + got[:, :, start : start + a.shape[2]].astype(jnp.float32))
            start += a.shape[2]

    def step(self):
        self.add(self.move(self.send()))

    def finish(self):
        while self.left:
            self.step()
        return [a[0] for a in self.kept]


def tie(*values):
    return lax.optimization_barrier(values)


def finale_kernel(c_ref, f_ref, e_ref, s_ref, b_ref, g_ref, h_ref, v_ref,
                  oc_ref, of_ref, os_ref, ob_ref, og_ref, ov_ref,
                  by, bz, sz, gc, gs, gx, vs, vc, vx, vy, vz, send, recv):
    dp, mem = lax.axis_index("dp"), lax.axis_index("mem")
    y, row = dp % 2, dp // 2
    groups = b_ref.shape[0]
    f32 = jnp.float32
    wide = b_ref.shape[3] // 2
    tall = h_ref.shape[0] // 2

    def quarter_of(m):
        return 2 * (m % 2) + m // 2

    def block_of(m):
        return (m // 2) + (m % 2) * (3 - 2 * (m // 2))

    barrier = pltpu.get_barrier_semaphore()
    core_peer, chip_peer, y_peer = {"mem": mem ^ 1}, {"mem": mem ^ 2}, {"dp": dp ^ 1}
    row_peers = [{"dp": (row ^ j) * 2 + y} for j in range(1, groups)]
    peers = [core_peer, chip_peer, y_peer] + row_peers
    for peer in peers:
        pl.semaphore_signal(barrier, inc=1, device_id=peer, device_id_type=pl.DeviceIdType.MESH)
    pl.semaphore_wait(barrier, len(peers))

    sent = []

    def start(src, dst, peer):
        n = len(sent)
        copy = pltpu.make_async_remote_copy(
            src_ref=src, dst_ref=dst, send_sem=send.at[n], recv_sem=recv.at[n],
            device_id=peer, device_id_type=pl.DeviceIdType.MESH,
        )
        copy.start()
        sent.append(copy)
        return copy

    def to_rows(source, target, own):
        return [start(source(row ^ j), target(own), row_peers[j - 1]) for j in range(1, groups)]

    def wait_all(copies):
        for copy in copies:
            copy.wait_recv()

    def columns(n):
        return pl.ds(n * wide, wide)

    def lines(n):
        return pl.ds(n * tall, tall)

    mine_q, other_q = quarter_of(mem), quarter_of(mem ^ 2)
    block, other = block_of(mem), block_of(mem ^ 2)

    copy_vy = start(v_ref, vy, y_peer)
    copies_by = [start(b_ref.at[:, 1 - y, :, columns(n)], by.at[:, :, columns(n)], y_peer) for n in range(2)]
    copy_g3 = start(g_ref.at[block_of(mem ^ 3)], gc.at[1], core_peer)
    copy_cx = start(c_ref, oc_ref.at[mine_q], chip_peer)
    copies_sz = to_rows(lambda t: s_ref.at[t], lambda t: sz.at[t], row)
    copy_g1 = start(g_ref.at[block_of(mem ^ 1)], gc.at[0], core_peer)
    copy_cc = start(c_ref, oc_ref.at[mine_q], core_peer)
    copy_f0 = start(f_ref, of_ref.at[mine_q], core_peer)
    copy_f1 = start(e_ref, of_ref.at[other_q], core_peer)
    sz[row] = s_ref[row]

    copy_g3.wait_recv()
    copies_gx = []
    for n in range(2):
        gs[lines(n)] = (g_ref[other, lines(n)].astype(f32) + gc[1, lines(n)].astype(f32)).astype(low)
        copies_gx.append(start(gs.at[lines(n)], gx.at[lines(n)], chip_peer))
    copy_vy.wait_recv()
    vs[0] = v_ref[...] + vy[...]
    vz[row] = vs[0]
    copies_vz = to_rows(lambda t: vs.at[0], lambda t: vz.at[t], row)
    oc_ref[mine_q] = c_ref[...]
    of_ref[mine_q] = f_ref[...]
    of_ref[other_q] = e_ref[...]
    copy_g1.wait_recv()

    copies_bz = []

    def first_half(n):
        copies_by[n].wait_recv()
        for t in range(groups):
            by[t, :, columns(n)] = (
                by[t, :, columns(n)].astype(f32) + b_ref[t, y, :, columns(n)].astype(f32)
            ).astype(low)
        bz[row, :, columns(n)] = by[row, :, columns(n)]
        copies_bz.append(
            to_rows(lambda t: by.at[t, :, columns(n)], lambda t: bz.at[t, :, columns(n)], row)
        )

    def rows_total(n):
        copies_gx[n].wait_recv()
        total = h_ref[lines(n)] + g_ref[block, lines(n)].astype(f32)
        total = total + gc[0, lines(n)].astype(f32) + gx[lines(n)].astype(f32)
        og_ref[block, lines(n)] = total.astype(low)
        piece = og_ref.at[block, lines(n)]
        return [start(piece, piece, chip_peer), start(piece, piece, core_peer)]

    first_half(0)
    wait_all(copies_vz)
    total = vz[0]
    for t in range(1, groups):
        total = total + vz[t]
    vs[1] = total
    copy_vc = start(vs.at[1], vc, core_peer)
    wait_all(copies_sz)
    total = sz[0].astype(f32)
    for t in range(1, groups):
        total = total + sz[t].astype(f32)
    os_ref[mine_q] = total.astype(low)
    piece_s = os_ref.at[mine_q]
    copy_sx, copy_sc = start(piece_s, piece_s, chip_peer), start(piece_s, piece_s, core_peer)
    copies_g0 = rows_total(0)
    copy_vc.wait_recv()
    vs[2] = vs[1] + vc[...]
    copy_vx = start(vs.at[2], vx, chip_peer)
    copy_cx.wait_recv()
    copy_cr = start(oc_ref.at[other_q], oc_ref.at[other_q], core_peer)
    first_half(1)
    copies_g1 = rows_total(1)
    copy_sx.wait_recv()
    copy_sr = start(os_ref.at[other_q], os_ref.at[other_q], core_peer)

    copies_b, relays = [], []
    for n in range(2):
        wait_all(copies_bz[n])
        total = bz[0, :, columns(n)].astype(f32)
        for t in range(1, groups):
            total = total + bz[t, :, columns(n)].astype(f32)
        ob_ref[mine_q, :, columns(n)] = total.astype(low)
        piece = ob_ref.at[mine_q, :, columns(n)]
        copies_b.append([start(piece, piece, chip_peer), start(piece, piece, core_peer)])
        (copies_g0, copies_g1)[n][0].wait_recv()
        piece = og_ref.at[other, lines(n)]
        relays.append(start(piece, piece, core_peer))
    copy_vx.wait_recv()
    ov_ref[...] = vs[2] + vx[...]
    for n in range(2):
        copies_b[n][0].wait_recv()
        piece = ob_ref.at[other_q, :, columns(n)]
        relays.append(start(piece, piece, core_peer))
    wait_all([copy_cc, copy_f0, copy_f1, copy_cr, copy_sc, copy_sr])
    wait_all([copies_g0[1], copies_g1[1], copies_b[0][1], copies_b[1][1]] + relays)
    for copy in sent:
        copy.wait_send()


def finale(c, f, e, s, b, g, h, v):
    groups, _, r, wb = b.shape
    ws = s.shape[2]
    copies = 29 + 4 * (groups - 1)
    vmem = pl.BlockSpec(memory_space=pltpu.VMEM)
    f32 = jnp.float32
    half_rows = pltpu.VMEM(g.shape[1:], low)
    vector = pltpu.VMEM(v.shape, f32)
    return pl.pallas_call(
        finale_kernel,
        out_shape=[jax.ShapeDtypeStruct((4, r, a.shape[-1]), low) for a in (c, f, s, b)]
        + [jax.ShapeDtypeStruct(g.shape, low), jax.ShapeDtypeStruct(v.shape, f32)],
        in_specs=[vmem] * 8,
        out_specs=[vmem] * 6,
        scratch_shapes=[
            pltpu.VMEM((groups, r, wb), low),
            pltpu.VMEM((groups, r, wb), low),
            pltpu.VMEM((groups, r, ws), low),
            pltpu.VMEM((2,) + g.shape[1:], low),
            half_rows,
            half_rows,
            pltpu.VMEM((3,) + v.shape, f32),
            vector,
            vector,
            vector,
            pltpu.VMEM((groups,) + v.shape, f32),
            pltpu.SemaphoreType.DMA((copies,)),
            pltpu.SemaphoreType.DMA((copies,)),
        ],
        compiler_params=pltpu.CompilerParams(
            collective_id=0, has_side_effects=True, vmem_limit_bytes=VMEM_LIMIT
        ),
        cost_estimate=pl.CostEstimate(flops=10**6, bytes_accessed=10**8, transcendentals=0),
        name="finale",
    )(c, f, e, s, b, g, h, v)


def unpack_kernel(c_ref, f_ref, s_ref, b_ref, g_ref, v_ref, qkv_ref, so_ref, cq_ref, ckv_ref, co_ref, fi_ref, fo_ref, gd_ref,
                  pb_ref, ng_ref, ns_ref, fb_ref, *, quarter, piece):
    f32 = jnp.float32

    def spread(source, start, count, size, target):
        for p in range(4):
            for n in range(count):
                target[:, (n * 4 + p) * size : (n * 4 + p + 1) * size] = source[
                    p, :, start + n * size : start + (n + 1) * size
                ].astype(f32)

    spread(b_ref, 0, 3, quarter, qkv_ref)
    spread(c_ref, 0, 1, quarter, co_ref)
    spread(c_ref, quarter, 1, quarter, cq_ref)
    spread(c_ref, 2 * quarter, 2, quarter, ckv_ref)
    spread(s_ref, 0, 1, quarter, so_ref)
    spread(f_ref, 0, quarter * 4 // piece, piece, fi_ref)
    for p in range(4):
        fo_ref[p] = f_ref[p, :, 4 * quarter :].astype(f32)
        gd_ref[p] = g_ref[p].astype(f32)
    at = 0
    for target in (pb_ref, ng_ref, ns_ref, fb_ref):
        target[...] = v_ref[at : at + target.shape[0], :]
        at += target.shape[0]


def unpack(c, f, s, b, g, v, width, hidden, piece):
    r = c.shape[1]
    steps = 4 if r % 64 == 0 else 1
    h, gh = r // steps, g.shape[1] // steps
    f32 = jnp.float32

    def slots(x, n):
        return pl.BlockSpec((4, n, x.shape[2]), lambda i: (0, i, 0))

    wide = [3 * width, width, width, 2 * width, width, hidden]
    counts = [7, 3, 3, hidden // width]
    return pl.pallas_call(
        functools.partial(unpack_kernel, quarter=width // 4, piece=piece),
        out_shape=[jax.ShapeDtypeStruct((r, w), f32) for w in wide]
        + [jax.ShapeDtypeStruct((4, r, width), f32), jax.ShapeDtypeStruct(g.shape, f32)]
        + [jax.ShapeDtypeStruct((n, width), f32) for n in counts],
        grid=(steps,),
        in_specs=[slots(c, h), slots(f, h), slots(s, h), slots(b, h), slots(g, gh), pl.BlockSpec(v.shape, lambda i: (0, 0))],
        out_specs=[pl.BlockSpec((h, w), lambda i: (i, 0)) for w in wide]
        + [pl.BlockSpec((4, h, width), lambda i: (0, i, 0)), slots(g, gh)]
        + [pl.BlockSpec((n, width), lambda i: (0, 0)) for n in counts],
        compiler_params=pltpu.CompilerParams(vmem_limit_bytes=VMEM_LIMIT),
        cost_estimate=pl.CostEstimate(flops=10**6, bytes_accessed=2 * 10**7, transcendentals=0),
        name="unpack",
    )(c, f, s, b, g, v)


def per_device(
    dec_in,
    memory,
    dec_len,
    mem_len,
    grad_out,
    self_qkv,
    self_out,
    cross_q,
    cross_kv,
    cross_out,
    ffn_in,
    ffn_out,
    proj_bias,
    ffn_bias,
    norm_gain,
    norm_shift,
):
    x_full = dec_in[0]
    rows, width = x_full.shape
    hidden = ffn_in.shape[1]
    block = rows // 4
    half, quarter = width // 2, width // 4
    groups = lax.axis_size("dp")
    mem_rows = memory[0]
    mem_block = mem_rows.shape[0]
    me = lax.axis_index("mem")
    chip, core = me // 2, me % 2
    quart = 2 * core + chip

    def block_of(m):
        return jnp.where(m // 2 == 0, 3 * (m % 2), 1 + m % 2)

    def cut(a, start, size, axis=1):
        return lax.dynamic_slice_in_dim(a, start, size, axis)

    def own_rows(a):
        return cut(a, block_of(me) * block, block, 0)

    def by_block(gathered):
        size = gathered.shape[0] // 4
        where = [0, 2, 3, 1]
        pieces = []
        for n in range(4):
            offset = me ^ where[n]
            slot = (offset % 2) * 2 + offset // 2
            pieces.append(cut(gathered, slot * size, size, 0))
        return jnp.concatenate(pieces, axis=0)

    def by_quarter(slots):
        stacked = jnp.stack(slots)
        where = [0, 2, 1, 3]
        out = []
        for n in range(4):
            offset = me ^ where[n]
            out.append(lax.dynamic_index_in_dim(stacked, (offset % 2) * 2 + offset // 2, 0, False))
        return out

    mem_far = swap(mem_rows, "mem", 2)

    side = core * half
    qkv8 = project(core, x_full, self_qkv, proj_bias, (0, None, 1), (0.125, 1.0, 1.0))
    info_f = jnp.stack([chip, dec_len[0]]).astype(jnp.int32)
    att8 = self_forward(info_f, qkv8)
    att8, mem_far = tie(att8, mem_far)
    mem_full = join(mem_rows, mem_far)

    def heads_to_rows(a8):
        mine = cut(a8, core * block, block, 0)
        other = swap(cut(a8, (1 - core) * block, block, 0), "mem", 1)
        return jnp.where(
            core == 0, jnp.concatenate([mine, other], axis=1), jnp.concatenate([other, mine], axis=1)
        )

    attended = heads_to_rows(att8)
    x_own = own_rows(x_full).astype(jnp.float32)
    first, first_norm, first_inv = normalize(
        x_own + product(attended, self_out) + proj_bias[2], norm_gain[0], norm_shift[0]
    )
    first_low = first.astype(low)
    first_other = swap(first_low, "mem", 1)
    first_chip = jnp.where(
        core == 0,
        jnp.concatenate([first_low, first_other], axis=0),
        jnp.concatenate([first_other, first_low], axis=0),
    )

    cq8 = ((product(first_chip, cut(cross_q, side, half)) + cut(proj_bias[3], side, half, 0)) * 0.125).astype(low)
    kvc8 = project(core, mem_full, cross_kv, proj_bias, (None, 4), (1.0, 1.0))
    slot_pos = jnp.stack([(me ^ k) * mem_block for k in ORDER])
    mem_pos = (slot_pos[:, None] + jnp.arange(mem_block, dtype=jnp.int32)[None, :]).reshape(-1)
    mem_bias = jnp.where(mem_pos < mem_len[0], 0.0, neg_fill).astype(jnp.float32)
    crossed = heads_to_rows(cross_forward(cq8, kvc8, mem_bias[None, :]))
    second, second_norm, second_inv = normalize(
        first + product(crossed, cross_out) + proj_bias[5], norm_gain[1], norm_shift[1]
    )
    second_low = second.astype(low)

    second_full = gather_rows(second_low)
    inner = product(second_low, ffn_in) + ffn_bias
    act, act_grad = gelu_parts(inner)
    act, act_grad = act.astype(low), act_grad.astype(low)
    third, third_norm, third_inv = normalize(
        second + product(act, ffn_out) + proj_bias[6], norm_gain[2], norm_shift[2]
    )
    row_pos = block_of(me) * block + jnp.arange(block, dtype=jnp.int32)
    cot = jnp.where((row_pos < dec_len[0])[:, None], own_rows(grad_out[0]).astype(jnp.float32), 0.0)
    dh3, gain_three, shift_three = norm_back(cot, third_norm, third_inv, norm_gain[2])
    dz = dh3.astype(low)
    first_full = gather_rows(first_low)
    dz, late = tie(dz, quart)
    piece = hidden // groups // 4
    if piece % 128 == 0:
        w_in_q = pick_columns(ffn_in, piece, groups, 4, late)
    else:
        w_in_q = lax.dynamic_index_in_dim(ffn_in.reshape(width, groups, 4, piece), late, 2, False)
        w_in_q = w_in_q.reshape(width, hidden // 4)
    w_out_q = lax.dynamic_index_in_dim(ffn_out.reshape(groups, 4, piece, width), late, 1, False)
    w_out_q = w_out_q.reshape(hidden // 4, width)
    dz_far = swap(dz, "mem", 2)
    wide = quart * quarter
    cq4 = ((product(first_full, cut(cross_q, wide, quarter)) + cut(proj_bias[3], wide, quarter, 0)) * 0.125).astype(low)
    du = (product_nt(dz, ffn_out) * act_grad.astype(jnp.float32)).astype(low)
    du, dz_far = tie(du, dz_far)
    dh2, gain_two, shift_two = norm_back(
        dh3 + product_nt(du, ffn_in), second_norm, second_inv, norm_gain[1]
    )
    dco = dh2.astype(low)

    dz_full = join(dz, dz_far)
    dco_far = swap(dco, "mem", 2)
    b_in_q = lax.dynamic_index_in_dim(ffn_bias.reshape(groups, 4, piece), quart, 1, False).reshape(-1)
    act_q, slope_q = gelu_parts(product(second_full, w_in_q) + b_in_q)
    act_q = act_q.astype(low)
    du_q = (product_nt(dz_full, w_out_q) * slope_q).astype(low)
    du_q, dco_far, third_low = tie(du_q, dco_far, third.astype(low))
    dco_full = join(dco, dco_far)
    third_far = swap(third_low, "mem", 2)
    sum_in = Halving([product_tn(second_full, du_q)], 1)
    sum_out = Halving([product_tn(act_q, dz_full)], min(2, groups // 2))
    send_in, send_out = sum_in.send(), sum_out.send()

    dx4 = product_nt(dco_full, cut(cross_out, wide, quarter, 0)).astype(low)
    pair_base = chip * (quarter // 128)
    info_c = jnp.stack([pair_base]).astype(jnp.int32)
    bias_col = jnp.broadcast_to(mem_bias[:, None], (mem_bias.shape[0], 128))
    dx4, send_in, send_out, third_far, crossed_late = tie(dx4, send_in, send_out, third_far, crossed)
    crossed_far = swap(crossed_late, "mem", 2)
    got_in, got_out = sum_in.move(send_in), sum_out.move(send_out)
    dq4, dkc4, dvc4 = attention_back(info_c, cq4, kvc8, dx4, bias_col, False)
    dq4, dkc4, dvc4, got_in, got_out, crossed_far = tie(dq4, dkc4, dvc4, got_in, got_out, crossed_far)
    sum_in.add(got_in)
    sum_out.add(got_out)
    dkv4 = jnp.concatenate([dkc4, dvc4], axis=1)

    def over_chips(a):
        b0, b2, b1, b3 = jnp.split(a, 4, axis=0)
        return jnp.concatenate([b2, b3], axis=0), b0, b1

    def to_rows(over, b0, b1):
        size = b0.shape[0]
        mine = jnp.concatenate([b0, over[:size]], axis=0)
        other = swap(jnp.concatenate([b1, over[size:]], axis=0), "mem", 1)
        return by_quarter([mine[:size], mine[size:], other[:size], other[size:]])

    dq_leave, dq_0, dq_1 = over_chips(dq4)
    dkv_leave, dkv_0, dkv_1 = over_chips(dkv4)
    dq_far = swap(dq_leave, "mem", 2)
    send_in, send_out = sum_in.send(), sum_out.send()
    dq_far, send_in, send_out = tie(dq_far, send_in, send_out)
    dq_own = jnp.concatenate(to_rows(dq_far, dq_0, dq_1), axis=1)
    got_in, got_out = sum_in.move(send_in), sum_out.move(send_out)
    crossed_full = join(crossed, crossed_far)
    attended_full = gather_rows(attended)
    dh1, gain_one, shift_one = norm_back(
        dh2 + product_nt(dq_own, cross_q), first_norm, first_inv, norm_gain[0]
    )
    do = dh1.astype(low)
    sum_w = Halving(
        [product_tn(crossed_full, cut(dco_full, wide, quarter)), product_tn(first_full, dq4)], 1
    )
    sum_kv = Halving([product_tn(mem_full, dkv4)], min(2, groups // 2))
    got_w, got_kv = sum_w.move(sum_w.send()), sum_kv.move(sum_kv.send())
    do_far = swap(do, "mem", 2)
    do_far, got_in, got_out, got_w = tie(do_far, got_in, got_out, got_w)
    do_full, got_kv = tie(join(do, do_far), got_kv)
    sum_in.add(got_in)
    sum_out.add(got_out)
    sum_in.kept = sum_in.kept + sum_out.kept
    sum_w.add(got_w)
    sum_kv.add(got_kv)
    sum_so = Halving([product_tn(attended_full, cut(do_full, wide, quarter))], 1)

    da4 = product_nt(do_full, cut(self_out, wide, quarter, 0)).astype(low)
    where = [0, 2, 3, 1]
    slots = [((me ^ n) % 2) * 2 + (me ^ n) // 2 for n in where]
    info_s = jnp.stack([pair_base, dec_len[0]] + slots).astype(jnp.int32)
    send_in, send_w, send_kv, send_so = sum_in.send(), sum_w.send(), sum_kv.send(), sum_so.send()
    da4, send_in, send_w, send_kv, send_so, dkv_leave = tie(da4, send_in, send_w, send_kv, send_so, dkv_leave)
    got_in, got_w, got_kv = sum_in.move(send_in), sum_w.move(send_w), sum_kv.move(send_kv)
    got_so = sum_so.move(send_so)
    dkv_far = swap(dkv_leave, "mem", 2)
    sq4, sk4, sv4 = attention_back(info_s, qkv8, qkv8, da4, bias_col[:8], True)
    sq4, sk4, sv4, got_in, got_w, got_kv, got_so, dkv_far = tie(
        sq4, sk4, sv4, got_in, got_w, got_kv, got_so, dkv_far
    )
    sum_in.add(got_in)
    ffn_grad = jnp.concatenate([part.astype(low) for part in sum_in.finish()], axis=1)
    sum_w.add(got_w)
    sum_kv.add(got_kv)
    sum_so.add(got_so)
    sum_w.kept = sum_w.kept + sum_kv.kept
    send_w = sum_w.send()
    sq4, sk4, sv4, send_w, ffn_grad = tie(sq4, sk4, sv4, send_w, ffn_grad)
    ffn_far = swap(ffn_grad, "mem", 2)
    got_w = sum_w.move(send_w)
    dkv_parts = to_rows(dkv_far, dkv_0, dkv_1)
    dkv_own = jnp.concatenate(
        [a[:, :quarter] for a in dkv_parts] + [a[:, quarter:] for a in dkv_parts], axis=1
    )
    grad_memory = product_nt(dkv_own, cross_kv)[None]

    per = width // groups
    qkv_grad, partial, own_sums = self_weights(quart, x_full, sq4, sk4, sv4, self_qkv)
    qkv_grad = qkv_grad.reshape(groups // 2, 2, per, 3 * quarter)
    partial = partial.reshape(4, block, width)
    qkv_grad, got_w, ffn_far, grad_memory = tie(qkv_grad, got_w, ffn_far, grad_memory)
    sum_w.add(got_w)
    cross_grad = jnp.concatenate([part.astype(low) for part in sum_w.finish()], axis=1)
    so_grad = sum_so.kept[0].astype(low)
    layer_out = by_block(join(third_low, third_far))[None]

    place = jnp.zeros((2, width), jnp.float32)
    own_sums = own_sums[:2]
    place = lax.dynamic_update_slice(place, own_sums, (0, quart * quarter))
    packed = jnp.concatenate(
        [
            place,
            jnp.stack(
                [
                    column_sum(do),
                    column_sum(dq_own),
                    column_sum(dkv_own[:, width:]),
                    column_sum(dco),
                    column_sum(dz),
                    gain_one,
                    gain_two,
                    gain_three,
                    shift_one,
                    shift_two,
                    shift_three,
                ]
            ),
            column_sum(du).reshape(hidden // width, width),
        ],
        axis=0,
    )
    packed = jnp.pad(packed, ((0, -packed.shape[0] % 8), (0, 0)))
    cross_w, ffn_w, so_w, qkv_w, grad_rows, packed = finale(
        cross_grad, ffn_grad, ffn_far, so_grad, qkv_grad, partial, dh1, packed
    )
    w_qkv, w_so, w_cq, w_ckv, w_co, w_fi, w_fo, grad_dec, p_bias, n_gain, n_shift, f_bias = unpack(
        cross_w, ffn_w, so_w, qkv_w, grad_rows, packed, width, hidden, piece
    )
    return (
        layer_out,
        grad_dec.reshape(1, rows, width),
        grad_memory,
        w_qkv,
        w_so,
        w_cq,
        w_ckv,
        w_co,
        w_fi,
        w_fo.reshape(-1, width),
        p_bias,
        f_bias.reshape(hidden),
        n_gain,
        n_shift,
    )


def solution(mesh):
    in_specs = (
        P("dp", None, None),
        P("dp", "mem", None),
        P("dp"),
        P("dp"),
        P("dp", None, None),
    ) + (P(),) * 11
    out_specs = (
        P("dp", None, None),
        P("dp", None, None),
        P("dp", "mem", None),
    ) + (P("dp", None),) * 7 + (P(),) * 4
    return jax.shard_map(
        per_device, mesh=mesh, in_specs=in_specs, out_specs=out_specs, check_vma=False
    )
```

```python
import functools

import jax
import jax.numpy as jnp
from jax import lax
from jax.experimental import pallas as pl
from jax.experimental.pallas import tpu as pltpu
from jax.sharding import PartitionSpec as P

HEAD_DIM = 64
norm_eps = 1e-05
neg_fill = -1e30
low = jnp.bfloat16
VMEM_LIMIT = 56 * 1024 * 1024


def product(left_rows, right_rows):
    return jnp.dot(left_rows, right_rows, preferred_element_type=jnp.float32)


def product_tn(left_rows, right_rows):
    return lax.dot_general(
        left_rows, right_rows, (((0,), (0,)), ((), ())), preferred_element_type=jnp.float32
    )


def product_nt(left_rows, right_rows):
    return lax.dot_general(
        left_rows, right_rows, (((1,), (1,)), ((), ())), preferred_element_type=jnp.float32
    )


def normalize(hidden, scale_row, shift_row):
    row_mean = jnp.mean(hidden, axis=-1, keepdims=True)
    centered = hidden - row_mean
    variance = jnp.mean(centered * centered, axis=-1, keepdims=True)
    inverse = lax.rsqrt(variance + norm_eps)
    normed = centered * inverse
    return (normed * scale_row + shift_row, normed, inverse)


def norm_back(grad_rows, normed, inverse, scale_row):
    scaled = grad_rows * scale_row
    grad_hidden = inverse * (
        scaled
        - jnp.mean(scaled, axis=-1, keepdims=True)
        - normed * jnp.mean(scaled * normed, axis=-1, keepdims=True)
    )
    return (grad_hidden, jnp.sum(grad_rows * normed, axis=0), jnp.sum(grad_rows, axis=0))


def gelu_parts(values):
    cdf = 0.5 * (1.0 + lax.erf(values * 0.7071067811865476))
    density = jnp.exp(-0.5 * values * values) * 0.3989422804014327
    return values * cdf, cdf + values * density


def column_sum(matrix):
    return jnp.sum(matrix.astype(jnp.float32), axis=0)


def lane_head(rows):
    return lax.broadcasted_iota(jnp.int32, (rows, 128), 1) // HEAD_DIM


def pick_head(pair, h):
    return jnp.where(lane_head(pair.shape[0]) == h, pair, jnp.zeros_like(pair))


def project_kernel(info, x_ref, w_ref, bias_ref, o_ref, *, bias_rows, scales):
    total = product(x_ref[...], w_ref[...])
    for n, (bias_row, scale) in enumerate(zip(bias_rows, scales)):

        @pl.when(pl.program_id(0) == n)
        def _():
            out = total
            if bias_row is not None:
                out = out + bias_ref[bias_row : bias_row + 1, :]
            if scale != 1.0:
                out = out * scale
            o_ref[...] = out.astype(low)


def project(core, x, weight, bias, bias_rows, scales):
    rows, width = x.shape
    half = width // 2
    size = 256
    count = half // size
    parts = len(scales)
    return pl.pallas_call(
        functools.partial(project_kernel, bias_rows=bias_rows, scales=scales),
        out_shape=jax.ShapeDtypeStruct((rows, parts * half), low),
        grid_spec=pltpu.PrefetchScalarGridSpec(
            num_scalar_prefetch=1,
            grid=(parts, count),
            in_specs=[
                pl.BlockSpec((rows, width), lambda p, j, s: (0, 0)),
                pl.BlockSpec((width, size), lambda p, j, s: (0, p * 2 * count + s[0] * count + j)),
                pl.BlockSpec((bias.shape[0], size), lambda p, j, s: (0, s[0] * count + j)),
            ],
            out_specs=pl.BlockSpec((rows, size), lambda p, j, s: (0, p * count + j)),
        ),
        compiler_params=pltpu.CompilerParams(vmem_limit_bytes=VMEM_LIMIT),
        cost_estimate=pl.CostEstimate(
            flops=2 * rows * width * half * parts, bytes_accessed=2 * rows * width * (1 + parts), transcendentals=0
        ),
        name="project",
    )(core.astype(jnp.int32).reshape(1), x, weight, bias)


def self_fwd_kernel(info, q_ref, k_ref, v_ref, o_ref):
    rows = k_ref.shape[0]
    block = rows // 4
    dec_len = info[1]

    def process(qb, slot):
        keys = (qb + 1) * block
        kk, vv = k_ref[:keys, :], v_ref[:keys, :]
        qq = q_ref[qb * block : (qb + 1) * block, :]
        total = None
        for h in range(2):
            s = product_nt(pick_head(qq, h), kk)
            col = lax.broadcasted_iota(jnp.int32, s.shape, 1)
            row = lax.broadcasted_iota(jnp.int32, s.shape, 0) + qb * block
            s = jnp.where((col <= row) & (col < dec_len), s, neg_fill)
            p = jnp.exp(s - jnp.max(s, axis=1, keepdims=True))
            inv = 1.0 / jnp.sum(p, axis=1, keepdims=True)
            part = product(p.astype(low), pick_head(vv, h)) * inv
            total = part if total is None else total + part
        o_ref[slot * block : (slot + 1) * block, :] = total.astype(low)

    @pl.when(info[0] == 0)
    def _():
        process(0, 0)
        process(3, 1)

    @pl.when(info[0] == 1)
    def _():
        process(1, 0)
        process(2, 1)


def self_forward(info, qkv):
    rows, width = qkv.shape[0], qkv.shape[1] // 3
    pairs = width // 128

    def spec(n):
        return pl.BlockSpec((rows, 128), lambda i, s: (0, n * pairs + i))

    return pl.pallas_call(
        self_fwd_kernel,
        out_shape=jax.ShapeDtypeStruct((rows // 2, width), low),
        grid_spec=pltpu.PrefetchScalarGridSpec(
            num_scalar_prefetch=1,
            grid=(pairs,),
            in_specs=[spec(0), spec(1), spec(2)],
            out_specs=pl.BlockSpec((rows // 2, 128), lambda i, s: (0, i)),
        ),
        compiler_params=pltpu.CompilerParams(vmem_limit_bytes=VMEM_LIMIT),
        cost_estimate=pl.CostEstimate(
            flops=6 * rows * rows * width, bytes_accessed=8 * rows * width, transcendentals=rows * rows * 3
        ),
        name="self_forward",
    )(info, qkv, qkv, qkv)


def cross_fwd_kernel(q_ref, k_ref, v_ref, bias_ref, o_ref):
    block = 256
    for r in range(q_ref.shape[0] // block):
        qq = q_ref[r * block : (r + 1) * block, :]
        total = None
        for h in range(2):
            s = product_nt(pick_head(qq, h), k_ref[...]) + bias_ref[...]
            p = jnp.exp(s - jnp.max(s, axis=1, keepdims=True))
            inv = 1.0 / jnp.sum(p, axis=1, keepdims=True)
            part = product(p.astype(low), pick_head(v_ref[...], h)) * inv
            total = part if total is None else total + part
        o_ref[r * block : (r + 1) * block, :] = total.astype(low)


def cross_forward(q, kv, bias_row):
    rows, width = q.shape
    keys = kv.shape[0]
    return pl.pallas_call(
        cross_fwd_kernel,
        out_shape=jax.ShapeDtypeStruct((rows, width), low),
        grid=(width // 128,),
        in_specs=[
            pl.BlockSpec((rows, 128), lambda i: (0, i)),
            pl.BlockSpec((keys, 128), lambda i: (0, i)),
            pl.BlockSpec((keys, 128), lambda i: (0, width // 128 + i)),
            pl.BlockSpec((1, keys), lambda i: (0, 0)),
        ],
        out_specs=pl.BlockSpec((rows, 128), lambda i: (0, i)),
        compiler_params=pltpu.CompilerParams(vmem_limit_bytes=VMEM_LIMIT),
        cost_estimate=pl.CostEstimate(
            flops=16 * rows * keys * width, bytes_accessed=8 * rows * width, transcendentals=rows * keys * 8
        ),
        name="cross_forward",
    )(q, kv, kv, bias_row)


def back_kernel(info, q_ref, k_ref, v_ref, g0_ref, g1_ref, g2_ref, g3_ref, bias_ref, dq_ref, dk_ref, dv_ref, dk_acc, dv_acc, *, causal):
    rows = q_ref.shape[0]
    keys_all = k_ref.shape[0]
    block = rows // 4
    k_t = k_ref[...].T
    dk_acc[...] = jnp.zeros_like(dk_acc)
    dv_acc[...] = jnp.zeros_like(dv_acc)
    for qb in range(4):
        keys = (qb + 1) * block if causal else keys_all
        kk, vv = k_ref[:keys, :], v_ref[:keys, :]
        qq = q_ref[qb * block : (qb + 1) * block, :]
        gg = (g0_ref, g1_ref, g2_ref, g3_ref)[qb][...]
        q_parts = []
        for h in range(2):
            q_h, g_h = pick_head(qq, h), pick_head(gg, h)
            s = product_nt(kk, q_h)
            if causal:
                key = lax.broadcasted_iota(jnp.int32, s.shape, 0)
                row = lax.broadcasted_iota(jnp.int32, s.shape, 1) + qb * block
                s = jnp.where((key <= row) & (key < info[1]), s, neg_fill)
            else:
                s = s + jnp.concatenate([bias_ref[...]] * (block // 128), axis=1)
            p = jnp.exp(s - jnp.max(s, axis=0, keepdims=True))
            p = p * (1.0 / jnp.sum(p, axis=0, keepdims=True))
            dp = product_nt(vv, g_h)
            e = jnp.sum(p * dp, axis=0, keepdims=True)
            ds = (p * (dp - e)).astype(low)
            dv_acc[:keys, :] += product(p.astype(low), g_h)
            dk_acc[:keys, :] += product(ds, q_h)
            q_parts.append(product(k_t[h * HEAD_DIM : (h + 1) * HEAD_DIM, :keys], ds))
        dq_t = jnp.concatenate(q_parts, axis=0) * 0.125
        dq_ref[qb * block : (qb + 1) * block, :] = dq_t.T.astype(low)
    dk_ref[...] = dk_acc[...].astype(low)
    dv_ref[...] = dv_acc[...].astype(low)


def attention_back(info, q, kv, g, bias, causal):
    rows = q.shape[0]
    keys = kv.shape[0]
    own = pl.BlockSpec((rows, 128), lambda i, s: (0, i))
    pairs = g.shape[1] // 64

    def wide(n):
        return pl.BlockSpec((keys, 128), lambda i, s: (0, n * pairs + s[0] + i))

    mine = pl.BlockSpec((keys, 128), lambda i, s: (0, i))

    def g_block(n):
        return pl.BlockSpec((rows // 4, 128), lambda i, s: (s[2 + n] if causal else n, i))

    first = 1 if causal else 0
    q_spec = wide(0) if causal else own
    width = g.shape[1]
    return pl.pallas_call(
        functools.partial(back_kernel, causal=causal),
        out_shape=[
            jax.ShapeDtypeStruct((rows, width), low),
            jax.ShapeDtypeStruct((keys, width), low),
            jax.ShapeDtypeStruct((keys, width), low),
        ],
        grid_spec=pltpu.PrefetchScalarGridSpec(
            num_scalar_prefetch=1,
            grid=(width // 128,),
            in_specs=[q_spec, wide(first), wide(first + 1)] + [g_block(n) for n in range(4)] + [pl.BlockSpec(bias.shape, lambda i, s: (0, 0))],
            out_specs=[own, mine, mine],
            scratch_shapes=[pltpu.VMEM((keys, 128), jnp.float32), pltpu.VMEM((keys, 128), jnp.float32)],
        ),
        compiler_params=pltpu.CompilerParams(vmem_limit_bytes=VMEM_LIMIT),
        cost_estimate=pl.CostEstimate(
            flops=40 * rows * keys * width // (2 if causal else 1),
            bytes_accessed=14 * rows * width,
            transcendentals=rows * keys * 4,
        ),
        name="self_back" if causal else "cross_back",
    )(info, q, kv, kv, g, g, g, g, bias)


def self_weights_kernel(info, x_ref, q_ref, k_ref, v_ref, wq_ref, wk_ref, wv_ref, grad_ref, part_ref, sums_ref):
    block = part_ref.shape[0]
    size = q_ref.shape[1]
    at = pl.ds(pl.multiple_of(pl.program_id(0) * block, block), block)
    total = None
    for n, (d_ref, w_ref) in enumerate(((q_ref, wq_ref), (k_ref, wk_ref), (v_ref, wv_ref))):
        grad_ref[:, n * size : (n + 1) * size] = product_tn(x_ref[...], d_ref[...]).astype(low)
        part = product_nt(d_ref[at, :], w_ref[...])
        total = part if total is None else total + part
    part_ref[...] = total.astype(low)

    @pl.when(pl.program_id(0) == 0)
    def _():
        sums_ref[...] = jnp.zeros_like(sums_ref)
        sums_ref[0:1, :] = jnp.sum(q_ref[...].astype(jnp.float32), axis=0, keepdims=True)
        sums_ref[1:2, :] = jnp.sum(v_ref[...].astype(jnp.float32), axis=0, keepdims=True)


def self_weights(quart, x, dq, dk, dv, weight):
    rows, width = x.shape
    size = dq.shape[1]
    block = 256
    whole = pl.BlockSpec((rows, size), lambda i, s: (0, 0))

    def slab(n):
        return pl.BlockSpec((width, size), lambda i, s: (0, n * (width // size) + s[0]))

    return pl.pallas_call(
        self_weights_kernel,
        out_shape=[
            jax.ShapeDtypeStruct((width, 3 * size), low),
            jax.ShapeDtypeStruct((rows, width), low),
            jax.ShapeDtypeStruct((8, size), jnp.float32),
        ],
        grid_spec=pltpu.PrefetchScalarGridSpec(
            num_scalar_prefetch=1,
            grid=(rows // block,),
            in_specs=[pl.BlockSpec((rows, block), lambda i, s: (0, i)), whole, whole, whole, slab(0), slab(1), slab(2)],
            out_specs=[
                pl.BlockSpec((block, 3 * size), lambda i, s: (i, 0)),
                pl.BlockSpec((block, width), lambda i, s: (i, 0)),
                pl.BlockSpec((8, size), lambda i, s: (0, 0)),
            ],
        ),
        compiler_params=pltpu.CompilerParams(vmem_limit_bytes=VMEM_LIMIT),
        cost_estimate=pl.CostEstimate(
            flops=12 * rows * width * size, bytes_accessed=20 * rows * width, transcendentals=0
        ),
        name="self_weights",
    )(quart.astype(jnp.int32).reshape(1), x, dq, dk, dv, weight, weight, weight)


def pick_kernel(info, in_ref, out_ref):
    out_ref[...] = in_ref[...]


def pick_columns(matrix, size, count, stride, offset):
    rows = matrix.shape[0]
    return pl.pallas_call(
        pick_kernel,
        out_shape=jax.ShapeDtypeStruct((rows, size * count), matrix.dtype),
        grid_spec=pltpu.PrefetchScalarGridSpec(
            num_scalar_prefetch=1,
            grid=(count,),
            in_specs=[pl.BlockSpec((rows, size), lambda n, s: (0, n * stride + s[0]))],
            out_specs=pl.BlockSpec((rows, size), lambda n, s: (0, n)),
        ),
        cost_estimate=pl.CostEstimate(flops=0, bytes_accessed=4 * rows * size * count, transcendentals=0),
        name="pick_columns",
    )(offset.astype(jnp.int32).reshape(1), matrix)


def swap(part, axis, distance):
    count = lax.axis_size(axis)
    return lax.ppermute(part, axis, [(i, i ^ distance) for i in range(count)])


ORDER = (0, 2, 1, 3)


def gather_rows(part):
    pair = jnp.concatenate([part, swap(part, "mem", 2)], axis=0)
    return jnp.concatenate([pair, swap(pair, "mem", 1)], axis=0)


def bits_of(count, first):
    every = [1 << i for i in range(count.bit_length() - 1)]
    return [first] + [d for d in every if d != first]


def join(part, far):
    pair = jnp.concatenate([part, far], axis=0)
    return jnp.concatenate([pair, swap(pair, "mem", 1)], axis=0)


class Halving:
    def __init__(self, parts, first):
        count = lax.axis_size("dp")
        self.dims = [count]
        self.kept = [a.reshape(count, a.shape[0] // count, a.shape[1]) for a in parts]
        self.left = bits_of(count, first)
        self.done_bits = []
        self.count = count

    def send(self):
        me = lax.axis_index("dp")
        distance = self.left[0]
        below = sum(1 for d in self.left if d < distance)
        low_size = 1 << below
        bit = (me // distance) % 2
        self.mine, theirs = [], []
        for a in self.kept:
            n, r, w = a.shape
            split = a.reshape(n // (2 * low_size), 2, low_size, r, w)
            self.mine.append(lax.dynamic_index_in_dim(split, bit, 1, False).reshape(n // 2, r, w))
            theirs.append(lax.dynamic_index_in_dim(split, 1 - bit, 1, False).reshape(n // 2, r, w))
        return jnp.concatenate([t.astype(low) for t in theirs], axis=2)

    def move(self, sent):
        return swap(sent, "dp", self.left.pop(0))

    def add(self, got):
        start, self.kept = 0, []
        for a in self.mine:
            self.kept.append(a + got[:, :, start : start + a.shape[2]].astype(jnp.float32))
            start += a.shape[2]

    def step(self):
        self.add(self.move(self.send()))

    def finish(self):
        while self.left:
            self.step()
        return [a[0] for a in self.kept]


def tie(*values):
    return lax.optimization_barrier(values)


def finale_kernel(c_ref, f_ref, e_ref, s_ref, b_ref, g_ref, h_ref, v_ref,
                  oc_ref, of_ref, os_ref, ob_ref, og_ref, ov_ref,
                  by, bz, sz, gc, gs, gx, vs, vc, vx, vy, vz, send, recv):
    dp, mem = lax.axis_index("dp"), lax.axis_index("mem")
    y, row = dp % 2, dp // 2
    groups = b_ref.shape[0]
    f32 = jnp.float32
    wide = b_ref.shape[3] // 2
    tall = h_ref.shape[0] // 2

    def quarter_of(m):
        return 2 * (m % 2) + m // 2

    def block_of(m):
        return (m // 2) + (m % 2) * (3 - 2 * (m // 2))

    barrier = pltpu.get_barrier_semaphore()
    core_peer, chip_peer, y_peer = {"mem": mem ^ 1}, {"mem": mem ^ 2}, {"dp": dp ^ 1}
    row_peers = [{"dp": (row ^ j) * 2 + y} for j in range(1, groups)]
    peers = [core_peer, chip_peer, y_peer] + row_peers
    for peer in peers:
        pl.semaphore_signal(barrier, inc=1, device_id=peer, device_id_type=pl.DeviceIdType.MESH)
    pl.semaphore_wait(barrier, len(peers))

    sent = []

    def start(src, dst, peer):
        n = len(sent)
        copy = pltpu.make_async_remote_copy(
            src_ref=src, dst_ref=dst, send_sem=send.at[n], recv_sem=recv.at[n],
            device_id=peer, device_id_type=pl.DeviceIdType.MESH,
        )
        copy.start()
        sent.append(copy)
        return copy

    def to_rows(source, target, own):
        return [start(source(row ^ j), target(own), row_peers[j - 1]) for j in range(1, groups)]

    def wait_all(copies):
        for copy in copies:
            copy.wait_recv()

    def columns(n):
        return pl.ds(n * wide, wide)

    def lines(n):
        return pl.ds(n * tall, tall)

    mine_q, other_q = quarter_of(mem), quarter_of(mem ^ 2)
    block, other = block_of(mem), block_of(mem ^ 2)

    copy_vy = start(v_ref, vy, y_peer)
    copies_by = [start(b_ref.at[:, 1 - y, :, columns(n)], by.at[:, :, columns(n)], y_peer) for n in range(2)]
    copy_g3 = start(g_ref.at[block_of(mem ^ 3)], gc.at[1], core_peer)
    copy_cx = start(c_ref, oc_ref.at[mine_q], chip_peer)
    copies_sz = to_rows(lambda t: s_ref.at[t], lambda t: sz.at[t], row)
    copy_g1 = start(g_ref.at[block_of(mem ^ 1)], gc.at[0], core_peer)
    copy_cc = start(c_ref, oc_ref.at[mine_q], core_peer)
    copy_f0 = start(f_ref, of_ref.at[mine_q], core_peer)
    copy_f1 = start(e_ref, of_ref.at[other_q], core_peer)
    sz[row] = s_ref[row]

    copy_g3.wait_recv()
    copies_gx = []
    for n in range(2):
        gs[lines(n)] = (g_ref[other, lines(n)].astype(f32) + gc[1, lines(n)].astype(f32)).astype(low)
        copies_gx.append(start(gs.at[lines(n)], gx.at[lines(n)], chip_peer))
    copy_vy.wait_recv()
    vs[0] = v_ref[...] + vy[...]
    vz[row] = vs[0]
    copies_vz = to_rows(lambda t: vs.at[0], lambda t: vz.at[t], row)
    oc_ref[mine_q] = c_ref[...]
    of_ref[mine_q] = f_ref[...]
    of_ref[other_q] = e_ref[...]
    copy_g1.wait_recv()

    copies_bz = []

    def first_half(n):
        copies_by[n].wait_recv()
        for t in range(groups):
            by[t, :, columns(n)] = (
                by[t, :, columns(n)].astype(f32) + b_ref[t, y, :, columns(n)].astype(f32)
            ).astype(low)
        bz[row, :, columns(n)] = by[row, :, columns(n)]
        copies_bz.append(
            to_rows(lambda t: by.at[t, :, columns(n)], lambda t: bz.at[t, :, columns(n)], row)
        )

    def rows_total(n):
        copies_gx[n].wait_recv()
        total = h_ref[lines(n)] + g_ref[block, lines(n)].astype(f32)
        total = total + gc[0, lines(n)].astype(f32) + gx[lines(n)].astype(f32)
        og_ref[block, lines(n)] = total.astype(low)
        piece = og_ref.at[block, lines(n)]
        return [start(piece, piece, chip_peer), start(piece, piece, core_peer)]

    first_half(0)
    wait_all(copies_vz)
    total = vz[0]
    for t in range(1, groups):
        total = total + vz[t]
    vs[1] = total
    copy_vc = start(vs.at[1], vc, core_peer)
    wait_all(copies_sz)
    total = sz[0].astype(f32)
    for t in range(1, groups):
        total = total + sz[t].astype(f32)
    os_ref[mine_q] = total.astype(low)
    piece_s = os_ref.at[mine_q]
    copy_sx, copy_sc = start(piece_s, piece_s, chip_peer), start(piece_s, piece_s, core_peer)
    copies_g0 = rows_total(0)
    copy_vc.wait_recv()
    vs[2] = vs[1] + vc[...]
    copy_vx = start(vs.at[2], vx, chip_peer)
    copy_cx.wait_recv()
    copy_cr = start(oc_ref.at[other_q], oc_ref.at[other_q], core_peer)
    first_half(1)
    copies_g1 = rows_total(1)
    copy_sx.wait_recv()
    copy_sr = start(os_ref.at[other_q], os_ref.at[other_q], core_peer)

    copies_b, relays = [], []
    for n in range(2):
        wait_all(copies_bz[n])
        total = bz[0, :, columns(n)].astype(f32)
        for t in range(1, groups):
            total = total + bz[t, :, columns(n)].astype(f32)
        ob_ref[mine_q, :, columns(n)] = total.astype(low)
        piece = ob_ref.at[mine_q, :, columns(n)]
        copies_b.append([start(piece, piece, chip_peer), start(piece, piece, core_peer)])
        (copies_g0, copies_g1)[n][0].wait_recv()
        piece = og_ref.at[other, lines(n)]
        relays.append(start(piece, piece, core_peer))
    copy_vx.wait_recv()
    ov_ref[...] = vs[2] + vx[...]
    for n in range(2):
        copies_b[n][0].wait_recv()
        piece = ob_ref.at[other_q, :, columns(n)]
        relays.append(start(piece, piece, core_peer))
    wait_all([copy_cc, copy_f0, copy_f1, copy_cr, copy_sc, copy_sr])
    wait_all([copies_g0[1], copies_g1[1], copies_b[0][1], copies_b[1][1]] + relays)
    for copy in sent:
        copy.wait_send()


def finale(c, f, e, s, b, g, h, v):
    groups, _, r, wb = b.shape
    ws = s.shape[2]
    copies = 29 + 4 * (groups - 1)
    vmem = pl.BlockSpec(memory_space=pltpu.VMEM)
    f32 = jnp.float32
    half_rows = pltpu.VMEM(g.shape[1:], low)
    vector = pltpu.VMEM(v.shape, f32)
    return pl.pallas_call(
        finale_kernel,
        out_shape=[jax.ShapeDtypeStruct((4, r, a.shape[-1]), low) for a in (c, f, s, b)]
        + [jax.ShapeDtypeStruct(g.shape, low), jax.ShapeDtypeStruct(v.shape, f32)],
        in_specs=[vmem] * 8,
        out_specs=[vmem] * 6,
        scratch_shapes=[
            pltpu.VMEM((groups, r, wb), low),
            pltpu.VMEM((groups, r, wb), low),
            pltpu.VMEM((groups, r, ws), low),
            pltpu.VMEM((2,) + g.shape[1:], low),
            half_rows,
            half_rows,
            pltpu.VMEM((3,) + v.shape, f32),
            vector,
            vector,
            vector,
            pltpu.VMEM((groups,) + v.shape, f32),
            pltpu.SemaphoreType.DMA((copies,)),
            pltpu.SemaphoreType.DMA((copies,)),
        ],
        compiler_params=pltpu.CompilerParams(
            collective_id=0, has_side_effects=True, vmem_limit_bytes=VMEM_LIMIT
        ),
        cost_estimate=pl.CostEstimate(flops=10**6, bytes_accessed=10**8, transcendentals=0),
        name="finale",
    )(c, f, e, s, b, g, h, v)


def unpack_kernel(c_ref, f_ref, s_ref, b_ref, g_ref, v_ref, qkv_ref, so_ref, cq_ref, ckv_ref, co_ref, fi_ref, fo_ref, gd_ref,
                  pb_ref, ng_ref, ns_ref, fb_ref, *, quarter, piece):
    f32 = jnp.float32

    def spread(source, start, count, size, target):
        for p in range(4):
            for n in range(count):
                target[:, (n * 4 + p) * size : (n * 4 + p + 1) * size] = source[
                    p, :, start + n * size : start + (n + 1) * size
                ].astype(f32)

    spread(b_ref, 0, 3, quarter, qkv_ref)
    spread(c_ref, 0, 1, quarter, co_ref)
    spread(c_ref, quarter, 1, quarter, cq_ref)
    spread(c_ref, 2 * quarter, 2, quarter, ckv_ref)
    spread(s_ref, 0, 1, quarter, so_ref)
    spread(f_ref, 0, quarter * 4 // piece, piece, fi_ref)
    for p in range(4):
        fo_ref[p] = f_ref[p, :, 4 * quarter :].astype(f32)
        gd_ref[p] = g_ref[p].astype(f32)
    at = 0
    for target in (pb_ref, ng_ref, ns_ref, fb_ref):
        target[...] = v_ref[at : at + target.shape[0], :]
        at += target.shape[0]


def unpack(c, f, s, b, g, v, width, hidden, piece):
    r = c.shape[1]
    steps = 4 if r % 64 == 0 else 1
    h, gh = r // steps, g.shape[1] // steps
    f32 = jnp.float32

    def slots(x, n):
        return pl.BlockSpec((4, n, x.shape[2]), lambda i: (0, i, 0))

    wide = [3 * width, width, width, 2 * width, width, hidden]
    counts = [7, 3, 3, hidden // width]
    return pl.pallas_call(
        functools.partial(unpack_kernel, quarter=width // 4, piece=piece),
        out_shape=[jax.ShapeDtypeStruct((r, w), f32) for w in wide]
        + [jax.ShapeDtypeStruct((4, r, width), f32), jax.ShapeDtypeStruct(g.shape, f32)]
        + [jax.ShapeDtypeStruct((n, width), f32) for n in counts],
        grid=(steps,),
        in_specs=[slots(c, h), slots(f, h), slots(s, h), slots(b, h), slots(g, gh), pl.BlockSpec(v.shape, lambda i: (0, 0))],
        out_specs=[pl.BlockSpec((h, w), lambda i: (i, 0)) for w in wide]
        + [pl.BlockSpec((4, h, width), lambda i: (0, i, 0)), slots(g, gh)]
        + [pl.BlockSpec((n, width), lambda i: (0, 0)) for n in counts],
        compiler_params=pltpu.CompilerParams(vmem_limit_bytes=VMEM_LIMIT),
        cost_estimate=pl.CostEstimate(flops=10**6, bytes_accessed=2 * 10**7, transcendentals=0),
        name="unpack",
    )(c, f, s, b, g, v)


def per_device(
    dec_in,
    memory,
    dec_len,
    mem_len,
    grad_out,
    self_qkv,
    self_out,
    cross_q,
    cross_kv,
    cross_out,
    ffn_in,
    ffn_out,
    proj_bias,
    ffn_bias,
    norm_gain,
    norm_shift,
):
    x_full = dec_in[0]
    rows, width = x_full.shape
    hidden = ffn_in.shape[1]
    block = rows // 4
    half, quarter = width // 2, width // 4
    groups = lax.axis_size("dp")
    mem_rows = memory[0]
    mem_block = mem_rows.shape[0]
    me = lax.axis_index("mem")
    chip, core = me // 2, me % 2
    quart = 2 * core + chip

    def block_of(m):
        return jnp.where(m // 2 == 0, 3 * (m % 2), 1 + m % 2)

    def cut(a, start, size, axis=1):
        return lax.dynamic_slice_in_dim(a, start, size, axis)

    def own_rows(a):
        return cut(a, block_of(me) * block, block, 0)

    def by_block(gathered):
        size = gathered.shape[0] // 4
        where = [0, 2, 3, 1]
        pieces = []
        for n in range(4):
            offset = me ^ where[n]
            slot = (offset % 2) * 2 + offset // 2
            pieces.append(cut(gathered, slot * size, size, 0))
        return jnp.concatenate(pieces, axis=0)

    def by_quarter(slots):
        stacked = jnp.stack(slots)
        where = [0, 2, 1, 3]
        out = []
        for n in range(4):
            offset = me ^ where[n]
            out.append(lax.dynamic_index_in_dim(stacked, (offset % 2) * 2 + offset // 2, 0, False))
        return out

    mem_far = swap(mem_rows, "mem", 2)

    side = core * half
    qkv8 = project(core, x_full, self_qkv, proj_bias, (0, None, 1), (0.125, 1.0, 1.0))
    info_f = jnp.stack([chip, dec_len[0]]).astype(jnp.int32)
    att8 = self_forward(info_f, qkv8)
    att8, mem_far = tie(att8, mem_far)
    mem_full = join(mem_rows, mem_far)

    def heads_to_rows(a8):
        mine = cut(a8, core * block, block, 0)
        other = swap(cut(a8, (1 - core) * block, block, 0), "mem", 1)
        return jnp.where(
            core == 0, jnp.concatenate([mine, other], axis=1), jnp.concatenate([other, mine], axis=1)
        )

    attended = heads_to_rows(att8)
    x_own = own_rows(x_full).astype(jnp.float32)
    first, first_norm, first_inv = normalize(
        x_own + product(attended, self_out) + proj_bias[2], norm_gain[0], norm_shift[0]
    )
    first_low = first.astype(low)
    first_other = swap(first_low, "mem", 1)
    first_chip = jnp.where(
        core == 0,
        jnp.concatenate([first_low, first_other], axis=0),
        jnp.concatenate([first_other, first_low], axis=0),
    )

    cq8 = ((product(first_chip, cut(cross_q, side, half)) + cut(proj_bias[3], side, half, 0)) * 0.125).astype(low)
    kvc8 = project(core, mem_full, cross_kv, proj_bias, (None, 4), (1.0, 1.0))
    slot_pos = jnp.stack([(me ^ k) * mem_block for k in ORDER])
    mem_pos = (slot_pos[:, None] + jnp.arange(mem_block, dtype=jnp.int32)[None, :]).reshape(-1)
    mem_bias = jnp.where(mem_pos < mem_len[0], 0.0, neg_fill).astype(jnp.float32)
    crossed = heads_to_rows(cross_forward(cq8, kvc8, mem_bias[None, :]))
    second, second_norm, second_inv = normalize(
        first + product(crossed, cross_out) + proj_bias[5], norm_gain[1], norm_shift[1]
    )
    second_low = second.astype(low)

    second_full = gather_rows(second_low)
    inner = product(second_low, ffn_in) + ffn_bias
    act, act_grad = gelu_parts(inner)
    act, act_grad = act.astype(low), act_grad.astype(low)
    third, third_norm, third_inv = normalize(
        second + product(act, ffn_out) + proj_bias[6], norm_gain[2], norm_shift[2]
    )
    row_pos = block_of(me) * block + jnp.arange(block, dtype=jnp.int32)
    cot = jnp.where((row_pos < dec_len[0])[:, None], own_rows(grad_out[0]).astype(jnp.float32), 0.0)
    dh3, gain_three, shift_three = norm_back(cot, third_norm, third_inv, norm_gain[2])
    dz = dh3.astype(low)
    first_full = gather_rows(first_low)
    dz, late = tie(dz, quart)
    piece = hidden // groups // 4
    if piece % 128 == 0:
        w_in_q = pick_columns(ffn_in, piece, groups, 4, late)
    else:
        w_in_q = lax.dynamic_index_in_dim(ffn_in.reshape(width, groups, 4, piece), late, 2, False)
        w_in_q = w_in_q.reshape(width, hidden // 4)
    w_out_q = lax.dynamic_index_in_dim(ffn_out.reshape(groups, 4, piece, width), late, 1, False)
    w_out_q = w_out_q.reshape(hidden // 4, width)
    dz_far = swap(dz, "mem", 2)
    wide = quart * quarter
    cq4 = ((product(first_full, cut(cross_q, wide, quarter)) + cut(proj_bias[3], wide, quarter, 0)) * 0.125).astype(low)
    du = (product_nt(dz, ffn_out) * act_grad.astype(jnp.float32)).astype(low)
    du, dz_far = tie(du, dz_far)
    dh2, gain_two, shift_two = norm_back(
        dh3 + product_nt(du, ffn_in), second_norm, second_inv, norm_gain[1]
    )
    dco = dh2.astype(low)

    dz_full = join(dz, dz_far)
    dco_far = swap(dco, "mem", 2)
    b_in_q = lax.dynamic_index_in_dim(ffn_bias.reshape(groups, 4, piece), quart, 1, False).reshape(-1)
    act_q, slope_q = gelu_parts(product(second_full, w_in_q) + b_in_q)
    act_q = act_q.astype(low)
    du_q = (product_nt(dz_full, w_out_q) * slope_q).astype(low)
    du_q, dco_far, third_low = tie(du_q, dco_far, third.astype(low))
    dco_full = join(dco, dco_far)
    third_far = swap(third_low, "mem", 2)
    sum_in = Halving([product_tn(second_full, du_q)], 1)
    sum_out = Halving([product_tn(act_q, dz_full)], min(2, groups // 2))
    send_in, send_out = sum_in.send(), sum_out.send()

    dx4 = product_nt(dco_full, cut(cross_out, wide, quarter, 0)).astype(low)
    pair_base = chip * (quarter // 128)
    info_c = jnp.stack([pair_base]).astype(jnp.int32)
    bias_col = jnp.broadcast_to(mem_bias[:, None], (mem_bias.shape[0], 128))
    dx4, send_in, send_out, third_far, crossed_late = tie(dx4, send_in, send_out, third_far, crossed)
    crossed_far = swap(crossed_late, "mem", 2)
    got_in, got_out = sum_in.move(send_in), sum_out.move(send_out)
    dq4, dkc4, dvc4 = attention_back(info_c, cq4, kvc8, dx4, bias_col, False)
    dq4, dkc4, dvc4, got_in, got_out, crossed_far = tie(dq4, dkc4, dvc4, got_in, got_out, crossed_far)

    def over_chips(a):
        b0, b2, b1, b3 = jnp.split(a, 4, axis=0)
        return jnp.concatenate([b2, b3], axis=0), b0, b1

    def to_rows(over, b0, b1):
        size = b0.shape[0]
        mine = jnp.concatenate([b0, over[:size]], axis=0)
        other = swap(jnp.concatenate([b1, over[size:]], axis=0), "mem", 1)
        return by_quarter([mine[:size], mine[size:], other[:size], other[size:]])

    dq_leave, dq_0, dq_1 = over_chips(dq4)
    dq_far = swap(dq_leave, "mem", 2)
    dq_far, dq4, dkc4, dvc4, got_in, got_out = tie(dq_far, dq4, dkc4, dvc4, got_in, got_out)
    sum_in.add(got_in)
    sum_out.add(got_out)
    dkv4 = jnp.concatenate([dkc4, dvc4], axis=1)
    dkv_leave, dkv_0, dkv_1 = over_chips(dkv4)
    send_in, send_out = sum_in.send(), sum_out.send()
    dq_own = jnp.concatenate(to_rows(dq_far, dq_0, dq_1), axis=1)
    got_in, got_out = sum_in.move(send_in), sum_out.move(send_out)
    crossed_full = join(crossed, crossed_far)
    attended_full = gather_rows(attended)
    dh1, gain_one, shift_one = norm_back(
        dh2 + product_nt(dq_own, cross_q), first_norm, first_inv, norm_gain[0]
    )
    do = dh1.astype(low)
    sum_w = Halving(
        [product_tn(crossed_full, cut(dco_full, wide, quarter)), product_tn(first_full, dq4)], 1
    )
    sum_kv = Halving([product_tn(mem_full, dkv4)], min(2, groups // 2))
    got_w, got_kv = sum_w.move(sum_w.send()), sum_kv.move(sum_kv.send())
    do_far = swap(do, "mem", 2)
    do_far, got_in, got_out, got_w = tie(do_far, got_in, got_out, got_w)
    do_full, got_kv = tie(join(do, do_far), got_kv)
    sum_in.add(got_in)
    sum_out.add(got_out)
    sum_in.kept = sum_in.kept + sum_out.kept
    sum_w.add(got_w)
    sum_kv.add(got_kv)
    sum_so = Halving([product_tn(attended_full, cut(do_full, wide, quarter))], 1)

    da4 = product_nt(do_full, cut(self_out, wide, quarter, 0)).astype(low)
    where = [0, 2, 3, 1]
    slots = [((me ^ n) % 2) * 2 + (me ^ n) // 2 for n in where]
    info_s = jnp.stack([pair_base, dec_len[0]] + slots).astype(jnp.int32)
    send_in, send_w, send_kv, send_so = sum_in.send(), sum_w.send(), sum_kv.send(), sum_so.send()
    da4, send_in, send_w, send_kv, send_so, dkv_leave = tie(da4, send_in, send_w, send_kv, send_so, dkv_leave)
    got_in, got_w, got_kv = sum_in.move(send_in), sum_w.move(send_w), sum_kv.move(send_kv)
    got_so = sum_so.move(send_so)
    dkv_far = swap(dkv_leave, "mem", 2)
    sq4, sk4, sv4 = attention_back(info_s, qkv8, qkv8, da4, bias_col[:8], True)
    sq4, sk4, sv4, got_in, got_w, got_kv, got_so, dkv_far = tie(
        sq4, sk4, sv4, got_in, got_w, got_kv, got_so, dkv_far
    )
    sum_in.add(got_in)
    ffn_grad = jnp.concatenate([part.astype(low) for part in sum_in.finish()], axis=1)
    sum_w.add(got_w)
    sum_kv.add(got_kv)
    sum_so.add(got_so)
    sum_w.kept = sum_w.kept + sum_kv.kept
    send_w = sum_w.send()
    sq4, sk4, sv4, send_w, ffn_grad = tie(sq4, sk4, sv4, send_w, ffn_grad)
    ffn_far = swap(ffn_grad, "mem", 2)
    got_w = sum_w.move(send_w)
    dkv_parts = to_rows(dkv_far, dkv_0, dkv_1)
    dkv_own = jnp.concatenate(
        [a[:, :quarter] for a in dkv_parts] + [a[:, quarter:] for a in dkv_parts], axis=1
    )
    grad_memory = product_nt(dkv_own, cross_kv)[None]

    per = width // groups
    qkv_grad, partial, own_sums = self_weights(quart, x_full, sq4, sk4, sv4, self_qkv)
    qkv_grad = qkv_grad.reshape(groups // 2, 2, per, 3 * quarter)
    partial = partial.reshape(4, block, width)
    qkv_grad, got_w, ffn_far, grad_memory = tie(qkv_grad, got_w, ffn_far, grad_memory)
    sum_w.add(got_w)
    cross_grad = jnp.concatenate([part.astype(low) for part in sum_w.finish()], axis=1)
    so_grad = sum_so.kept[0].astype(low)
    layer_out = by_block(join(third_low, third_far))[None]

    place = jnp.zeros((2, width), jnp.float32)
    own_sums = own_sums[:2]
    place = lax.dynamic_update_slice(place, own_sums, (0, quart * quarter))
    packed = jnp.concatenate(
        [
            place,
            jnp.stack(
                [
                    column_sum(do),
                    column_sum(dq_own),
                    column_sum(dkv_own[:, width:]),
                    column_sum(dco),
                    column_sum(dz),
                    gain_one,
                    gain_two,
                    gain_three,
                    shift_one,
                    shift_two,
                    shift_three,
                ]
            ),
            column_sum(du).reshape(hidden // width, width),
        ],
        axis=0,
    )
    packed = jnp.pad(packed, ((0, -packed.shape[0] % 8), (0, 0)))
    cross_w, ffn_w, so_w, qkv_w, grad_rows, packed = finale(
        cross_grad, ffn_grad, ffn_far, so_grad, qkv_grad, partial, dh1, packed
    )
    w_qkv, w_so, w_cq, w_ckv, w_co, w_fi, w_fo, grad_dec, p_bias, n_gain, n_shift, f_bias = unpack(
        cross_w, ffn_w, so_w, qkv_w, grad_rows, packed, width, hidden, piece
    )
    return (
        layer_out,
        grad_dec.reshape(1, rows, width),
        grad_memory,
        w_qkv,
        w_so,
        w_cq,
        w_ckv,
        w_co,
        w_fi,
        w_fo.reshape(-1, width),
        p_bias,
        f_bias.reshape(hidden),
        n_gain,
        n_shift,
    )


def solution(mesh):
    in_specs = (
        P("dp", None, None),
        P("dp", "mem", None),
        P("dp"),
        P("dp"),
        P("dp", None, None),
    ) + (P(),) * 11
    out_specs = (
        P("dp", None, None),
        P("dp", None, None),
        P("dp", "mem", None),
    ) + (P("dp", None),) * 7 + (P(),) * 4
    return jax.shard_map(
        per_device, mesh=mesh, in_specs=in_specs, out_specs=out_specs, check_vma=False
    )
```

```python
import functools

import jax
import jax.numpy as jnp
from jax import lax
from jax.experimental import pallas as pl
from jax.experimental.pallas import tpu as pltpu
from jax.sharding import PartitionSpec as P

HEAD_DIM = 64
norm_eps = 1e-05
neg_fill = -1e30
low = jnp.bfloat16
VMEM_LIMIT = 56 * 1024 * 1024


def product(left_rows, right_rows):
    return jnp.dot(left_rows, right_rows, preferred_element_type=jnp.float32)


def product_tn(left_rows, right_rows):
    return lax.dot_general(
        left_rows, right_rows, (((0,), (0,)), ((), ())), preferred_element_type=jnp.float32
    )


def product_nt(left_rows, right_rows):
    return lax.dot_general(
        left_rows, right_rows, (((1,), (1,)), ((), ())), preferred_element_type=jnp.float32
    )


def normalize(hidden, scale_row, shift_row):
    row_mean = jnp.mean(hidden, axis=-1, keepdims=True)
    centered = hidden - row_mean
    variance = jnp.mean(centered * centered, axis=-1, keepdims=True)
    inverse = lax.rsqrt(variance + norm_eps)
    normed = centered * inverse
    return (normed * scale_row + shift_row, normed, inverse)


def norm_back(grad_rows, normed, inverse, scale_row):
    scaled = grad_rows * scale_row
    grad_hidden = inverse * (
        scaled
        - jnp.mean(scaled, axis=-1, keepdims=True)
        - normed * jnp.mean(scaled * normed, axis=-1, keepdims=True)
    )
    return (grad_hidden, jnp.sum(grad_rows * normed, axis=0), jnp.sum(grad_rows, axis=0))


def gelu_parts(values):
    cdf = 0.5 * (1.0 + lax.erf(values * 0.7071067811865476))
    density = jnp.exp(-0.5 * values * values) * 0.3989422804014327
    return values * cdf, cdf + values * density


def column_sum(matrix):
    return jnp.sum(matrix.astype(jnp.float32), axis=0)


def lane_head(rows):
    return lax.broadcasted_iota(jnp.int32, (rows, 128), 1) // HEAD_DIM


def pick_head(pair, h):
    return jnp.where(lane_head(pair.shape[0]) == h, pair, jnp.zeros_like(pair))


def project_kernel(info, x_ref, w_ref, bias_ref, o_ref, *, bias_rows, scales):
    total = product(x_ref[...], w_ref[...])
    for n, (bias_row, scale) in enumerate(zip(bias_rows, scales)):

        @pl.when(pl.program_id(0) == n)
        def _():
            out = total
            if bias_row is not None:
                out = out + bias_ref[bias_row : bias_row + 1, :]
            if scale != 1.0:
                out = out * scale
            o_ref[...] = out.astype(low)


def project(core, x, weight, bias, bias_rows, scales):
    rows, width = x.shape
    half = width // 2
    size = 256
    count = half // size
    parts = len(scales)
    return pl.pallas_call(
        functools.partial(project_kernel, bias_rows=bias_rows, scales=scales),
        out_shape=jax.ShapeDtypeStruct((rows, parts * half), low),
        grid_spec=pltpu.PrefetchScalarGridSpec(
            num_scalar_prefetch=1,
            grid=(parts, count),
            in_specs=[
                pl.BlockSpec((rows, width), lambda p, j, s: (0, 0)),
                pl.BlockSpec((width, size), lambda p, j, s: (0, p * 2 * count + s[0] * count + j)),
                pl.BlockSpec((bias.shape[0], size), lambda p, j, s: (0, s[0] * count + j)),
            ],
            out_specs=pl.BlockSpec((rows, size), lambda p, j, s: (0, p * count + j)),
        ),
        compiler_params=pltpu.CompilerParams(vmem_limit_bytes=VMEM_LIMIT),
        cost_estimate=pl.CostEstimate(
            flops=2 * rows * width * half * parts, bytes_accessed=2 * rows * width * (1 + parts), transcendentals=0
        ),
        name="project",
    )(core.astype(jnp.int32).reshape(1), x, weight, bias)


def self_fwd_kernel(info, q_ref, k_ref, v_ref, o_ref):
    rows = k_ref.shape[0]
    block = rows // 4
    dec_len = info[1]

    def process(qb, slot):
        keys = (qb + 1) * block
        kk, vv = k_ref[:keys, :], v_ref[:keys, :]
        qq = q_ref[qb * block : (qb + 1) * block, :]
        total = None
        for h in range(2):
            s = product_nt(pick_head(qq, h), kk)
            col = lax.broadcasted_iota(jnp.int32, s.shape, 1)
            row = lax.broadcasted_iota(jnp.int32, s.shape, 0) + qb * block
            s = jnp.where((col <= row) & (col < dec_len), s, neg_fill)
            p = jnp.exp(s - jnp.max(s, axis=1, keepdims=True))
            inv = 1.0 / jnp.sum(p, axis=1, keepdims=True)
            part = product(p.astype(low), pick_head(vv, h)) * inv
            total = part if total is None else total + part
        o_ref[slot * block : (slot + 1) * block, :] = total.astype(low)

    @pl.when(info[0] == 0)
    def _():
        process(0, 0)
        process(3, 1)

    @pl.when(info[0] == 1)
    def _():
        process(1, 0)
        process(2, 1)


def self_forward(info, qkv):
    rows, width = qkv.shape[0], qkv.shape[1] // 3
    pairs = width // 128

    def spec(n):
        return pl.BlockSpec((rows, 128), lambda i, s: (0, n * pairs + i))

    return pl.pallas_call(
        self_fwd_kernel,
        out_shape=jax.ShapeDtypeStruct((rows // 2, width), low),
        grid_spec=pltpu.PrefetchScalarGridSpec(
            num_scalar_prefetch=1,
            grid=(pairs,),
            in_specs=[spec(0), spec(1), spec(2)],
            out_specs=pl.BlockSpec((rows // 2, 128), lambda i, s: (0, i)),
        ),
        compiler_params=pltpu.CompilerParams(vmem_limit_bytes=VMEM_LIMIT),
        cost_estimate=pl.CostEstimate(
            flops=6 * rows * rows * width, bytes_accessed=8 * rows * width, transcendentals=rows * rows * 3
        ),
        name="self_forward",
    )(info, qkv, qkv, qkv)


def cross_fwd_kernel(q_ref, k_ref, v_ref, bias_ref, o_ref):
    block = 256
    for r in range(q_ref.shape[0] // block):
        qq = q_ref[r * block : (r + 1) * block, :]
        total = None
        for h in range(2):
            s = product_nt(pick_head(qq, h), k_ref[...]) + bias_ref[...]
            p = jnp.exp(s - jnp.max(s, axis=1, keepdims=True))
            inv = 1.0 / jnp.sum(p, axis=1, keepdims=True)
            part = product(p.astype(low), pick_head(v_ref[...], h)) * inv
            total = part if total is None else total + part
        o_ref[r * block : (r + 1) * block, :] = total.astype(low)


def cross_forward(q, kv, bias_row):
    rows, width = q.shape
    keys = kv.shape[0]
    return pl.pallas_call(
        cross_fwd_kernel,
        out_shape=jax.ShapeDtypeStruct((rows, width), low),
        grid=(width // 128,),
        in_specs=[
            pl.BlockSpec((rows, 128), lambda i: (0, i)),
            pl.BlockSpec((keys, 128), lambda i: (0, i)),
            pl.BlockSpec((keys, 128), lambda i: (0, width // 128 + i)),
            pl.BlockSpec((1, keys), lambda i: (0, 0)),
        ],
        out_specs=pl.BlockSpec((rows, 128), lambda i: (0, i)),
        compiler_params=pltpu.CompilerParams(vmem_limit_bytes=VMEM_LIMIT),
        cost_estimate=pl.CostEstimate(
            flops=16 * rows * keys * width, bytes_accessed=8 * rows * width, transcendentals=rows * keys * 8
        ),
        name="cross_forward",
    )(q, kv, kv, bias_row)


def back_kernel(info, q_ref, k_ref, v_ref, g0_ref, g1_ref, g2_ref, g3_ref, bias_ref, dq_ref, dk_ref, dv_ref, dk_acc, dv_acc, *, causal):
    rows = q_ref.shape[0]
    keys_all = k_ref.shape[0]
    block = rows // 4
    k_t = k_ref[...].T
    dk_acc[...] = jnp.zeros_like(dk_acc)
    dv_acc[...] = jnp.zeros_like(dv_acc)
    for qb in range(4):
        keys = (qb + 1) * block if causal else keys_all
        kk, vv = k_ref[:keys, :], v_ref[:keys, :]
        qq = q_ref[qb * block : (qb + 1) * block, :]
        gg = (g0_ref, g1_ref, g2_ref, g3_ref)[qb][...]
        q_parts = []
        for h in range(2):
            q_h, g_h = pick_head(qq, h), pick_head(gg, h)
            s = product_nt(kk, q_h)
            if causal:
                key = lax.broadcasted_iota(jnp.int32, s.shape, 0)
                row = lax.broadcasted_iota(jnp.int32, s.shape, 1) + qb * block
                s = jnp.where((key <= row) & (key < info[1]), s, neg_fill)
            else:
                s = s + jnp.concatenate([bias_ref[...]] * (block // 128), axis=1)
            p = jnp.exp(s - jnp.max(s, axis=0, keepdims=True))
            p = p * (1.0 / jnp.sum(p, axis=0, keepdims=True))
            dp = product_nt(vv, g_h)
            e = jnp.sum(p * dp, axis=0, keepdims=True)
            ds = (p * (dp - e)).astype(low)
            dv_acc[:keys, :] += product(p.astype(low), g_h)
            dk_acc[:keys, :] += product(ds, q_h)
            q_parts.append(product(k_t[h * HEAD_DIM : (h + 1) * HEAD_DIM, :keys], ds))
        dq_t = jnp.concatenate(q_parts, axis=0) * 0.125
        dq_ref[qb * block : (qb + 1) * block, :] = dq_t.T.astype(low)
    dk_ref[...] = dk_acc[...].astype(low)
    dv_ref[...] = dv_acc[...].astype(low)


def attention_back(info, q, kv, g, bias, causal):
    rows = q.shape[0]
    keys = kv.shape[0]
    own = pl.BlockSpec((rows, 128), lambda i, s: (0, i))
    pairs = g.shape[1] // 64

    def wide(n):
        return pl.BlockSpec((keys, 128), lambda i, s: (0, n * pairs + s[0] + i))

    mine = pl.BlockSpec((keys, 128), lambda i, s: (0, i))

    def g_block(n):
        return pl.BlockSpec((rows // 4, 128), lambda i, s: (s[2 + n] if causal else n, i))

    first = 1 if causal else 0
    q_spec = wide(0) if causal else own
    width = g.shape[1]
    return pl.pallas_call(
        functools.partial(back_kernel, causal=causal),
        out_shape=[
            jax.ShapeDtypeStruct((rows, width), low),
            jax.ShapeDtypeStruct((keys, width), low),
            jax.ShapeDtypeStruct((keys, width), low),
        ],
        grid_spec=pltpu.PrefetchScalarGridSpec(
            num_scalar_prefetch=1,
            grid=(width // 128,),
            in_specs=[q_spec, wide(first), wide(first + 1)] + [g_block(n) for n in range(4)] + [pl.BlockSpec(bias.shape, lambda i, s: (0, 0))],
            out_specs=[own, mine, mine],
            scratch_shapes=[pltpu.VMEM((keys, 128), jnp.float32), pltpu.VMEM((keys, 128), jnp.float32)],
        ),
        compiler_params=pltpu.CompilerParams(vmem_limit_bytes=VMEM_LIMIT),
        cost_estimate=pl.CostEstimate(
            flops=40 * rows * keys * width // (2 if causal else 1),
            bytes_accessed=14 * rows * width,
            transcendentals=rows * keys * 4,
        ),
        name="self_back" if causal else "cross_back",
    )(info, q, kv, kv, g, g, g, g, bias)


def self_weights_kernel(info, x_ref, q_ref, k_ref, v_ref, wq_ref, wk_ref, wv_ref, grad_ref, part_ref, sums_ref):
    block = part_ref.shape[0]
    size = q_ref.shape[1]
    at = pl.ds(pl.multiple_of(pl.program_id(0) * block, block), block)
    total = None
    for n, (d_ref, w_ref) in enumerate(((q_ref, wq_ref), (k_ref, wk_ref), (v_ref, wv_ref))):
        grad_ref[:, n * size : (n + 1) * size] = product_tn(x_ref[...], d_ref[...]).astype(low)
        part = product_nt(d_ref[at, :], w_ref[...])
        total = part if total is None else total + part
    part_ref[...] = total.astype(low)

    @pl.when(pl.program_id(0) == 0)
    def _():
        sums_ref[...] = jnp.zeros_like(sums_ref)
        sums_ref[0:1, :] = jnp.sum(q_ref[...].astype(jnp.float32), axis=0, keepdims=True)
        sums_ref[1:2, :] = jnp.sum(v_ref[...].astype(jnp.float32), axis=0, keepdims=True)


def self_weights(quart, x, dq, dk, dv, weight):
    rows, width = x.shape
    size = dq.shape[1]
    block = 256
    whole = pl.BlockSpec((rows, size), lambda i, s: (0, 0))

    def slab(n):
        return pl.BlockSpec((width, size), lambda i, s: (0, n * (width // size) + s[0]))

    return pl.pallas_call(
        self_weights_kernel,
        out_shape=[
            jax.ShapeDtypeStruct((width, 3 * size), low),
            jax.ShapeDtypeStruct((rows, width), low),
            jax.ShapeDtypeStruct((8, size), jnp.float32),
        ],
        grid_spec=pltpu.PrefetchScalarGridSpec(
            num_scalar_prefetch=1,
            grid=(rows // block,),
            in_specs=[pl.BlockSpec((rows, block), lambda i, s: (0, i)), whole, whole, whole, slab(0), slab(1), slab(2)],
            out_specs=[
                pl.BlockSpec((block, 3 * size), lambda i, s: (i, 0)),
                pl.BlockSpec((block, width), lambda i, s: (i, 0)),
                pl.BlockSpec((8, size), lambda i, s: (0, 0)),
            ],
        ),
        compiler_params=pltpu.CompilerParams(vmem_limit_bytes=VMEM_LIMIT),
        cost_estimate=pl.CostEstimate(
            flops=12 * rows * width * size, bytes_accessed=20 * rows * width, transcendentals=0
        ),
        name="self_weights",
    )(quart.astype(jnp.int32).reshape(1), x, dq, dk, dv, weight, weight, weight)


def pick_kernel(info, in_ref, out_ref):
    out_ref[...] = in_ref[...]


def pick_columns(matrix, size, count, stride, offset):
    rows = matrix.shape[0]
    return pl.pallas_call(
        pick_kernel,
        out_shape=jax.ShapeDtypeStruct((rows, size * count), matrix.dtype),
        grid_spec=pltpu.PrefetchScalarGridSpec(
            num_scalar_prefetch=1,
            grid=(count,),
            in_specs=[pl.BlockSpec((rows, size), lambda n, s: (0, n * stride + s[0]))],
            out_specs=pl.BlockSpec((rows, size), lambda n, s: (0, n)),
        ),
        cost_estimate=pl.CostEstimate(flops=0, bytes_accessed=4 * rows * size * count, transcendentals=0),
        name="pick_columns",
    )(offset.astype(jnp.int32).reshape(1), matrix)


def swap(part, axis, distance):
    count = lax.axis_size(axis)
    return lax.ppermute(part, axis, [(i, i ^ distance) for i in range(count)])


ORDER = (0, 2, 1, 3)


def gather_rows(part):
    pair = jnp.concatenate([part, swap(part, "mem", 2)], axis=0)
    return jnp.concatenate([pair, swap(pair, "mem", 1)], axis=0)


def bits_of(count, first):
    every = [1 << i for i in range(count.bit_length() - 1)]
    return [first] + [d for d in every if d != first]


def join(part, far):
    pair = jnp.concatenate([part, far], axis=0)
    return jnp.concatenate([pair, swap(pair, "mem", 1)], axis=0)


class Halving:
    def __init__(self, parts, first):
        count = lax.axis_size("dp")
        self.dims = [count]
        self.kept = [a.reshape(count, a.shape[0] // count, a.shape[1]) for a in parts]
        self.left = bits_of(count, first)
        self.done_bits = []
        self.count = count

    def send(self):
        me = lax.axis_index("dp")
        distance = self.left[0]
        below = sum(1 for d in self.left if d < distance)
        low_size = 1 << below
        bit = (me // distance) % 2
        self.mine, theirs = [], []
        for a in self.kept:
            n, r, w = a.shape
            split = a.reshape(n // (2 * low_size), 2, low_size, r, w)
            self.mine.append(lax.dynamic_index_in_dim(split, bit, 1, False).reshape(n // 2, r, w))
            theirs.append(lax.dynamic_index_in_dim(split, 1 - bit, 1, False).reshape(n // 2, r, w))
        return jnp.concatenate([t.astype(low) for t in theirs], axis=2)

    def move(self, sent):
        return swap(sent, "dp", self.left.pop(0))

    def add(self, got):
        start, self.kept = 0, []
        for a in self.mine:
            self.kept.append(a + got[:, :, start : start + a.shape[2]].astype(jnp.float32))
            start += a.shape[2]

    def step(self):
        self.add(self.move(self.send()))

    def finish(self):
        while self.left:
            self.step()
        return [a[0] for a in self.kept]


def tie(*values):
    return lax.optimization_barrier(values)


def finale_kernel(c_ref, f_ref, e_ref, s_ref, b_ref, g_ref, h_ref, v_ref,
                  oc_ref, of_ref, os_ref, ob_ref, og_ref, ov_ref,
                  by, bz, sz, gc, gs, gx, vs, vc, vx, vy, vz, send, recv):
    dp, mem = lax.axis_index("dp"), lax.axis_index("mem")
    y, row = dp % 2, dp // 2
    groups = b_ref.shape[0]
    f32 = jnp.float32
    wide = b_ref.shape[3] // 2
    tall = h_ref.shape[0] // 2

    def quarter_of(m):
        return 2 * (m % 2) + m // 2

    def block_of(m):
        return (m // 2) + (m % 2) * (3 - 2 * (m // 2))

    barrier = pltpu.get_barrier_semaphore()
    core_peer, chip_peer, y_peer = {"mem": mem ^ 1}, {"mem": mem ^ 2}, {"dp": dp ^ 1}
    row_peers = [{"dp": (row ^ j) * 2 + y} for j in range(1, groups)]
    peers = [core_peer, chip_peer, y_peer] + row_peers
    for peer in peers:
        pl.semaphore_signal(barrier, inc=1, device_id=peer, device_id_type=pl.DeviceIdType.MESH)
    pl.semaphore_wait(barrier, len(peers))

    sent = []

    def start(src, dst, peer):
        n = len(sent)
        copy = pltpu.make_async_remote_copy(
            src_ref=src, dst_ref=dst, send_sem=send.at[n], recv_sem=recv.at[n],
            device_id=peer, device_id_type=pl.DeviceIdType.MESH,
        )
        copy.start()
        sent.append(copy)
        return copy

    def to_rows(source, target, own):
        return [start(source(row ^ j), target(own), row_peers[j - 1]) for j in range(1, groups)]

    def wait_all(copies):
        for copy in copies:
            copy.wait_recv()

    def columns(n):
        return pl.ds(n * wide, wide)

    def lines(n):
        return pl.ds(n * tall, tall)

    mine_q, other_q = quarter_of(mem), quarter_of(mem ^ 2)
    block, other = block_of(mem), block_of(mem ^ 2)

    copy_vy = start(v_ref, vy, y_peer)
    copies_by = [start(b_ref.at[:, 1 - y, :, columns(n)], by.at[:, :, columns(n)], y_peer) for n in range(2)]
    copy_g3 = start(g_ref.at[block_of(mem ^ 3)], gc.at[1], core_peer)
    copy_cx = start(c_ref, oc_ref.at[mine_q], chip_peer)
    copies_sz = to_rows(lambda t: s_ref.at[t], lambda t: sz.at[t], row)
    copy_g1 = start(g_ref.at[block_of(mem ^ 1)], gc.at[0], core_peer)
    copy_cc = start(c_ref, oc_ref.at[mine_q], core_peer)
    copy_f0 = start(f_ref, of_ref.at[mine_q], core_peer)
    copy_f1 = start(e_ref, of_ref.at[other_q], core_peer)
    sz[row] = s_ref[row]

    copy_g3.wait_recv()
    copies_gx = []
    for n in range(2):
        gs[lines(n)] = (g_ref[other, lines(n)].astype(f32) + gc[1, lines(n)].astype(f32)).astype(low)
        copies_gx.append(start(gs.at[lines(n)], gx.at[lines(n)], chip_peer))
    copy_vy.wait_recv()
    vs[0] = v_ref[...] + vy[...]
    vz[row] = vs[0]
    copies_vz = to_rows(lambda t: vs.at[0], lambda t: vz.at[t], row)
    oc_ref[mine_q] = c_ref[...]
    of_ref[mine_q] = f_ref[...]
    of_ref[other_q] = e_ref[...]
    copy_g1.wait_recv()

    copies_bz = []

    def first_half(n):
        copies_by[n].wait_recv()
        for t in range(groups):
            by[t, :, columns(n)] = (
                by[t, :, columns(n)].astype(f32) + b_ref[t, y, :, columns(n)].astype(f32)
            ).astype(low)
        bz[row, :, columns(n)] = by[row, :, columns(n)]
        copies_bz.append(
            to_rows(lambda t: by.at[t, :, columns(n)], lambda t: bz.at[t, :, columns(n)], row)
        )

    def rows_total(n):
        copies_gx[n].wait_recv()
        total = h_ref[lines(n)] + g_ref[block, lines(n)].astype(f32)
        total = total + gc[0, lines(n)].astype(f32) + gx[lines(n)].astype(f32)
        og_ref[block, lines(n)] = total.astype(low)
        piece = og_ref.at[block, lines(n)]
        return [start(piece, piece, chip_peer), start(piece, piece, core_peer)]

    first_half(0)
    wait_all(copies_vz)
    total = vz[0]
    for t in range(1, groups):
        total = total + vz[t]
    vs[1] = total
    copy_vc = start(vs.at[1], vc, core_peer)
    wait_all(copies_sz)
    total = sz[0].astype(f32)
    for t in range(1, groups):
        total = total + sz[t].astype(f32)
    os_ref[mine_q] = total.astype(low)
    piece_s = os_ref.at[mine_q]
    copy_sx, copy_sc = start(piece_s, piece_s, chip_peer), start(piece_s, piece_s, core_peer)
    copies_g0 = rows_total(0)
    copy_vc.wait_recv()
    vs[2] = vs[1] + vc[...]
    copy_vx = start(vs.at[2], vx, chip_peer)
    copy_cx.wait_recv()
    copy_cr = start(oc_ref.at[other_q], oc_ref.at[other_q], core_peer)
    first_half(1)
    copies_g1 = rows_total(1)
    copy_sx.wait_recv()
    copy_sr = start(os_ref.at[other_q], os_ref.at[other_q], core_peer)

    copies_b, relays = [], []
    for n in range(2):
        wait_all(copies_bz[n])
        total = bz[0, :, columns(n)].astype(f32)
        for t in range(1, groups):
            total = total + bz[t, :, columns(n)].astype(f32)
        ob_ref[mine_q, :, columns(n)] = total.astype(low)
        piece = ob_ref.at[mine_q, :, columns(n)]
        copies_b.append([start(piece, piece, chip_peer), start(piece, piece, core_peer)])
        (copies_g0, copies_g1)[n][0].wait_recv()
        piece = og_ref.at[other, lines(n)]
        relays.append(start(piece, piece, core_peer))
    copy_vx.wait_recv()
    ov_ref[...] = vs[2] + vx[...]
    for n in range(2):
        copies_b[n][0].wait_recv()
        piece = ob_ref.at[other_q, :, columns(n)]
        relays.append(start(piece, piece, core_peer))
    wait_all([copy_cc, copy_f0, copy_f1, copy_cr, copy_sc, copy_sr])
    wait_all([copies_g0[1], copies_g1[1], copies_b[0][1], copies_b[1][1]] + relays)
    for copy in sent:
        copy.wait_send()


def finale(c, f, e, s, b, g, h, v):
    groups, _, r, wb = b.shape
    ws = s.shape[2]
    copies = 29 + 4 * (groups - 1)
    vmem = pl.BlockSpec(memory_space=pltpu.VMEM)
    f32 = jnp.float32
    half_rows = pltpu.VMEM(g.shape[1:], low)
    vector = pltpu.VMEM(v.shape, f32)
    return pl.pallas_call(
        finale_kernel,
        out_shape=[jax.ShapeDtypeStruct((4, r, a.shape[-1]), low) for a in (c, f, s, b)]
        + [jax.ShapeDtypeStruct(g.shape, low), jax.ShapeDtypeStruct(v.shape, f32)],
        in_specs=[vmem] * 8,
        out_specs=[vmem] * 6,
        scratch_shapes=[
            pltpu.VMEM((groups, r, wb), low),
            pltpu.VMEM((groups, r, wb), low),
            pltpu.VMEM((groups, r, ws), low),
            pltpu.VMEM((2,) + g.shape[1:], low),
            half_rows,
            half_rows,
            pltpu.VMEM((3,) + v.shape, f32),
            vector,
            vector,
            vector,
            pltpu.VMEM((groups,) + v.shape, f32),
            pltpu.SemaphoreType.DMA((copies,)),
            pltpu.SemaphoreType.DMA((copies,)),
        ],
        compiler_params=pltpu.CompilerParams(
            collective_id=0, has_side_effects=True, vmem_limit_bytes=VMEM_LIMIT
        ),
        cost_estimate=pl.CostEstimate(flops=10**6, bytes_accessed=10**8, transcendentals=0),
        name="finale",
    )(c, f, e, s, b, g, h, v)


def unpack_kernel(c_ref, f_ref, s_ref, b_ref, g_ref, v_ref, qkv_ref, so_ref, cq_ref, ckv_ref, co_ref, fi_ref, fo_ref, gd_ref,
                  pb_ref, ng_ref, ns_ref, fb_ref, *, quarter, piece):
    f32 = jnp.float32

    def spread(source, start, count, size, target):
        for p in range(4):
            for n in range(count):
                target[:, (n * 4 + p) * size : (n * 4 + p + 1) * size] = source[
                    p, :, start + n * size : start + (n + 1) * size
                ].astype(f32)

    spread(b_ref, 0, 3, quarter, qkv_ref)
    spread(c_ref, 0, 1, quarter, co_ref)
    spread(c_ref, quarter, 1, quarter, cq_ref)
    spread(c_ref, 2 * quarter, 2, quarter, ckv_ref)
    spread(s_ref, 0, 1, quarter, so_ref)
    spread(f_ref, 0, quarter * 4 // piece, piece, fi_ref)
    for p in range(4):
        fo_ref[p] = f_ref[p, :, 4 * quarter :].astype(f32)
        gd_ref[p] = g_ref[p].astype(f32)
    at = 0
    for target in (pb_ref, ng_ref, ns_ref, fb_ref):
        target[...] = v_ref[at : at + target.shape[0], :]
        at += target.shape[0]


def unpack(c, f, s, b, g, v, width, hidden, piece):
    r = c.shape[1]
    steps = 4 if r % 64 == 0 else 1
    h, gh = r // steps, g.shape[1] // steps
    f32 = jnp.float32

    def slots(x, n):
        return pl.BlockSpec((4, n, x.shape[2]), lambda i: (0, i, 0))

    wide = [3 * width, width, width, 2 * width, width, hidden]
    counts = [7, 3, 3, hidden // width]
    return pl.pallas_call(
        functools.partial(unpack_kernel, quarter=width // 4, piece=piece),
        out_shape=[jax.ShapeDtypeStruct((r, w), f32) for w in wide]
        + [jax.ShapeDtypeStruct((4, r, width), f32), jax.ShapeDtypeStruct(g.shape, f32)]
        + [jax.ShapeDtypeStruct((n, width), f32) for n in counts],
        grid=(steps,),
        in_specs=[slots(c, h), slots(f, h), slots(s, h), slots(b, h), slots(g, gh), pl.BlockSpec(v.shape, lambda i: (0, 0))],
        out_specs=[pl.BlockSpec((h, w), lambda i: (i, 0)) for w in wide]
        + [pl.BlockSpec((4, h, width), lambda i: (0, i, 0)), slots(g, gh)]
        + [pl.BlockSpec((n, width), lambda i: (0, 0)) for n in counts],
        compiler_params=pltpu.CompilerParams(vmem_limit_bytes=VMEM_LIMIT),
        cost_estimate=pl.CostEstimate(flops=10**6, bytes_accessed=2 * 10**7, transcendentals=0),
        name="unpack",
    )(c, f, s, b, g, v)


def per_device(
    dec_in,
    memory,
    dec_len,
    mem_len,
    grad_out,
    self_qkv,
    self_out,
    cross_q,
    cross_kv,
    cross_out,
    ffn_in,
    ffn_out,
    proj_bias,
    ffn_bias,
    norm_gain,
    norm_shift,
):
    x_full = dec_in[0]
    rows, width = x_full.shape
    hidden = ffn_in.shape[1]
    block = rows // 4
    half, quarter = width // 2, width // 4
    groups = lax.axis_size("dp")
    mem_rows = memory[0]
    mem_block = mem_rows.shape[0]
    me = lax.axis_index("mem")
    chip, core = me // 2, me % 2
    quart = 2 * core + chip

    def block_of(m):
        return jnp.where(m // 2 == 0, 3 * (m % 2), 1 + m % 2)

    def cut(a, start, size, axis=1):
        return lax.dynamic_slice_in_dim(a, start, size, axis)

    def own_rows(a):
        return cut(a, block_of(me) * block, block, 0)

    def by_block(gathered):
        size = gathered.shape[0] // 4
        where = [0, 2, 3, 1]
        pieces = []
        for n in range(4):
            offset = me ^ where[n]
            slot = (offset % 2) * 2 + offset // 2
            pieces.append(cut(gathered, slot * size, size, 0))
        return jnp.concatenate(pieces, axis=0)

    def by_quarter(slots):
        stacked = jnp.stack(slots)
        where = [0, 2, 1, 3]
        out = []
        for n in range(4):
            offset = me ^ where[n]
            out.append(lax.dynamic_index_in_dim(stacked, (offset % 2) * 2 + offset // 2, 0, False))
        return out

    mem_far = swap(mem_rows, "mem", 2)

    side = core * half
    qkv8 = project(core, x_full, self_qkv, proj_bias, (0, None, 1), (0.125, 1.0, 1.0))
    info_f = jnp.stack([chip, dec_len[0]]).astype(jnp.int32)
    att8 = self_forward(info_f, qkv8)
    att8, mem_far = tie(att8, mem_far)
    mem_full = join(mem_rows, mem_far)

    def heads_to_rows(a8):
        mine = cut(a8, core * block, block, 0)
        other = swap(cut(a8, (1 - core) * block, block, 0), "mem", 1)
        return jnp.where(
            core == 0, jnp.concatenate([mine, other], axis=1), jnp.concatenate([other, mine], axis=1)
        )

    attended = heads_to_rows(att8)
    x_own = own_rows(x_full).astype(jnp.float32)
    first, first_norm, first_inv = normalize(
        x_own + product(attended, self_out) + proj_bias[2], norm_gain[0], norm_shift[0]
    )
    first_low = first.astype(low)
    first_other = swap(first_low, "mem", 1)
    first_chip = jnp.where(
        core == 0,
        jnp.concatenate([first_low, first_other], axis=0),
        jnp.concatenate([first_other, first_low], axis=0),
    )

    cq8 = ((product(first_chip, cut(cross_q, side, half)) + cut(proj_bias[3], side, half, 0)) * 0.125).astype(low)
    kvc8 = project(core, mem_full, cross_kv, proj_bias, (None, 4), (1.0, 1.0))
    slot_pos = jnp.stack([(me ^ k) * mem_block for k in ORDER])
    mem_pos = (slot_pos[:, None] + jnp.arange(mem_block, dtype=jnp.int32)[None, :]).reshape(-1)
    mem_bias = jnp.where(mem_pos < mem_len[0], 0.0, neg_fill).astype(jnp.float32)
    crossed = heads_to_rows(cross_forward(cq8, kvc8, mem_bias[None, :]))
    second, second_norm, second_inv = normalize(
        first + product(crossed, cross_out) + proj_bias[5], norm_gain[1], norm_shift[1]
    )
    second_low = second.astype(low)

    second_full = gather_rows(second_low)
    inner = product(second_low, ffn_in) + ffn_bias
    act, act_grad = gelu_parts(inner)
    act, act_grad = act.astype(low), act_grad.astype(low)
    third, third_norm, third_inv = normalize(
        second + product(act, ffn_out) + proj_bias[6], norm_gain[2], norm_shift[2]
    )
    row_pos = block_of(me) * block + jnp.arange(block, dtype=jnp.int32)
    cot = jnp.where((row_pos < dec_len[0])[:, None], own_rows(grad_out[0]).astype(jnp.float32), 0.0)
    dh3, gain_three, shift_three = norm_back(cot, third_norm, third_inv, norm_gain[2])
    dz = dh3.astype(low)
    first_full = gather_rows(first_low)
    dz_far = swap(dz, "mem", 2)
    wide = quart * quarter
    cq4 = ((product(first_full, cut(cross_q, wide, quarter)) + cut(proj_bias[3], wide, quarter, 0)) * 0.125).astype(low)
    du = (product_nt(dz, ffn_out) * act_grad.astype(jnp.float32)).astype(low)
    du, dz_far, late = tie(du, dz_far, quart)
    piece = hidden // groups // 4
    if piece % 128 == 0:
        w_in_q = pick_columns(ffn_in, piece, groups, 4, late)
    else:
        w_in_q = lax.dynamic_index_in_dim(ffn_in.reshape(width, groups, 4, piece), late, 2, False)
        w_in_q = w_in_q.reshape(width, hidden // 4)
    w_out_q = lax.dynamic_index_in_dim(ffn_out.reshape(groups, 4, piece, width), late, 1, False)
    w_out_q = w_out_q.reshape(hidden // 4, width)
    dh2, gain_two, shift_two = norm_back(
        dh3 + product_nt(du, ffn_in), second_norm, second_inv, norm_gain[1]
    )
    dco = dh2.astype(low)

    dz_full = join(dz, dz_far)
    dco_far = swap(dco, "mem", 2)
    b_in_q = lax.dynamic_index_in_dim(ffn_bias.reshape(groups, 4, piece), quart, 1, False).reshape(-1)
    act_q, slope_q = gelu_parts(product(second_full, w_in_q) + b_in_q)
    act_q = act_q.astype(low)
    du_q = (product_nt(dz_full, w_out_q) * slope_q).astype(low)
    du_q, dco_far, third_low = tie(du_q, dco_far, third.astype(low))
    dco_full = join(dco, dco_far)
    third_far = swap(third_low, "mem", 2)
    sum_in = Halving([product_tn(second_full, du_q)], 1)
    sum_out = Halving([product_tn(act_q, dz_full)], min(2, groups // 2))
    send_in, send_out = sum_in.send(), sum_out.send()

    dx4 = product_nt(dco_full, cut(cross_out, wide, quarter, 0)).astype(low)
    pair_base = chip * (quarter // 128)
    info_c = jnp.stack([pair_base]).astype(jnp.int32)
    bias_col = jnp.broadcast_to(mem_bias[:, None], (mem_bias.shape[0], 128))
    dx4, send_in, send_out, third_far, crossed_late = tie(dx4, send_in, send_out, third_far, crossed)
    crossed_far = swap(crossed_late, "mem", 2)
    got_in, got_out = sum_in.move(send_in), sum_out.move(send_out)
    dq4, dkc4, dvc4 = attention_back(info_c, cq4, kvc8, dx4, bias_col, False)
    dq4, dkc4, dvc4, got_in, got_out, crossed_far = tie(dq4, dkc4, dvc4, got_in, got_out, crossed_far)

    def over_chips(a):
        b0, b2, b1, b3 = jnp.split(a, 4, axis=0)
        return jnp.concatenate([b2, b3], axis=0), b0, b1

    def to_rows(over, b0, b1):
        size = b0.shape[0]
        mine = jnp.concatenate([b0, over[:size]], axis=0)
        other = swap(jnp.concatenate([b1, over[size:]], axis=0), "mem", 1)
        return by_quarter([mine[:size], mine[size:], other[:size], other[size:]])

    dq_leave, dq_0, dq_1 = over_chips(dq4)
    dq_far = swap(dq_leave, "mem", 2)
    dq_far, dq4, dkc4, dvc4, got_in, got_out = tie(dq_far, dq4, dkc4, dvc4, got_in, got_out)
    sum_in.add(got_in)
    sum_out.add(got_out)
    dkv4 = jnp.concatenate([dkc4, dvc4], axis=1)
    dkv_leave, dkv_0, dkv_1 = over_chips(dkv4)
    send_in, send_out = sum_in.send(), sum_out.send()
    dq_own = jnp.concatenate(to_rows(dq_far, dq_0, dq_1), axis=1)
    got_in, got_out = sum_in.move(send_in), sum_out.move(send_out)
    crossed_full = join(crossed, crossed_far)
    attended_full = gather_rows(attended)
    dh1, gain_one, shift_one = norm_back(
        dh2 + product_nt(dq_own, cross_q), first_norm, first_inv, norm_gain[0]
    )
    do = dh1.astype(low)
    sum_w = Halving(
        [product_tn(crossed_full, cut(dco_full, wide, quarter)), product_tn(first_full, dq4)], 1
    )
    sum_kv = Halving([product_tn(mem_full, dkv4)], min(2, groups // 2))
    got_w, got_kv = sum_w.move(sum_w.send()), sum_kv.move(sum_kv.send())
    do_far = swap(do, "mem", 2)
    do_far, got_in, got_out, got_w = tie(do_far, got_in, got_out, got_w)
    do_full, got_kv = tie(join(do, do_far), got_kv)
    sum_in.add(got_in)
    sum_out.add(got_out)
    sum_in.kept = sum_in.kept + sum_out.kept
    sum_w.add(got_w)
    sum_kv.add(got_kv)
    sum_so = Halving([product_tn(attended_full, cut(do_full, wide, quarter))], 1)

    da4 = product_nt(do_full, cut(self_out, wide, quarter, 0)).astype(low)
    where = [0, 2, 3, 1]
    slots = [((me ^ n) % 2) * 2 + (me ^ n) // 2 for n in where]
    info_s = jnp.stack([pair_base, dec_len[0]] + slots).astype(jnp.int32)
    send_in, send_w, send_kv, send_so = sum_in.send(), sum_w.send(), sum_kv.send(), sum_so.send()
    da4, send_in, send_w, send_kv, send_so, dkv_leave = tie(da4, send_in, send_w, send_kv, send_so, dkv_leave)
    got_in, got_w, got_kv = sum_in.move(send_in), sum_w.move(send_w), sum_kv.move(send_kv)
    got_so = sum_so.move(send_so)
    dkv_far = swap(dkv_leave, "mem", 2)
    sq4, sk4, sv4 = attention_back(info_s, qkv8, qkv8, da4, bias_col[:8], True)
    sq4, sk4, sv4, got_in, got_w, got_kv, got_so, dkv_far = tie(
        sq4, sk4, sv4, got_in, got_w, got_kv, got_so, dkv_far
    )
    sum_in.add(got_in)
    ffn_grad = jnp.concatenate([part.astype(low) for part in sum_in.finish()], axis=1)
    sum_w.add(got_w)
    sum_kv.add(got_kv)
    sum_so.add(got_so)
    sum_w.kept = sum_w.kept + sum_kv.kept
    send_w = sum_w.send()
    sq4, sk4, sv4, send_w, ffn_grad = tie(sq4, sk4, sv4, send_w, ffn_grad)
    ffn_far = swap(ffn_grad, "mem", 2)
    got_w = sum_w.move(send_w)
    dkv_parts = to_rows(dkv_far, dkv_0, dkv_1)
    dkv_own = jnp.concatenate(
        [a[:, :quarter] for a in dkv_parts] + [a[:, quarter:] for a in dkv_parts], axis=1
    )
    grad_memory = product_nt(dkv_own, cross_kv)[None]

    per = width // groups
    qkv_grad, partial, own_sums = self_weights(quart, x_full, sq4, sk4, sv4, self_qkv)
    qkv_grad = qkv_grad.reshape(groups // 2, 2, per, 3 * quarter)
    partial = partial.reshape(4, block, width)
    qkv_grad, got_w, ffn_far, grad_memory = tie(qkv_grad, got_w, ffn_far, grad_memory)
    sum_w.add(got_w)
    cross_grad = jnp.concatenate([part.astype(low) for part in sum_w.finish()], axis=1)
    so_grad = sum_so.kept[0].astype(low)
    layer_out = by_block(join(third_low, third_far))[None]

    place = jnp.zeros((2, width), jnp.float32)
    own_sums = own_sums[:2]
    place = lax.dynamic_update_slice(place, own_sums, (0, quart * quarter))
    packed = jnp.concatenate(
        [
            place,
            jnp.stack(
                [
                    column_sum(do),
                    column_sum(dq_own),
                    column_sum(dkv_own[:, width:]),
                    column_sum(dco),
                    column_sum(dz),
                    gain_one,
                    gain_two,
                    gain_three,
                    shift_one,
                    shift_two,
                    shift_three,
                ]
            ),
            column_sum(du).reshape(hidden // width, width),
        ],
        axis=0,
    )
    packed = jnp.pad(packed, ((0, -packed.shape[0] % 8), (0, 0)))
    cross_w, ffn_w, so_w, qkv_w, grad_rows, packed = finale(
        cross_grad, ffn_grad, ffn_far, so_grad, qkv_grad, partial, dh1, packed
    )
    w_qkv, w_so, w_cq, w_ckv, w_co, w_fi, w_fo, grad_dec, p_bias, n_gain, n_shift, f_bias = unpack(
        cross_w, ffn_w, so_w, qkv_w, grad_rows, packed, width, hidden, piece
    )
    return (
        layer_out,
        grad_dec.reshape(1, rows, width),
        grad_memory,
        w_qkv,
        w_so,
        w_cq,
        w_ckv,
        w_co,
        w_fi,
        w_fo.reshape(-1, width),
        p_bias,
        f_bias.reshape(hidden),
        n_gain,
        n_shift,
    )


def solution(mesh):
    in_specs = (
        P("dp", None, None),
        P("dp", "mem", None),
        P("dp"),
        P("dp"),
        P("dp", None, None),
    ) + (P(),) * 11
    out_specs = (
        P("dp", None, None),
        P("dp", None, None),
        P("dp", "mem", None),
    ) + (P("dp", None),) * 7 + (P(),) * 4
    return jax.shard_map(
        per_device, mesh=mesh, in_specs=in_specs, out_specs=out_specs, check_vma=False
    )
```
